128 devices in a mesh: gx: 16 (over y_hi, z, core), gy: 8 (over x, y_lo).
Axes of the slice: x: 4, y: 4 (y_hi: 2, y_lo: 2; y = y_hi * 2 + y_lo), z: 4, core: 2. Of those that a mesh axis runs over, the one named last changes fastest.
Arguments:
- cotangent: float32 [64, 128, 1024], P(None, 'gx', 'gy'), may hold values from -6 to 6
- saved_temp: float32 [64, 128, 1024], P(None, 'gx', 'gy'), may hold values from -6 to 6
- substrate_top: int32 [128, 1024], P('gx', 'gy'), may hold values from 16 to 31
- deposit_top: int32 [128, 1024], P('gx', 'gy'), may hold values from 32 to 64
- top_class: int32 [128, 1024], P('gx', 'gy'), may hold values from 0 to 3
Outputs:
- grad_temp: float32 [64, 128, 1024], P(None, 'gx', 'gy')
- grad_source: float32 [64, 128, 1024], P(None, 'gx', 'gy')
The draws below stay inside these ranges and needn't reach their ends.
All inputs are finite; a program needn't handle non-finite values.
Results may differ from the reference program's by a relative error of at most 0.0005.
Values sent between devices are 32-bit elements; how exact they have to be, the bound alone decides.
No kernel may reach another device: no remote copies, remote signals or barrier semaphores. Data moves between devices by JAX's collectives and lax.ppermute only.
A program may use at most 64 MiB of HBM per device.

```python
import jax
import jax.numpy as jnp
from jax import lax

NZ = 64
NX = 128
NY = 1024


def draw_cotangent(key, part):
    random_part = jnp.clip(jax.random.normal(key, (NZ, NX, NY), jnp.float32), -5.0, 5.0)
    return random_part


def place_ends(result, rng, low, high):
    shape = result.shape
    place = [jax.random.randint(jax.random.fold_in(rng, axis), (), 0, shape[axis]) for axis in range(len(shape))]
    result = result.at[tuple(place)].set(low)
    longest = shape.index(max(shape))
    place[longest] = (place[longest] + 1) % shape[longest]
    return result.at[tuple(place)].set(high)


def levels(key, dims, pieces, smallest, largest):
    gain, own = 1.0, jax.random.fold_in(key, 6)
    for axis_at, shards_of in pieces:
        steps = jnp.exp(jax.random.uniform(jax.random.fold_in(own, axis_at), (shards_of,), jnp.float32, smallest / len(pieces), largest / len(pieces)))
        gain = gain * jnp.repeat(steps, dims[axis_at] // shards_of).reshape([-1 if axis == axis_at else 1 for axis in range(len(dims))])
    return gain


def normal_values(key, shape, spread, bound, shards=(), kind=jnp.bfloat16):
    array = jax.random.normal(key, shape, jnp.float32) * spread
    if len(shards) > 0:
        array = levels(key, shape, shards, -0.22, 0.18) * array
    return jnp.clip(array, min=-bound, max=bound).astype(kind)


def setup_inputs(seed: int = 0) -> dict:
    key_of = jax.random.split(jax.random.key(seed), 6)
    cotangent = draw_cotangent(jax.random.fold_in(key_of[5], 71), 0)
    saved_temp = normal_values(key_of[1], (NZ, NX, NY), 1.0, 6.0, ((1, 16), (2, 8)), jnp.float32)
    substrate_top = place_ends(jax.random.randint(key_of[2], (NX, NY), NZ // 4, NZ // 2), jax.random.fold_in(key_of[2], 1), NZ // 4, (NZ // 2) - 1).astype(jnp.int32)
    deposit_top = place_ends(jax.random.randint(key_of[3], (NX, NY), NZ // 2, NZ + 1), jax.random.fold_in(key_of[3], 1), NZ // 2, NZ).astype(jnp.int32)
    top_class = place_ends(jax.random.randint(key_of[4], (NX, NY), 0, 4), jax.random.fold_in(key_of[4], 1), 0, 3).astype(jnp.int32)
    return dict(cotangent=cotangent, saved_temp=saved_temp, substrate_top=substrate_top, deposit_top=deposit_top, top_class=top_class)


step_ratio = 1000.0
side_film = 0.3
bottom_film = 0.5
top_films = (0.05, 0.25, 0.8, 2.0)


def neighbor(values, axis_extent, offset, filler):
    length = values.shape[axis_extent]
    edge_shape = list(values.shape)
    edge_shape[axis_extent] = abs(offset)
    border = jnp.full(edge_shape, filler, values.dtype)
    if offset > 0:
        inside = lax.slice_in_dim(values, offset, length, axis=axis_extent)
        return jnp.concatenate([inside, border], axis=axis_extent)
    inside = lax.slice_in_dim(values, 0, length + offset, axis=axis_extent)
    return jnp.concatenate([border, inside], axis=axis_extent)


def film_table(classes):
    total = jnp.zeros(classes.shape, jnp.float32)
    for number in range(4):
        total = total + top_films[number] * (classes == number).astype(jnp.float32)
    return total


def material_fields(saved_temp, substrate_top, deposit_top, z_index):
    substrate = z_index < substrate_top[None]
    active = z_index < deposit_top[None]
    ones_field = jnp.ones_like(saved_temp)
    capacity = jnp.where(substrate, ones_field, 0.6 * ones_field)
    base = jnp.where(substrate, ones_field, 0.45 * ones_field)
    conduct = jnp.where(active, base * (0.5 + jax.nn.sigmoid(saved_temp)), jnp.zeros_like(saved_temp))
    return capacity, conduct


def band(conduct_before, conduct, conduct_after, capacity, film_line):
    flux_low = jnp.minimum(conduct_before, conduct)
    flux_high = jnp.minimum(conduct, conduct_after)
    main_diagonal = capacity + step_ratio * (flux_low + flux_high + film_line)
    return -step_ratio * flux_low, main_diagonal, -step_ratio * flux_high


def thomas_solve(lower_diagonal, main_diagonal, upper_diagonal, right_hand_vector, axis_extent):
    moved = tuple(jnp.moveaxis(jnp.broadcast_to(item, right_hand_vector.shape), axis_extent, 0) for item in (lower_diagonal, main_diagonal, upper_diagonal, right_hand_vector))
    zero_row = jnp.zeros_like(moved[3][0])

    def forward(carried, row_vals):
        prev_c, prev_d = carried
        sub_row, main_row, sup_row, rhs_row = row_vals
        divisor = main_row - sub_row * prev_c
        next_c = sup_row / divisor
        next_d = (rhs_row - sub_row * prev_d) / divisor
        return (next_c, next_d), (next_c, next_d)

    unused, (c_all, d_all) = lax.scan(forward, (zero_row, zero_row), moved)

    def backward(carried, row_vals):
        c_row, d_row = row_vals
        value_row = d_row - c_row * carried
        return value_row, value_row

    unused, solved = lax.scan(backward, zero_row, (c_all, d_all), reverse=True)
    return jnp.moveaxis(solved, 0, axis_extent)


def apply_lines(values, conduct, film_line, axis_extent):
    flux_low = jnp.minimum(neighbor(conduct, axis_extent, -1, 0.0), conduct)
    flux_high = jnp.minimum(conduct, neighbor(conduct, axis_extent, 1, 0.0))
    before = neighbor(values, axis_extent, -1, 0.0)
    after = neighbor(values, axis_extent, 1, 0.0)
    return flux_low * (before - values) + flux_high * (after - values) - film_line * values


def reference(cotangent, saved_temp, substrate_top, deposit_top, top_class):
    z_index = lax.broadcasted_iota(jnp.int32, (NZ, 1, 1), 0)
    x_index = lax.broadcasted_iota(jnp.int32, (1, NX, 1), 1)
    y_index = lax.broadcasted_iota(jnp.int32, (1, 1, NY), 2)
    capacity, conduct = material_fields(saved_temp, substrate_top, deposit_top, z_index)
    film_z = bottom_film * (z_index == 0).astype(jnp.float32) + film_table(top_class)[None] * (z_index == deposit_top[None] - 1).astype(jnp.float32)
    film_x = side_film * ((x_index == 0) | (x_index == NX - 1)).astype(jnp.float32)
    film_y = side_film * ((y_index == 0) | (y_index == NY - 1)).astype(jnp.float32)
    depth_band = band(neighbor(conduct, 0, -1, 0.0), conduct, neighbor(conduct, 0, 1, 0.0), capacity, film_z)
    y_band = band(neighbor(conduct, 2, -1, 0.0), conduct, neighbor(conduct, 2, 1, 0.0), capacity, film_y)
    x_band = band(neighbor(conduct, 1, -1, 0.0), conduct, neighbor(conduct, 1, 1, 0.0), capacity, film_x)
    scaled_third = thomas_solve(depth_band[0], depth_band[1], depth_band[2], cotangent, 0)
    adjoint_three = capacity * scaled_third
    scaled_two = thomas_solve(y_band[0], y_band[1], y_band[2], adjoint_three, 2)
    adjoint_two = capacity * scaled_two
    scaled_one = thomas_solve(x_band[0], x_band[1], x_band[2], adjoint_two, 1)
    grad_source = capacity * scaled_one
    lateral = apply_lines(scaled_one, conduct, film_y, 2)
    vertical = apply_lines(scaled_one, conduct, film_z, 0)
    grad_temp = 2.0 * grad_source - 2.0 * adjoint_two + cotangent + 2.0 * step_ratio * (lateral + vertical)
    return grad_temp, grad_source
```

```python
import functools

import jax
import jax.numpy as jnp
from jax import lax
from jax.experimental import pallas as pl
from jax.experimental.pallas import tpu as pltpu
from jax.sharding import PartitionSpec as P

R = 1000.0
SIDE = 0.3
BOTTOM = 0.5
TOPS = (0.05, 0.25, 0.8, 2.0)
F32 = jnp.float32
NLEV = 6


def recip(v):
    return 1.0 / v


def reduce_chain(c, s, d, track):
    levels, port, ties = [], None, []
    while len(s) > 1:
        half = len(s) // 2
        ml, mr, dv = [], [], []
        for j in range(half):
            i = 2 * j
            total = s[i] + c[i]
            if j:
                total = total + c[i - 1]
            inv = recip(total)
            mr.append(c[i] * inv)
            ml.append(c[i - 1] * inv if j else None)
            dv.append(d[i] * inv)
            if track and j == 0:
                if port is None:
                    port = [dv[0], inv, mr[0]]
                    ties.append(inv)
                else:
                    p, z, t = port
                    tie = t * inv
                    ties.append(tie)
                    port = [p + t * dv[0], z + t * tie, t * mr[0]]
        ns, nd, nc = [], [], []
        for j in range(half):
            e, o = 2 * j, 2 * j + 1
            sv = s[o] + mr[j] * s[e]
            dn = d[o] + mr[j] * d[e]
            if j + 1 < half:
                sv = sv + ml[j + 1] * s[e + 2]
                dn = dn + ml[j + 1] * d[e + 2]
                nc.append(ml[j + 1] * c[e + 2])
            ns.append(sv)
            nd.append(dn)
        levels.append((dv, ml, mr))
        c, s, d = nc, ns, nd
    return s[0], d[0], levels, port, ties


def expand_chain(u_last, levels, ties, flux):
    u = [u_last]
    for lev in range(len(levels) - 1, -1, -1):
        dv, ml, mr = levels[lev]
        out = []
        for j in range(len(u)):
            even = dv[j] + mr[j] * u[j]
            if j:
                even = even + ml[j] * u[j - 1]
            elif ties is not None:
                even = even + ties[lev] * flux
            out += [even, u[j]]
        u = out
    return u


def merge_ports(a, b):
    kfa, kla, za, ta, ga, pa, qa = a
    kfb, klb, zb, tb, gb, pb, qb = b
    link = R * jnp.minimum(kla, kfb)
    lk = link * recip(1.0 + link * zb)
    inv = recip(ga + lk)
    h = inv * (qa + lk * pb)
    ti = ta * inv
    lt = lk * tb
    w = lt * inv
    merged = (
        kfa,
        klb,
        za + ta * ti,
        ta * w,
        gb + lt * tb * (ga * inv),
        pa + ta * h,
        qb + lt * (h - pb),
    )
    return merged, (h, ti, w, lk, pb, tb)


def descend(saved, flux, u_b):
    h, ti, w, lk, pb, tb = saved
    u_a = h + ti * flux + w * u_b
    flux_b = lk * (u_a - pb - tb * u_b)
    return u_a, flux_b


def film_top(cls):
    total = jnp.zeros(cls.shape, F32)
    for n in range(4):
        total = total + TOPS[n] * (cls == n).astype(F32)
    return total


def node_order(half, lev):
    base, n = 0, half
    for _ in range(lev):
        base += n
        n //= 2
    return base, n


def put_levels(ref, levels):
    half = len(levels[0][0])
    for lev, triple in enumerate(levels):
        base, n = node_order(half, lev)
        for kind in range(3):
            for j in range(n):
                if triple[kind][j] is not None:
                    ref[kind, base + j] = triple[kind][j]


def get_levels(read, half):
    levels, lev = [], 0
    while half >> lev:
        base, n = node_order(half, lev)
        levels.append(
            tuple([None if kind == 1 and j == 0 else read(kind, base + j) for j in range(n)] for kind in range(3))
        )
        lev += 1
    return levels


def first_kernel(cot, temp, sub, dep, cls, ypack, cond, fac, tie_out, mid, tr):
    me_y = lax.axis_index("gy")
    sub_v, dep_v = sub[...], dep[...]
    top = film_top(cls[...])
    k, cap, s = [], [], []
    for z in range(64):
        under = z < sub_v
        sg = 0.5 + jax.nn.sigmoid(temp[8 * z : 8 * z + 8])
        kz = jnp.where(z < dep_v, jnp.where(under, 1.0, 0.45) * sg, 0.0)
        cond[8 * z : 8 * z + 8] = kz
        k.append(kz)
        cap.append(jnp.where(under, 1.0, 0.6))
        film = top * (dep_v - 1 == z).astype(F32)
        if z == 0:
            film = film + BOTTOM
        s.append(cap[z] + R * film)
    c = [R * jnp.minimum(k[z], k[z + 1]) for z in range(63)] + [None]
    d = [cot[8 * z : 8 * z + 8] for z in range(64)]
    g, q, levels, _, _ = reduce_chain(c, s, d, False)
    u = expand_chain(q * recip(g), levels, None, None)
    for z in range(64):
        tr[8 * z : 8 * z + 8] = cap[z] * u[z]

    def turned(src, dst):
        for pair in range(4):
            rows = jnp.concatenate(
                [src[pl.ds(2 * pair, 64, stride=8), :], src[pl.ds(2 * pair + 1, 64, stride=8), :]], axis=0
            )
            block = jnp.transpose(rows)
            for h in range(2):
                dst[pl.ds(4 * h + pair, 64, stride=8), :] = block[64 * h : 64 * h + 64]

    turned(cond, mid.at[0])
    turned(tr, mid.at[1])

    subf = sub_v.astype(F32)
    for pair in range(4):
        rows = jnp.concatenate(
            [
                jnp.broadcast_to(subf[2 * pair : 2 * pair + 1], (64, 128)),
                jnp.broadcast_to(subf[2 * pair + 1 : 2 * pair + 2], (64, 128)),
            ],
            axis=0,
        )
        block = jnp.transpose(rows)
        for h in range(2):
            mid[2, pl.ds(4 * h + pair, 64, stride=8), :] = block[64 * h : 64 * h + 64]
    z_lane = (lax.broadcasted_iota(jnp.int32, (8, 128), 1) & 63).astype(F32)
    row = lax.broadcasted_iota(jnp.int32, (8, 128), 0)
    ky, sy, dy = [], [], []
    for y in range(64):
        ky.append(mid[0, 8 * y : 8 * y + 8])
        dy.append(mid[1, 8 * y : 8 * y + 8])
        sy.append(jnp.where(z_lane < mid[2, 8 * y : 8 * y + 8], 1.0, 0.6))
    cap_first, cap_last = sy[0][0:4], sy[63][4:8]
    low = jnp.where(me_y == 0, R * SIDE, 0.0)
    high = jnp.where(me_y == 7, R * SIDE, 0.0)
    sy[0] = sy[0] + jnp.where(row < 4, low, 0.0)
    sy[63] = sy[63] + jnp.where(row >= 4, high, 0.0)
    cy = [R * jnp.minimum(ky[y], ky[y + 1]) for y in range(63)] + [None]
    g, q, levels, (p, zz, t), ties = reduce_chain(cy, sy, dy, True)
    put_levels(fac, levels)
    for lev in range(NLEV):
        tie_out[lev] = ties[lev]
    kf, kl = ky[0], ky[63]
    side_a = tuple(v[0:4] for v in (kf, kl, zz, t, g, p, q))
    side_b = tuple(v[4:8] for v in (kf, kl, zz, t, g, p, q))
    merged, saved = merge_ports(side_a, side_b)
    for i, v in enumerate(saved):
        tie_out[NLEV + i, 0:4] = v
    pack = jnp.concatenate(list(merged) + [cap_first, cap_last, jnp.zeros((4, 128), F32)], axis=0)
    for n in range(8):
        ypack[n] = pack


def second_kernel(gat, fac, ties, cond, sub, keep, send, xfac, xhfac, a2_out, kh_out, pick, flat, planes, xp):
    me_y = lax.axis_index("gy")
    me_x = lax.axis_index("gx")
    seg = [[gat[n, 4 * i : 4 * i + 4] for i in range(9)] for n in range(8)]
    gam, rhs = seg[0][4], seg[0][6]
    down, links = [None], [None]
    for n in range(1, 8):
        kf, kl, z, t, g, p, q = seg[n][:7]
        link = R * jnp.minimum(seg[n - 1][1], kf)
        lk = link * recip(1.0 + link * z)
        inv = recip(gam + lk)
        h = inv * (rhs + lk * p)
        lt = lk * t
        down.append((h, lt * inv))
        links.append(lk)
        rhs = q + lt * (h - p)
        gam = g + lt * t * (gam * inv)
    u = [None] * 8
    u[7] = rhs * recip(gam)
    for n in range(7, 0, -1):
        u[n - 1] = down[n][0] + down[n][1] * u[n]
    zero4 = jnp.zeros((4, 128), F32)
    fl, uf = [zero4], [None]
    for n in range(1, 8):
        kf, kl, z, t, g, p, q = seg[n][:7]
        fl.append(links[n] * (u[n - 1] - p - t * u[n]))
        uf.append(p + z * fl[n] + t * u[n])
    for n in range(8):
        rows = [fl[n], u[n]]
        if n:
            rows += [seg[n - 1][8] * u[n - 1], seg[n - 1][1], seg[n - 1][8]]
        else:
            rows += [zero4, zero4, zero4 + 1.0]
        if n < 7:
            rows += [seg[n + 1][7] * uf[n + 1], seg[n + 1][0], seg[n + 1][7]]
        else:
            rows += [zero4, zero4, zero4 + 1.0]
        for i, v in enumerate(rows):
            pick[n, 4 * i : 4 * i + 4] = v
    mine = [pick[me_y, 4 * i : 4 * i + 4] for i in range(8)]
    flux, u_b = mine[0], mine[1]
    saved = tuple(ties[NLEV + i, 0:4] for i in range(6))
    u_a, flux_b = descend(saved, flux, u_b)
    flux8 = jnp.concatenate([flux, flux_b], axis=0)
    last8 = jnp.concatenate([u_a, u_b], axis=0)
    levels = get_levels(lambda kind, i: fac[kind, i], 32)
    u_nodes = expand_chain(last8, levels, [ties[i] for i in range(NLEV)], flux8)
    for y in range(64):
        flat[8 * y : 8 * y + 8] = u_nodes[y]
    subf = sub[...]
    for pair in range(4):
        block = jnp.transpose(
            jnp.concatenate([flat[pl.ds(pair, 64, stride=8), :], flat[pl.ds(4 + pair, 64, stride=8), :]], axis=0)
        )
        for odd in range(2):
            x = 2 * pair + odd
            planes[x] = block[64 * odd : 64 * odd + 64]

    lane = lax.broadcasted_iota(jnp.int32, (4, 128), 1)

    def both(left, right):
        even = jnp.where(lane < 64, left, pltpu.roll(right, 64, 1))
        odd = jnp.where(lane < 64, pltpu.roll(left, 64, 1), right)
        return [(odd if x & 1 else even)[x // 2 : x // 2 + 1] for x in range(8)]

    dh, kh, caph = both(mine[2], mine[5]), both(mine[3], mine[6]), both(mine[4], mine[7])
    for x in range(8):
        kh_out[x : x + 1] = kh[x]

    low = jnp.where(me_x == 0, R * SIDE, 0.0)
    high = jnp.where(me_x == 15, R * SIDE, 0.0)

    def x_chain(k, cap, d):
        s = list(cap)
        s[0] = s[0] + low
        s[7] = s[7] + high
        c = [R * jnp.minimum(k[x], k[x + 1]) for x in range(7)] + [None]
        g, q, levels, (p, z, t), tie = reduce_chain(c, s, d, True)
        return levels, tie, (k[0], k[7], z, t, g, p, q)

    base_z = lax.broadcasted_iota(jnp.int32, (8, 128), 0)
    for chunk in range(8):
        zi = base_z + 8 * chunk
        k, cap, d = [], [], []
        for x in range(8):
            k.append(cond[pl.ds(64 * chunk + x, 8, stride=8), :])
            cap.append(jnp.where(zi < subf[x : x + 1], 1.0, 0.6))
            dx = cap[x] * planes[x, 8 * chunk : 8 * chunk + 8]
            a2_out[pl.ds(64 * chunk + x, 8, stride=8), :] = dx
            d.append(dx)
        levels, tie, port = x_chain(k, cap, d)
        store_x(xfac.at[chunk], levels, tie)
        for i in range(7):
            xp[i, 8 * chunk : 8 * chunk + 8] = port[i]
    levels, tie, port = x_chain(kh, caph, dh)
    store_x(xhfac, levels, tie)
    core = lax.rem(me_x, 2)
    for i in range(7):
        keep[32 * i : 32 * i + 32] = xp[i, pl.ds(pl.multiple_of(32 * core, 32), 32), :]
        send[32 * i : 32 * i + 32] = xp[i, pl.ds(pl.multiple_of(32 - 32 * core, 32), 32), :]
    tile = jnp.concatenate(list(port) + [jnp.zeros((1, 128), F32)], axis=0)
    keep[224:232] = tile
    send[224:232] = tile


def store_x(ref, levels, tie):
    for lev, triple in enumerate(levels):
        base, n = node_order(4, lev)
        for kind in range(3):
            for j in range(n):
                if triple[kind][j] is not None:
                    ref[7 * kind + base + j] = triple[kind][j]
    for lev in range(3):
        ref[21 + lev] = tie[lev]


def load_x(ref):
    levels = get_levels(lambda kind, i: ref[7 * kind + i], 4)
    return levels, [ref[21 + lev] for lev in range(3)]


def read_pack(ref, n):
    main = tuple(ref[32 * i : 32 * i + 32] for i in range(n))
    edge = tuple(ref[32 * n + i : 32 * n + i + 1] for i in range(n))
    return main, edge


def write_pack(ref, main, edge):
    n = len(main)
    for i in range(n):
        ref[32 * i : 32 * i + 32] = main[i]
        ref[32 * n + i : 32 * n + i + 1] = edge[i]


def order(right, mine, theirs):
    a = tuple(jnp.where(right, t, m) for m, t in zip(mine, theirs))
    b = tuple(jnp.where(right, m, t) for m, t in zip(mine, theirs))
    return a, b


def merge_kernel(bit, last, mine, theirs, merged_out, saved_out, *rest):
    me_x = lax.axis_index("gx")
    right = lax.rem(lax.div(me_x, bit), 2) == 1
    m, t = read_pack(mine, 7), read_pack(theirs, 7)
    done = []
    for part in range(2):
        a, b = order(right, m[part], t[part])
        done.append(merge_ports(a, b))
    write_pack(merged_out, done[0][0], done[1][0])
    write_pack(saved_out, done[0][1], done[1][1])
    if last:
        far = lax.div(me_x, 8) == 1
        outs = []
        for part in range(2):
            kf, kl, z, tt, g, p, q = done[part][0]
            gi = recip(g)
            tg = tt * gi
            outs.append(
                (
                    jnp.where(far, z + tt * tg, g),
                    jnp.where(far, p + tg * q, q),
                    jnp.where(far, kf, kl),
                )
            )
        write_pack(rest[0], outs[0], outs[1])


def top_kernel(merged, near, theirs, sv1, sv2, sv3, own, send):
    me_x = lax.axis_index("gx")
    far = lax.div(me_x, 8) == 1
    mm = read_pack(merged, 7)
    n, t = read_pack(near, 3), read_pack(theirs, 3)
    saved = [read_pack(r, 6) for r in (sv1, sv2, sv3)]
    final = []
    for part in range(2):
        (ga, qa, ka), (zb, pb, kb) = order(far, n[part], t[part])
        link = R * jnp.minimum(ka, kb)
        lk = link * recip(1.0 + link * zb)
        u_a = (qa + lk * pb) * recip(ga + lk)
        kf, kl, z, tt, g, p, q = mm[part]
        flux = jnp.where(far, lk * (u_a - pb), 0.0)
        u = jnp.where(far, (q + tt * flux) * recip(g), u_a)
        for bit, lev in ((4, 2), (2, 1)):
            right = lax.rem(lax.div(me_x, bit), 2) == 1
            ua, fb = descend(saved[lev][part], flux, u)
            flux = jnp.where(right, fb, flux)
            u = jnp.where(right, u, ua)
        ua, fb = descend(saved[0][part], flux, u)
        odd = lax.rem(me_x, 2) == 1
        final.append((jnp.where(odd, fb, flux), jnp.where(odd, u, ua), jnp.where(odd, flux, fb), jnp.where(odd, ua, u)))
    write_pack(own, final[0][:2], final[1][:2])
    send[0:32] = final[0][2]
    send[32:64] = final[0][3]


def last_kernel(own, got, xfac, xhfac, kh, cond, a2, cot, sub, dep, cls, temp_out, src_out, s1, fu):
    me_x = lax.axis_index("gx")
    me_y = lax.axis_index("gy")
    core = lax.rem(me_x, 2)
    for i in range(2):
        fu[i, pl.ds(pl.multiple_of(32 * core, 32), 32), :] = own[32 * i : 32 * i + 32]
        fu[i, pl.ds(pl.multiple_of(32 - 32 * core, 32), 32), :] = got[32 * i : 32 * i + 32]
    for chunk in range(8):
        levels, tie = load_x(xfac.at[chunk])
        u = expand_chain(fu[1, 8 * chunk : 8 * chunk + 8], levels, tie, fu[0, 8 * chunk : 8 * chunk + 8])
        for x in range(8):
            s1[pl.ds(64 * chunk + x, 8, stride=8), :] = u[x]
    levels, tie = load_x(xhfac)
    uh = jnp.concatenate(expand_chain(own[65:66], levels, tie, own[64:65]), axis=0)
    kh_v = kh[...]
    sub_v, dep_v = sub[...], dep[...]
    top = film_top(cls[...])
    lane = lax.broadcasted_iota(jnp.int32, (8, 128), 1)
    first, final = lane == 0, lane == 127
    film_y = jnp.where(first & (me_y == 0), SIDE, 0.0) + jnp.where(final & (me_y == 7), SIDE, 0.0)
    up = None
    for z in range(64):
        rows = slice(8 * z, 8 * z + 8)
        s, k = s1[rows], cond[rows]
        s_r = jnp.where(final, pltpu.roll(uh, 63 - z, 1), pltpu.roll(s, 127, 1))
        k_r = jnp.where(final, pltpu.roll(kh_v, 63 - z, 1), pltpu.roll(k, 127, 1))
        s_l = pltpu.roll(uh, (128 - z) % 128, 1) if z else uh
        k_l = pltpu.roll(kh_v, (128 - z) % 128, 1) if z else kh_v
        f_y = jnp.minimum(k, k_r) * (s_r - s)
        f_l = jnp.minimum(k, k_l) * (s - s_l)
        total = f_y - jnp.where(first, f_l, pltpu.roll(f_y, 1, 1))
        film = film_y + top * (dep_v - 1 == z).astype(F32)
        if z == 0:
            film = film + BOTTOM
        if z < 63:
            nxt = slice(8 * z + 8, 8 * z + 16)
            f_z = jnp.minimum(k, cond[nxt]) * (s1[nxt] - s)
            total = total + f_z
        if z:
            total = total - up
        up = f_z
        total = total - film * s
        src = jnp.where(z < sub_v, 1.0, 0.6) * s
        src_out[rows] = src
        temp_out[rows] = 2.0 * src - 2.0 * a2[rows] + cot[rows] + (2.0 * R) * total


def call(kernel, outs, scratch, name, *args):
    vmem = pl.BlockSpec(memory_space=pltpu.VMEM)
    return pl.pallas_call(
        kernel,
        out_shape=[jax.ShapeDtypeStruct(s, F32) for s in outs],
        in_specs=[vmem] * len(args),
        out_specs=[vmem] * len(outs),
        scratch_shapes=[pltpu.VMEM(s, F32) for s in scratch],
        compiler_params=pltpu.CompilerParams(vmem_limit_bytes=40 * 1024 * 1024),
        name=name,
    )(*args)


def swap(v, bit):
    return lax.ppermute(v, "gx", [(i, i ^ bit) for i in range(16)])


def body(cotangent, saved_temp, substrate_top, deposit_top, top_class):
    cot = cotangent.reshape(512, 128)
    temp = saved_temp.reshape(512, 128)
    ypack, cond, fac, ties = call(
        first_kernel,
        [(8, 40, 128), (512, 128), (3, 63, 8, 128), (12, 8, 128)],
        [(3, 512, 128), (512, 128)],
        "first",
        cot, temp, substrate_top, deposit_top, top_class,
    )
    gat = lax.all_to_all(ypack, "gy", split_axis=0, concat_axis=0, tiled=True)
    keep, send, xfac, xhfac, a2, kh = call(
        second_kernel,
        [(232, 128), (232, 128), (8, 24, 8, 128), (24, 1, 128), (512, 128), (8, 128)],
        [(8, 32, 128), (512, 128), (8, 64, 128), (7, 64, 128)],
        "second",
        gat, fac, ties, cond, substrate_top,
    )
    m1, sv1 = call(functools.partial(merge_kernel, 1, False), [(232, 128), (200, 128)], [], "merge_core", keep, swap(send, 1))
    m2, sv2 = call(functools.partial(merge_kernel, 2, False), [(232, 128), (200, 128)], [], "merge_near", m1, swap(m1, 2))
    m3, sv3, near = call(
        functools.partial(merge_kernel, 4, True), [(232, 128), (200, 128), (104, 128)], [], "merge_far", m2, swap(m2, 6)
    )
    own, out = call(top_kernel, [(72, 128), (64, 128)], [], "top", m3, near, swap(near, 8), sv1, sv2, sv3)
    got = swap(out, 1)
    grad_temp, grad_source = call(
        last_kernel,
        [(512, 128), (512, 128)],
        [(512, 128), (2, 64, 128)],
        "last",
        own, got, xfac, xhfac, kh, cond, a2, cot, substrate_top, deposit_top, top_class,
    )
    return grad_temp.reshape(cotangent.shape), grad_source.reshape(cotangent.shape)


def solution(mesh):
    in_specs = (
        P(None, "gx", "gy"),
        P(None, "gx", "gy"),
        P("gx", "gy"),
        P("gx", "gy"),
        P("gx", "gy"),
    )
    out_specs = (P(None, "gx", "gy"), P(None, "gx", "gy"))
    return jax.shard_map(body, mesh=mesh, in_specs=in_specs, out_specs=out_specs, check_vma=False)
```

```python
import functools

import jax
import jax.numpy as jnp
from jax import lax
from jax.experimental import pallas as pl
from jax.experimental.pallas import tpu as pltpu
from jax.sharding import PartitionSpec as P

R = 1000.0
SIDE = 0.3
BOTTOM = 0.5
TOPS = (0.05, 0.25, 0.8, 2.0)
F32 = jnp.float32
NLEV = 6


def recip(v):
    return 1.0 / v


def reduce_chain(c, s, d, track):
    levels, port, ties = [], None, []
    while len(s) > 1:
        half = len(s) // 2
        ml, mr, dv = [], [], []
        for j in range(half):
            i = 2 * j
            total = s[i] + c[i]
            if j:
                total = total + c[i - 1]
            inv = recip(total)
            mr.append(c[i] * inv)
            ml.append(c[i - 1] * inv if j else None)
            dv.append(d[i] * inv)
            if track and j == 0:
                if port is None:
                    port = [dv[0], inv, mr[0]]
                    ties.append(inv)
                else:
                    p, z, t = port
                    tie = t * inv
                    ties.append(tie)
                    port = [p + t * dv[0], z + t * tie, t * mr[0]]
        ns, nd, nc = [], [], []
        for j in range(half):
            e, o = 2 * j, 2 * j + 1
            sv = s[o] + mr[j] * s[e]
            dn = d[o] + mr[j] * d[e]
            if j + 1 < half:
                sv = sv + ml[j + 1] * s[e + 2]
                dn = dn + ml[j + 1] * d[e + 2]
                nc.append(ml[j + 1] * c[e + 2])
            ns.append(sv)
            nd.append(dn)
        levels.append((dv, ml, mr))
        c, s, d = nc, ns, nd
    return s[0], d[0], levels, port, ties


def expand_chain(u_last, levels, ties, flux):
    u = [u_last]
    for lev in range(len(levels) - 1, -1, -1):
        dv, ml, mr = levels[lev]
        out = []
        for j in range(len(u)):
            even = dv[j] + mr[j] * u[j]
            if j:
                even = even + ml[j] * u[j - 1]
            elif ties is not None:
                even = even + ties[lev] * flux
            out += [even, u[j]]
        u = out
    return u


def merge_ports(a, b):
    kfa, kla, za, ta, ga, pa, qa = a
    kfb, klb, zb, tb, gb, pb, qb = b
    link = R * jnp.minimum(kla, kfb)
    lk = link * recip(1.0 + link * zb)
    inv = recip(ga + lk)
    h = inv * (qa + lk * pb)
    ti = ta * inv
    lt = lk * tb
    w = lt * inv
    merged = (
        kfa,
        klb,
        za + ta * ti,
        ta * w,
        gb + lt * tb * (ga * inv),
        pa + ta * h,
        qb + lt * (h - pb),
    )
    return merged, (h, ti, w, lk, pb, tb)


def descend(saved, flux, u_b):
    h, ti, w, lk, pb, tb = saved
    u_a = h + ti * flux + w * u_b
    flux_b = lk * (u_a - pb - tb * u_b)
    return u_a, flux_b


def film_top(cls):
    total = jnp.zeros(cls.shape, F32)
    for n in range(4):
        total = total + TOPS[n] * (cls == n).astype(F32)
    return total


def node_order(half, lev):
    base, n = 0, half
    for _ in range(lev):
        base += n
        n //= 2
    return base, n


def put_levels(ref, levels):
    half = len(levels[0][0])
    for lev, triple in enumerate(levels):
        base, n = node_order(half, lev)
        for kind in range(3):
            for j in range(n):
                if triple[kind][j] is not None:
                    ref[kind, base + j] = triple[kind][j]


def get_levels(read, half):
    levels, lev = [], 0
    while half >> lev:
        base, n = node_order(half, lev)
        levels.append(
            tuple([None if kind == 1 and j == 0 else read(kind, base + j) for j in range(n)] for kind in range(3))
        )
        lev += 1
    return levels


def first_kernel(
    cot_in, temp_in, sub_in, dep_in, cls_in, ypack, cond, fac, tie_out, cot, sub, dep, cls, temp, mid, tr, sems
):
    me_y = lax.axis_index("gy")
    pairs = ((sub_in, sub), (dep_in, dep), (temp_in, temp), (cls_in, cls), (cot_in, cot))
    copies = [pltpu.make_async_copy(a, b, sems.at[i]) for i, (a, b) in enumerate(pairs)]
    for cp in copies:
        cp.start()
    for cp in copies[:4]:
        cp.wait()
    sub_v, dep_v = sub[...], dep[...]
    top = film_top(cls[...])
    k, cap, s = [], [], []
    for z in range(64):
        under = z < sub_v
        sg = 0.5 + jax.nn.sigmoid(temp[8 * z : 8 * z + 8])
        kz = jnp.where(z < dep_v, jnp.where(under, 1.0, 0.45) * sg, 0.0)
        cond[8 * z : 8 * z + 8] = kz
        k.append(kz)
        cap.append(jnp.where(under, 1.0, 0.6))
        film = top * (dep_v - 1 == z).astype(F32)
        if z == 0:
            film = film + BOTTOM
        s.append(cap[z] + R * film)
    c = [R * jnp.minimum(k[z], k[z + 1]) for z in range(63)] + [None]
    copies[4].wait()
    d = [cot[8 * z : 8 * z + 8] for z in range(64)]
    g, q, levels, _, _ = reduce_chain(c, s, d, False)
    u = expand_chain(q * recip(g), levels, None, None)
    for z in range(64):
        tr[8 * z : 8 * z + 8] = cap[z] * u[z]

    def turned(src, dst):
        for pair in range(4):
            rows = jnp.concatenate(
                [src[pl.ds(2 * pair, 64, stride=8), :], src[pl.ds(2 * pair + 1, 64, stride=8), :]], axis=0
            )
            block = jnp.transpose(rows)
            for h in range(2):
                dst[pl.ds(4 * h + pair, 64, stride=8), :] = block[64 * h : 64 * h + 64]

    turned(cond, mid.at[0])
    turned(tr, mid.at[1])

    subf = sub_v.astype(F32)
    for pair in range(4):
        rows = jnp.concatenate(
            [
                jnp.broadcast_to(subf[2 * pair : 2 * pair + 1], (64, 128)),
                jnp.broadcast_to(subf[2 * pair + 1 : 2 * pair + 2], (64, 128)),
            ],
            axis=0,
        )
        block = jnp.transpose(rows)
        for h in range(2):
            mid[2, pl.ds(4 * h + pair, 64, stride=8), :] = block[64 * h : 64 * h + 64]
    z_lane = (lax.broadcasted_iota(jnp.int32, (8, 128), 1) & 63).astype(F32)
    row = lax.broadcasted_iota(jnp.int32, (8, 128), 0)
    ky, sy, dy = [], [], []
    for y in range(64):
        ky.append(mid[0, 8 * y : 8 * y + 8])
        dy.append(mid[1, 8 * y : 8 * y + 8])
        sy.append(jnp.where(z_lane < mid[2, 8 * y : 8 * y + 8], 1.0, 0.6))
    cap_first, cap_last = sy[0][0:4], sy[63][4:8]
    low = jnp.where(me_y == 0, R * SIDE, 0.0)
    high = jnp.where(me_y == 7, R * SIDE, 0.0)
    sy[0] = sy[0] + jnp.where(row < 4, low, 0.0)
    sy[63] = sy[63] + jnp.where(row >= 4, high, 0.0)
    cy = [R * jnp.minimum(ky[y], ky[y + 1]) for y in range(63)] + [None]
    g, q, levels, (p, zz, t), ties = reduce_chain(cy, sy, dy, True)
    put_levels(fac, levels)
    for lev in range(NLEV):
        tie_out[lev] = ties[lev]
    kf, kl = ky[0], ky[63]
    side_a = tuple(v[0:4] for v in (kf, kl, zz, t, g, p, q))
    side_b = tuple(v[4:8] for v in (kf, kl, zz, t, g, p, q))
    merged, saved = merge_ports(side_a, side_b)
    for i, v in enumerate(saved):
        tie_out[NLEV + i, 0:4] = v
    pack = jnp.concatenate(list(merged) + [cap_first, cap_last, jnp.zeros((4, 128), F32)], axis=0)
    for n in range(8):
        ypack[n] = pack


def second_kernel(gat, fac, ties, cond, sub, xpack, xfac, xhfac, a2_out, kh_out, pick, flat, planes):
    me_y = lax.axis_index("gy")
    me_x = lax.axis_index("gx")
    seg = [[gat[n, 4 * i : 4 * i + 4] for i in range(9)] for n in range(8)]
    gam, rhs = seg[0][4], seg[0][6]
    down, links = [None], [None]
    for n in range(1, 8):
        kf, kl, z, t, g, p, q = seg[n][:7]
        link = R * jnp.minimum(seg[n - 1][1], kf)
        lk = link * recip(1.0 + link * z)
        inv = recip(gam + lk)
        h = inv * (rhs + lk * p)
        lt = lk * t
        down.append((h, lt * inv))
        links.append(lk)
        rhs = q + lt * (h - p)
        gam = g + lt * t * (gam * inv)
    u = [None] * 8
    u[7] = rhs * recip(gam)
    for n in range(7, 0, -1):
        u[n - 1] = down[n][0] + down[n][1] * u[n]
    zero4 = jnp.zeros((4, 128), F32)
    fl, uf = [zero4], [None]
    for n in range(1, 8):
        kf, kl, z, t, g, p, q = seg[n][:7]
        fl.append(links[n] * (u[n - 1] - p - t * u[n]))
        uf.append(p + z * fl[n] + t * u[n])
    for n in range(8):
        rows = [fl[n], u[n]]
        if n:
            rows += [seg[n - 1][8] * u[n - 1], seg[n - 1][1], seg[n - 1][8]]
        else:
            rows += [zero4, zero4, zero4 + 1.0]
        if n < 7:
            rows += [seg[n + 1][7] * uf[n + 1], seg[n + 1][0], seg[n + 1][7]]
        else:
            rows += [zero4, zero4, zero4 + 1.0]
        for i, v in enumerate(rows):
            pick[n, 4 * i : 4 * i + 4] = v
    mine = [pick[me_y, 4 * i : 4 * i + 4] for i in range(8)]
    flux, u_b = mine[0], mine[1]
    saved = tuple(ties[NLEV + i, 0:4] for i in range(6))
    u_a, flux_b = descend(saved, flux, u_b)
    flux8 = jnp.concatenate([flux, flux_b], axis=0)
    last8 = jnp.concatenate([u_a, u_b], axis=0)
    levels = get_levels(lambda kind, i: fac[kind, i], 32)
    u_nodes = expand_chain(last8, levels, [ties[i] for i in range(NLEV)], flux8)
    for y in range(64):
        flat[8 * y : 8 * y + 8] = u_nodes[y]
    subf = sub[...]
    for pair in range(4):
        block = jnp.transpose(
            jnp.concatenate([flat[pl.ds(pair, 64, stride=8), :], flat[pl.ds(4 + pair, 64, stride=8), :]], axis=0)
        )
        for odd in range(2):
            x = 2 * pair + odd
            planes[x] = block[64 * odd : 64 * odd + 64]

    lane = lax.broadcasted_iota(jnp.int32, (4, 128), 1)

    def both(left, right):
        even = jnp.where(lane < 64, left, pltpu.roll(right, 64, 1))
        odd = jnp.where(lane < 64, pltpu.roll(left, 64, 1), right)
        return [(odd if x & 1 else even)[x // 2 : x // 2 + 1] for x in range(8)]

    dh, kh, caph = both(mine[2], mine[5]), both(mine[3], mine[6]), both(mine[4], mine[7])
    for x in range(8):
        kh_out[x : x + 1] = kh[x]

    low = jnp.where(me_x == 0, R * SIDE, 0.0)
    high = jnp.where(me_x == 15, R * SIDE, 0.0)

    def x_chain(k, cap, d):
        s = list(cap)
        s[0] = s[0] + low
        s[7] = s[7] + high
        c = [R * jnp.minimum(k[x], k[x + 1]) for x in range(7)] + [None]
        g, q, levels, (p, z, t), tie = reduce_chain(c, s, d, True)
        return levels, tie, (k[0], k[7], z, t, g, p, q)

    base_z = lax.broadcasted_iota(jnp.int32, (8, 128), 0)
    for chunk in range(8):
        zi = base_z + 8 * chunk
        k, cap, d = [], [], []
        for x in range(8):
            k.append(cond[pl.ds(64 * chunk + x, 8, stride=8), :])
            cap.append(jnp.where(zi < subf[x : x + 1], 1.0, 0.6))
            dx = cap[x] * planes[x, 8 * chunk : 8 * chunk + 8]
            a2_out[pl.ds(64 * chunk + x, 8, stride=8), :] = dx
            d.append(dx)
        levels, tie, port = x_chain(k, cap, d)
        store_x(xfac.at[chunk], levels, tie)
        for i in range(7):
            xpack[64 * i + 8 * chunk : 64 * i + 8 * chunk + 8] = port[i]
    levels, tie, port = x_chain(kh, caph, dh)
    store_x(xhfac, levels, tie)
    for i in range(7):
        xpack[448 + i : 449 + i] = port[i]


def store_x(ref, levels, tie):
    for lev, triple in enumerate(levels):
        base, n = node_order(4, lev)
        for kind in range(3):
            for j in range(n):
                if triple[kind][j] is not None:
                    ref[7 * kind + base + j] = triple[kind][j]
    for lev in range(3):
        ref[21 + lev] = tie[lev]


def load_x(ref):
    levels = get_levels(lambda kind, i: ref[7 * kind + i], 4)
    return levels, [ref[21 + lev] for lev in range(3)]


def read_pack(ref, n):
    main = tuple(ref[64 * i : 64 * i + 64] for i in range(n))
    edge = tuple(ref[64 * n + i : 64 * n + i + 1] for i in range(n))
    return main, edge


def write_pack(ref, main, edge):
    n = len(main)
    for i in range(n):
        ref[64 * i : 64 * i + 64] = main[i]
        ref[64 * n + i : 64 * n + i + 1] = edge[i]


def order(right, mine, theirs):
    a = tuple(jnp.where(right, t, m) for m, t in zip(mine, theirs))
    b = tuple(jnp.where(right, m, t) for m, t in zip(mine, theirs))
    return a, b


def merge_kernel(bit, last, mine, theirs, merged_out, saved_out, *rest):
    me_x = lax.axis_index("gx")
    right = lax.rem(lax.div(me_x, bit), 2) == 1
    m, t = read_pack(mine, 7), read_pack(theirs, 7)
    done = []
    for part in range(2):
        a, b = order(right, m[part], t[part])
        done.append(merge_ports(a, b))
    write_pack(merged_out, done[0][0], done[1][0])
    write_pack(saved_out, done[0][1], done[1][1])
    if last:
        far = lax.div(me_x, 8) == 1
        outs = []
        for part in range(2):
            kf, kl, z, tt, g, p, q = done[part][0]
            gi = recip(g)
            tg = tt * gi
            outs.append(
                (
                    jnp.where(far, z + tt * tg, g),
                    jnp.where(far, p + tg * q, q),
                    jnp.where(far, kf, kl),
                )
            )
        write_pack(rest[0], outs[0], outs[1])


def top_kernel(merged, near, theirs, sv1, sv2, sv3, own, send):
    me_x = lax.axis_index("gx")
    far = lax.div(me_x, 8) == 1
    mm = read_pack(merged, 7)
    n, t = read_pack(near, 3), read_pack(theirs, 3)
    saved = [read_pack(r, 6) for r in (sv1, sv2, sv3)]
    final = []
    for part in range(2):
        (ga, qa, ka), (zb, pb, kb) = order(far, n[part], t[part])
        link = R * jnp.minimum(ka, kb)
        lk = link * recip(1.0 + link * zb)
        u_a = (qa + lk * pb) * recip(ga + lk)
        kf, kl, z, tt, g, p, q = mm[part]
        flux = jnp.where(far, lk * (u_a - pb), 0.0)
        u = jnp.where(far, (q + tt * flux) * recip(g), u_a)
        for bit, lev in ((4, 2), (2, 1)):
            right = lax.rem(lax.div(me_x, bit), 2) == 1
            ua, fb = descend(saved[lev][part], flux, u)
            flux = jnp.where(right, fb, flux)
            u = jnp.where(right, u, ua)
        ua, fb = descend(saved[0][part], flux, u)
        final.append(((fb, u), (flux, ua)))
    write_pack(own, final[0][0], final[1][0])
    write_pack(send, final[0][1], final[1][1])


def last_kernel(
    own, got, xfac, xhfac, kh, cond, a2, cot, sub, dep, cls, temp_out, src_out, s1, fu, t_buf, s_buf, sems
):
    me_x = lax.axis_index("gx")
    me_y = lax.axis_index("gy")
    odd = lax.rem(me_x, 2) == 1
    fu[...] = jnp.where(odd, own[...], got[...])
    for chunk in range(8):
        levels, tie = load_x(xfac.at[chunk])
        u = expand_chain(fu[64 + 8 * chunk : 72 + 8 * chunk], levels, tie, fu[8 * chunk : 8 * chunk + 8])
        for x in range(8):
            s1[pl.ds(64 * chunk + x, 8, stride=8), :] = u[x]
    levels, tie = load_x(xhfac)
    uh = jnp.concatenate(expand_chain(fu[129:130], levels, tie, fu[128:129]), axis=0)
    kh_v = kh[...]
    sub_v, dep_v = sub[...], dep[...]
    top = film_top(cls[...])
    lane = lax.broadcasted_iota(jnp.int32, (8, 128), 1)
    first, final = lane == 0, lane == 127
    film_y = jnp.where(first & (me_y == 0), SIDE, 0.0) + jnp.where(final & (me_y == 7), SIDE, 0.0)
    up, copies = None, []
    for z in range(64):
        rows = slice(8 * z, 8 * z + 8)
        s, k = s1[rows], cond[rows]
        s_r = jnp.where(final, pltpu.roll(uh, 63 - z, 1), pltpu.roll(s, 127, 1))
        k_r = jnp.where(final, pltpu.roll(kh_v, 63 - z, 1), pltpu.roll(k, 127, 1))
        s_l = pltpu.roll(uh, (128 - z) % 128, 1) if z else uh
        k_l = pltpu.roll(kh_v, (128 - z) % 128, 1) if z else kh_v
        f_y = jnp.minimum(k, k_r) * (s_r - s)
        f_l = jnp.minimum(k, k_l) * (s - s_l)
        total = f_y - jnp.where(first, f_l, pltpu.roll(f_y, 1, 1))
        film = film_y + top * (dep_v - 1 == z).astype(F32)
        if z == 0:
            film = film + BOTTOM
        if z < 63:
            nxt = slice(8 * z + 8, 8 * z + 16)
            f_z = jnp.minimum(k, cond[nxt]) * (s1[nxt] - s)
            total = total + f_z
        if z:
            total = total - up
        up = f_z
        total = total - film * s
        src = jnp.where(z < sub_v, 1.0, 0.6) * s
        s_buf[rows] = src
        t_buf[rows] = 2.0 * src - 2.0 * a2[rows] + cot[rows] + (2.0 * R) * total
        if z & 7 == 7:
            part = slice(8 * z - 56, 8 * z + 8)
            for i, (buf, out) in enumerate(((s_buf, src_out), (t_buf, temp_out))):
                cp = pltpu.make_async_copy(buf.at[part], out.at[part], sems.at[2 * (z // 8) + i])
                cp.start()
                copies.append(cp)
    for cp in copies:
        cp.wait()


VMEM = pl.BlockSpec(memory_space=pltpu.VMEM)
HBM = pl.BlockSpec(memory_space=pltpu.MemorySpace.HBM)


def call(kernel, outs, scratch, name, *args, far_in=0, far_out=0, sems=0):
    shapes = [s if isinstance(s, jax.ShapeDtypeStruct) else jax.ShapeDtypeStruct(s, F32) for s in outs]
    scr = [pltpu.VMEM(s, F32) for s in scratch]
    args = [pltpu.with_memory_space_constraint(a, pltpu.MemorySpace.HBM) if i < far_in else a for i, a in enumerate(args)]
    if sems:
        scr.append(pltpu.SemaphoreType.DMA((sems,)))
    return pl.pallas_call(
        kernel,
        out_shape=shapes,
        in_specs=[HBM if i < far_in else VMEM for i in range(len(args))],
        out_specs=[HBM if i < far_out else VMEM for i in range(len(outs))],
        scratch_shapes=scr,
        compiler_params=pltpu.CompilerParams(vmem_limit_bytes=40 * 1024 * 1024),
        name=name,
    )(*args)


def swap(v, bit):
    return lax.ppermute(v, "gx", [(i, i ^ bit) for i in range(1, 16, 2)])


def body(cotangent, saved_temp, substrate_top, deposit_top, top_class):
    cot = cotangent.reshape(512, 128)
    temp = saved_temp.reshape(512, 128)
    small = jax.ShapeDtypeStruct((8, 128), jnp.int32)
    ypack, cond, fac, ties, cot, sub, dep, cls = call(
        first_kernel,
        [(8, 40, 128), (512, 128), (3, 63, 8, 128), (12, 8, 128), (512, 128), small, small, small],
        [(512, 128), (3, 512, 128), (512, 128)],
        "first",
        cot, temp, substrate_top, deposit_top, top_class,
        far_in=5, sems=5,
    )
    gat = lax.all_to_all(ypack, "gy", split_axis=0, concat_axis=0, tiled=True)
    xpack, xfac, xhfac, a2, kh = call(
        second_kernel,
        [(456, 128), (8, 24, 8, 128), (24, 1, 128), (512, 128), (8, 128)],
        [(8, 32, 128), (512, 128), (8, 64, 128)],
        "second",
        gat, fac, ties, cond, sub,
    )
    other = lax.ppermute(xpack, "gx", [(i, i + 1) for i in range(0, 16, 2)])
    m1, sv1 = call(functools.partial(merge_kernel, 1, False), [(456, 128), (392, 128)], [], "merge_core", xpack, other)
    m2, sv2 = call(functools.partial(merge_kernel, 2, False), [(456, 128), (392, 128)], [], "merge_near", m1, swap(m1, 2))
    m3, sv3, near = call(
        functools.partial(merge_kernel, 4, True), [(456, 128), (392, 128), (200, 128)], [], "merge_far", m2, swap(m2, 6)
    )
    own, out = call(top_kernel, [(136, 128), (136, 128)], [], "top", m3, near, swap(near, 8), sv1, sv2, sv3)
    got = lax.ppermute(out, "gx", [(i + 1, i) for i in range(0, 16, 2)])
    grad_temp, grad_source = call(
        last_kernel,
        [(512, 128), (512, 128)],
        [(512, 128), (136, 128), (512, 128), (512, 128)],
        "last",
        own, got, xfac, xhfac, kh, cond, a2, cot, sub, dep, cls,
        far_out=2, sems=16,
    )
    return grad_temp.reshape(cotangent.shape), grad_source.reshape(cotangent.shape)


def solution(mesh):
    in_specs = (
        P(None, "gx", "gy"),
        P(None, "gx", "gy"),
        P("gx", "gy"),
        P("gx", "gy"),
        P("gx", "gy"),
    )
    out_specs = (P(None, "gx", "gy"), P(None, "gx", "gy"))
    return jax.shard_map(body, mesh=mesh, in_specs=in_specs, out_specs=out_specs, check_vma=False)
```

```python
import functools

import jax
import jax.numpy as jnp
from jax import lax
from jax.experimental import pallas as pl
from jax.experimental.pallas import tpu as pltpu
from jax.sharding import PartitionSpec as P

R = 1000.0
SIDE = 0.3
BOTTOM = 0.5
TOPS = (0.05, 0.25, 0.8, 2.0)
F32 = jnp.float32
NLEV = 6


def recip(v):
    return 1.0 / v


def reduce_chain(c, s, d, track):
    levels, port, ties = [], None, []
    while len(s) > 1:
        half = len(s) // 2
        ml, mr, dv = [], [], []
        for j in range(half):
            i = 2 * j
            total = s[i] + c[i]
            if j:
                total = total + c[i - 1]
            inv = recip(total)
            mr.append(c[i] * inv)
            ml.append(c[i - 1] * inv if j else None)
            dv.append(d[i] * inv)
            if track and j == 0:
                if port is None:
                    port = [dv[0], inv, mr[0]]
                    ties.append(inv)
                else:
                    p, z, t = port
                    tie = t * inv
                    ties.append(tie)
                    port = [p + t * dv[0], z + t * tie, t * mr[0]]
        ns, nd, nc = [], [], []
        for j in range(half):
            e, o = 2 * j, 2 * j + 1
            sv = s[o] + mr[j] * s[e]
            dn = d[o] + mr[j] * d[e]
            if j + 1 < half:
                sv = sv + ml[j + 1] * s[e + 2]
                dn = dn + ml[j + 1] * d[e + 2]
                nc.append(ml[j + 1] * c[e + 2])
            ns.append(sv)
            nd.append(dn)
        levels.append((dv, ml, mr))
        c, s, d = nc, ns, nd
    return s[0], d[0], levels, port, ties


def expand_chain(u_last, levels, ties, flux):
    u = [u_last]
    for lev in range(len(levels) - 1, -1, -1):
        dv, ml, mr = levels[lev]
        out = []
        for j in range(len(u)):
            even = dv[j] + mr[j] * u[j]
            if j:
                even = even + ml[j] * u[j - 1]
            elif ties is not None:
                even = even + ties[lev] * flux
            out += [even, u[j]]
        u = out
    return u


def merge_ports(a, b):
    kfa, kla, za, ta, ga, pa, qa = a
    kfb, klb, zb, tb, gb, pb, qb = b
    link = R * jnp.minimum(kla, kfb)
    lk = link * recip(1.0 + link * zb)
    inv = recip(ga + lk)
    h = inv * (qa + lk * pb)
    ti = ta * inv
    lt = lk * tb
    w = lt * inv
    merged = (
        kfa,
        klb,
        za + ta * ti,
        ta * w,
        gb + lt * tb * (ga * inv),
        pa + ta * h,
        qb + lt * (h - pb),
    )
    return merged, (h, ti, w, lk, pb, tb)


def descend(saved, flux, u_b):
    h, ti, w, lk, pb, tb = saved
    u_a = h + ti * flux + w * u_b
    flux_b = lk * (u_a - pb - tb * u_b)
    return u_a, flux_b


def film_top(cls):
    total = jnp.zeros(cls.shape, F32)
    for n in range(4):
        total = total + TOPS[n] * (cls == n).astype(F32)
    return total


def node_order(half, lev):
    base, n = 0, half
    for _ in range(lev):
        base += n
        n //= 2
    return base, n


def put_levels(ref, levels):
    half = len(levels[0][0])
    for lev, triple in enumerate(levels):
        base, n = node_order(half, lev)
        for kind in range(3):
            for j in range(n):
                if triple[kind][j] is not None:
                    ref[kind, base + j] = triple[kind][j]


def get_levels(read, half):
    levels, lev = [], 0
    while half >> lev:
        base, n = node_order(half, lev)
        levels.append(
            tuple([None if kind == 1 and j == 0 else read(kind, base + j) for j in range(n)] for kind in range(3))
        )
        lev += 1
    return levels


def first_kernel(
    cot_in, temp_in, sub_in, dep_in, cls_in, ypack, cond, fac, tie_out, cot, sub, dep, cls, temp, mid, tr, sems
):
    me_y = lax.axis_index("gy")
    pairs = ((sub_in, sub), (dep_in, dep), (temp_in, temp), (cls_in, cls), (cot_in, cot))
    copies = [pltpu.make_async_copy(a, b, sems.at[i]) for i, (a, b) in enumerate(pairs)]
    for cp in copies:
        cp.start()
    for cp in copies[:4]:
        cp.wait()
    sub_v, dep_v = sub[...], dep[...]
    top = film_top(cls[...])
    k, cap, s = [], [], []
    for z in range(64):
        under = z < sub_v
        sg = 0.5 + jax.nn.sigmoid(temp[8 * z : 8 * z + 8])
        kz = jnp.where(z < dep_v, jnp.where(under, 1.0, 0.45) * sg, 0.0)
        cond[8 * z : 8 * z + 8] = kz
        k.append(kz)
        cap.append(jnp.where(under, 1.0, 0.6))
        film = top * (dep_v - 1 == z).astype(F32)
        if z == 0:
            film = film + BOTTOM
        s.append(cap[z] + R * film)
    c = [R * jnp.minimum(k[z], k[z + 1]) for z in range(63)] + [None]
    copies[4].wait()
    d = [cot[8 * z : 8 * z + 8] for z in range(64)]
    g, q, levels, _, _ = reduce_chain(c, s, d, False)
    u = expand_chain(q * recip(g), levels, None, None)
    for z in range(64):
        tr[8 * z : 8 * z + 8] = cap[z] * u[z]

    def turned(rows, dst, q):
        block = jnp.transpose(rows)
        for h in range(2):
            dst[pl.ds(4 * h + q, 64, stride=8), :] = block[64 * h : 64 * h + 64]

    subf = sub_v.astype(F32)
    upper = (lax.broadcasted_iota(jnp.int32, (128, 128), 0) & 1) == 1
    for q in range(4):
        turned(cond[pl.ds(q, 128, stride=4), :], mid.at[0], q)
        turned(tr[pl.ds(q, 128, stride=4), :], mid.at[1], q)
        turned(jnp.where(upper, subf[q + 4 : q + 5], subf[q : q + 1]), mid.at[2], q)
    z_lane = (lax.broadcasted_iota(jnp.int32, (8, 128), 1) >> 1).astype(F32)
    row = lax.broadcasted_iota(jnp.int32, (8, 128), 0)
    ky, sy, dy = [], [], []
    for y in range(64):
        ky.append(mid[0, 8 * y : 8 * y + 8])
        dy.append(mid[1, 8 * y : 8 * y + 8])
        sy.append(jnp.where(z_lane < mid[2, 8 * y : 8 * y + 8], 1.0, 0.6))
    cap_first, cap_last = sy[0][0:4], sy[63][4:8]
    low = jnp.where(me_y == 0, R * SIDE, 0.0)
    high = jnp.where(me_y == 7, R * SIDE, 0.0)
    sy[0] = sy[0] + jnp.where(row < 4, low, 0.0)
    sy[63] = sy[63] + jnp.where(row >= 4, high, 0.0)
    cy = [R * jnp.minimum(ky[y], ky[y + 1]) for y in range(63)] + [None]
    g, q, levels, (p, zz, t), ties = reduce_chain(cy, sy, dy, True)
    put_levels(fac, levels)
    for lev in range(NLEV):
        tie_out[lev] = ties[lev]
    kf, kl = ky[0], ky[63]
    side_a = tuple(v[0:4] for v in (kf, kl, zz, t, g, p, q))
    side_b = tuple(v[4:8] for v in (kf, kl, zz, t, g, p, q))
    merged, saved = merge_ports(side_a, side_b)
    for i, v in enumerate(saved):
        tie_out[NLEV + i, 0:4] = v
    pack = jnp.concatenate(list(merged) + [cap_first, cap_last, jnp.zeros((4, 128), F32)], axis=0)
    for n in range(8):
        ypack[n] = pack


def second_kernel(gat, fac, ties, cond, sub, keep, send, xfac, xhfac, a2_out, kh_out, pick, flat, planes, xp):
    me_y = lax.axis_index("gy")
    me_x = lax.axis_index("gx")
    seg = [[gat[n, 4 * i : 4 * i + 4] for i in range(9)] for n in range(8)]
    gam, rhs = seg[0][4], seg[0][6]
    down, links = [None], [None]
    for n in range(1, 8):
        kf, kl, z, t, g, p, q = seg[n][:7]
        link = R * jnp.minimum(seg[n - 1][1], kf)
        lk = link * recip(1.0 + link * z)
        inv = recip(gam + lk)
        h = inv * (rhs + lk * p)
        lt = lk * t
        down.append((h, lt * inv))
        links.append(lk)
        rhs = q + lt * (h - p)
        gam = g + lt * t * (gam * inv)
    u = [None] * 8
    u[7] = rhs * recip(gam)
    for n in range(7, 0, -1):
        u[n - 1] = down[n][0] + down[n][1] * u[n]
    zero4 = jnp.zeros((4, 128), F32)
    fl, uf = [zero4], [None]
    for n in range(1, 8):
        kf, kl, z, t, g, p, q = seg[n][:7]
        fl.append(links[n] * (u[n - 1] - p - t * u[n]))
        uf.append(p + z * fl[n] + t * u[n])
    for n in range(8):
        rows = [fl[n], u[n]]
        if n:
            rows += [seg[n - 1][8] * u[n - 1], seg[n - 1][1], seg[n - 1][8]]
        else:
            rows += [zero4, zero4, zero4 + 1.0]
        if n < 7:
            rows += [seg[n + 1][7] * uf[n + 1], seg[n + 1][0], seg[n + 1][7]]
        else:
            rows += [zero4, zero4, zero4 + 1.0]
        for i, v in enumerate(rows):
            pick[n, 4 * i : 4 * i + 4] = v
    mine = [pick[me_y, 4 * i : 4 * i + 4] for i in range(8)]
    flux, u_b = mine[0], mine[1]
    saved = tuple(ties[NLEV + i, 0:4] for i in range(6))
    u_a, flux_b = descend(saved, flux, u_b)
    flux8 = jnp.concatenate([flux, flux_b], axis=0)
    last8 = jnp.concatenate([u_a, u_b], axis=0)
    levels = get_levels(lambda kind, i: fac[kind, i], 32)
    u_nodes = expand_chain(last8, levels, [ties[i] for i in range(NLEV)], flux8)
    for y in range(64):
        flat[8 * y : 8 * y + 8] = u_nodes[y]
    subf = sub[...]
    for q in range(4):
        planes[pl.ds(q, 128, stride=4), :] = jnp.transpose(
            jnp.concatenate([flat[pl.ds(q, 64, stride=8), :], flat[pl.ds(4 + q, 64, stride=8), :]], axis=0)
        )

    even = (lax.broadcasted_iota(jnp.int32, (4, 128), 1) & 1) == 0

    def both(left, right):
        low = jnp.where(even, left, pltpu.roll(right, 127, 1))
        high = jnp.where(even, pltpu.roll(left, 127, 1), pltpu.roll(right, 126, 1))
        return [low[x : x + 1] for x in range(4)] + [high[x : x + 1] for x in range(4)]

    dh, kh, caph = both(mine[2], mine[5]), both(mine[3], mine[6]), both(mine[4], mine[7])
    for x in range(8):
        kh_out[x : x + 1] = kh[x]

    low = jnp.where(me_x == 0, R * SIDE, 0.0)
    high = jnp.where(me_x == 15, R * SIDE, 0.0)

    def x_chain(k, cap, d):
        s = list(cap)
        s[0] = s[0] + low
        s[7] = s[7] + high
        c = [R * jnp.minimum(k[x], k[x + 1]) for x in range(7)] + [None]
        g, q, levels, (p, z, t), tie = reduce_chain(c, s, d, True)
        return levels, tie, (k[0], k[7], z, t, g, p, q)

    base_z = lax.broadcasted_iota(jnp.int32, (8, 128), 0)
    for chunk in range(8):
        zi = base_z + 8 * chunk
        k, cap, d = [], [], []
        for x in range(8):
            k.append(cond[pl.ds(64 * chunk + x, 8, stride=8), :])
            cap.append(jnp.where(zi < subf[x : x + 1], 1.0, 0.6))
            dx = cap[x] * planes[pl.ds(64 * chunk + x, 8, stride=8), :]
            a2_out[pl.ds(64 * chunk + x, 8, stride=8), :] = dx
            d.append(dx)
        levels, tie, port = x_chain(k, cap, d)
        store_x(xfac.at[chunk], levels, tie)
        for i in range(7):
            xp[i, 8 * chunk : 8 * chunk + 8] = port[i]
    levels, tie, port = x_chain(kh, caph, dh)
    store_x(xhfac, levels, tie)
    core = lax.rem(me_x, 2)
    for i in range(7):
        keep[32 * i : 32 * i + 32] = xp[i, pl.ds(pl.multiple_of(32 * core, 32), 32), :]
        send[32 * i : 32 * i + 32] = xp[i, pl.ds(pl.multiple_of(32 - 32 * core, 32), 32), :]
        keep[224 + i : 225 + i] = port[i]
        send[224 + i : 225 + i] = port[i]


def store_x(ref, levels, tie):
    for lev, triple in enumerate(levels):
        base, n = node_order(4, lev)
        for kind in range(3):
            for j in range(n):
                if triple[kind][j] is not None:
                    ref[7 * kind + base + j] = triple[kind][j]
    for lev in range(3):
        ref[21 + lev] = tie[lev]


def load_x(ref):
    levels = get_levels(lambda kind, i: ref[7 * kind + i], 4)
    return levels, [ref[21 + lev] for lev in range(3)]


def read_pack(ref, n):
    main = tuple(ref[32 * i : 32 * i + 32] for i in range(n))
    edge = tuple(ref[32 * n + i : 32 * n + i + 1] for i in range(n))
    return main, edge


def write_pack(ref, main, edge):
    n = len(main)
    for i in range(n):
        ref[32 * i : 32 * i + 32] = main[i]
        ref[32 * n + i : 32 * n + i + 1] = edge[i]


def order(right, mine, theirs):
    a = tuple(jnp.where(right, t, m) for m, t in zip(mine, theirs))
    b = tuple(jnp.where(right, m, t) for m, t in zip(mine, theirs))
    return a, b


def merge_kernel(bit, last, mine, theirs, merged_out, saved_out, *rest):
    me_x = lax.axis_index("gx")
    right = lax.rem(lax.div(me_x, bit), 2) == 1
    m, t = read_pack(mine, 7), read_pack(theirs, 7)
    done = []
    for part in range(2):
        a, b = order(right, m[part], t[part])
        done.append(merge_ports(a, b))
    write_pack(merged_out, done[0][0], done[1][0])
    write_pack(saved_out, done[0][1], done[1][1])
    if last:
        far = lax.div(me_x, 8) == 1
        outs = []
        for part in range(2):
            kf, kl, z, tt, g, p, q = done[part][0]
            gi = recip(g)
            tg = tt * gi
            outs.append(
                (
                    jnp.where(far, z + tt * tg, g),
                    jnp.where(far, p + tg * q, q),
                    jnp.where(far, kf, kl),
                )
            )
        write_pack(rest[0], outs[0], outs[1])


def top_kernel(merged, near, theirs, sv1, sv2, sv3, own, send):
    me_x = lax.axis_index("gx")
    far = lax.div(me_x, 8) == 1
    mm = read_pack(merged, 7)
    n, t = read_pack(near, 3), read_pack(theirs, 3)
    saved = [read_pack(r, 6) for r in (sv1, sv2, sv3)]
    final = []
    for part in range(2):
        (ga, qa, ka), (zb, pb, kb) = order(far, n[part], t[part])
        link = R * jnp.minimum(ka, kb)
        lk = link * recip(1.0 + link * zb)
        u_a = (qa + lk * pb) * recip(ga + lk)
        kf, kl, z, tt, g, p, q = mm[part]
        flux = jnp.where(far, lk * (u_a - pb), 0.0)
        u = jnp.where(far, (q + tt * flux) * recip(g), u_a)
        for bit, lev in ((4, 2), (2, 1)):
            right = lax.rem(lax.div(me_x, bit), 2) == 1
            ua, fb = descend(saved[lev][part], flux, u)
            flux = jnp.where(right, fb, flux)
            u = jnp.where(right, u, ua)
        ua, fb = descend(saved[0][part], flux, u)
        odd = lax.rem(me_x, 2) == 1
        final.append((jnp.where(odd, fb, flux), jnp.where(odd, u, ua), jnp.where(odd, flux, fb), jnp.where(odd, ua, u)))
    write_pack(own, final[0][:2], final[1][:2])
    send[0:32] = final[0][2]
    send[32:64] = final[0][3]


def coef_kernel(cond, kh, a2, cot, sub, dep, cls, k_y, k_l, k_z, k_s, base):
    me_y = lax.axis_index("gy")
    sub_v, dep_v, kh_v = sub[...], dep[...], kh[...]
    top = film_top(cls[...])
    lane = lax.broadcasted_iota(jnp.int32, (8, 128), 1)
    first, final = lane == 0, lane == 127
    film_y = jnp.where(first & (me_y == 0), SIDE, 0.0) + jnp.where(final & (me_y == 7), SIDE, 0.0)
    for z in range(64):
        rows = slice(8 * z, 8 * z + 8)
        k = cond[rows]
        k_h = pltpu.roll(kh_v, 128 - 2 * z, 1) if z else kh_v
        k_y[rows] = (2.0 * R) * jnp.minimum(k, jnp.where(final, k_h, pltpu.roll(k, 127, 1)))
        k_l[rows] = (2.0 * R) * jnp.minimum(k, k_h)
        if z < 63:
            k_z[rows] = (2.0 * R) * jnp.minimum(k, cond[8 * z + 8 : 8 * z + 16])
        film = film_y + top * (dep_v - 1 == z).astype(F32)
        if z == 0:
            film = film + BOTTOM
        k_s[rows] = 2.0 * jnp.where(z < sub_v, 1.0, 0.6) - (2.0 * R) * film
        base[rows] = cot[rows] - 2.0 * a2[rows]


def last_kernel(
    own, got, xfac, xhfac, k_y, k_l, k_z, k_s, base, sub, temp_out, src_out, s1, fu, t_buf, s_buf, sems
):
    core = lax.rem(lax.axis_index("gx"), 2)
    for i in range(2):
        fu[i, pl.ds(pl.multiple_of(32 * core, 32), 32), :] = own[32 * i : 32 * i + 32]
        fu[i, pl.ds(pl.multiple_of(32 - 32 * core, 32), 32), :] = got[32 * i : 32 * i + 32]
    levels, tie = load_x(xhfac)
    uh = jnp.concatenate(expand_chain(own[65:66], levels, tie, own[64:65]), axis=0)
    sub_v = sub[...]
    lane = lax.broadcasted_iota(jnp.int32, (8, 128), 1)
    first, final = lane == 0, lane == 127
    up, copies = None, []

    def expand(chunk):
        rows = slice(8 * chunk, 8 * chunk + 8)
        levels, tie = load_x(xfac.at[chunk])
        u = expand_chain(fu[1, rows], levels, tie, fu[0, rows])
        for x in range(8):
            s1[pl.ds(64 * chunk + x, 8, stride=8), :] = u[x]

    expand(0)
    for z in range(64):
        if z & 7 == 0 and z < 56:
            expand(z // 8 + 1)
        rows = slice(8 * z, 8 * z + 8)
        s = s1[rows]
        s_h = pltpu.roll(uh, 128 - 2 * z, 1) if z else uh
        f_y = k_y[rows] * (jnp.where(final, s_h, pltpu.roll(s, 127, 1)) - s)
        f_l = k_l[rows] * (s - s_h)
        total = f_y - jnp.where(first, f_l, pltpu.roll(f_y, 1, 1))
        if z < 63:
            f_z = k_z[rows] * (s1[8 * z + 8 : 8 * z + 16] - s)
            total = total + f_z
        if z:
            total = total - up
        up = f_z
        s_buf[rows] = jnp.where(z < sub_v, 1.0, 0.6) * s
        t_buf[rows] = base[rows] + k_s[rows] * s + total
        if z & 7 == 7:
            part = slice(8 * z - 56, 8 * z + 8)
            for i, (buf, out) in enumerate(((s_buf, src_out), (t_buf, temp_out))):
                cp = pltpu.make_async_copy(buf.at[part], out.at[part], sems.at[2 * (z // 8) + i])
                cp.start()
                copies.append(cp)
    for cp in copies:
        cp.wait()


VMEM = pl.BlockSpec(memory_space=pltpu.VMEM)
HBM = pl.BlockSpec(memory_space=pltpu.MemorySpace.HBM)


def call(kernel, outs, scratch, name, *args, far_in=0, far_out=0, sems=0):
    shapes = [s if isinstance(s, jax.ShapeDtypeStruct) else jax.ShapeDtypeStruct(s, F32) for s in outs]
    scr = [pltpu.VMEM(s, F32) for s in scratch]
    args = [pltpu.with_memory_space_constraint(a, pltpu.MemorySpace.HBM) if i < far_in else a for i, a in enumerate(args)]
    if sems:
        scr.append(pltpu.SemaphoreType.DMA((sems,)))
    return pl.pallas_call(
        kernel,
        out_shape=shapes,
        in_specs=[HBM if i < far_in else VMEM for i in range(len(args))],
        out_specs=[HBM if i < far_out else VMEM for i in range(len(outs))],
        scratch_shapes=scr,
        compiler_params=pltpu.CompilerParams(vmem_limit_bytes=40 * 1024 * 1024),
        name=name,
    )(*args)


def swap(v, bit):
    return lax.ppermute(v, "gx", [(i, i ^ bit) for i in range(16)])


def body(cotangent, saved_temp, substrate_top, deposit_top, top_class):
    cot = cotangent.reshape(512, 128)
    temp = saved_temp.reshape(512, 128)
    small = jax.ShapeDtypeStruct((8, 128), jnp.int32)
    ypack, cond, fac, ties, cot, sub, dep, cls = call(
        first_kernel,
        [(8, 40, 128), (512, 128), (3, 63, 8, 128), (12, 8, 128), (512, 128), small, small, small],
        [(512, 128), (3, 512, 128), (512, 128)],
        "first",
        cot, temp, substrate_top, deposit_top, top_class,
        far_in=5, sems=5,
    )
    gat = lax.all_to_all(ypack, "gy", split_axis=0, concat_axis=0, tiled=True)
    keep, send, xfac, xhfac, a2, kh = call(
        second_kernel,
        [(232, 128), (232, 128), (8, 24, 8, 128), (24, 1, 128), (512, 128), (8, 128)],
        [(8, 32, 128), (512, 128), (512, 128), (7, 64, 128)],
        "second",
        gat, fac, ties, cond, sub,
    )
    m1, sv1 = call(functools.partial(merge_kernel, 1, False), [(232, 128), (200, 128)], [], "merge_core", keep, swap(send, 1))
    m2, sv2 = call(functools.partial(merge_kernel, 2, False), [(232, 128), (200, 128)], [], "merge_near", m1, swap(m1, 2))
    m3, sv3, near = call(
        functools.partial(merge_kernel, 4, True), [(232, 128), (200, 128), (104, 128)], [], "merge_far", m2, swap(m2, 6)
    )
    sv3, kh = lax.optimization_barrier((sv3, kh))
    coefs = call(coef_kernel, [(512, 128)] * 5, [], "coef", cond, kh, a2, cot, sub, dep, cls)
    opposite = swap(near, 8)
    sv3, coefs = lax.optimization_barrier((sv3, coefs))
    own, out = call(top_kernel, [(72, 128), (64, 128)], [], "top", m3, near, opposite, sv1, sv2, sv3)
    got = swap(out, 1)
    grad_temp, grad_source = call(
        last_kernel,
        [(512, 128), (512, 128)],
        [(512, 128), (2, 64, 128), (512, 128), (512, 128)],
        "last",
        own, got, xfac, xhfac, *coefs, sub,
        far_out=2, sems=16,
    )
    return grad_temp.reshape(cotangent.shape), grad_source.reshape(cotangent.shape)


def solution(mesh):
    in_specs = (
        P(None, "gx", "gy"),
        P(None, "gx", "gy"),
        P("gx", "gy"),
        P("gx", "gy"),
        P("gx", "gy"),
    )
    out_specs = (P(None, "gx", "gy"), P(None, "gx", "gy"))
    return jax.shard_map(body, mesh=mesh, in_specs=in_specs, out_specs=out_specs, check_vma=False)
```

```python
import jax
import jax.numpy as jnp
from jax import lax
from jax.experimental import pallas as pl
from jax.experimental.pallas import tpu as pltpu
from jax.sharding import PartitionSpec as P

R = 1000.0
SIDE = 0.3
BOTTOM = 0.5
TOPS = (0.05, 0.25, 0.8, 2.0)
F32 = jnp.float32
NLEV = 6


def recip(v):
    return 1.0 / v


def reduce_chain(c, s, d, track):
    levels, port, ties = [], None, []
    while len(s) > 1:
        half = len(s) // 2
        ml, mr, dv = [], [], []
        for j in range(half):
            i = 2 * j
            total = s[i] + c[i]
            if j:
                total = total + c[i - 1]
            inv = recip(total)
            mr.append(c[i] * inv)
            ml.append(c[i - 1] * inv if j else None)
            dv.append(d[i] * inv)
            if track and j == 0:
                if port is None:
                    port = [dv[0], inv, mr[0]]
                    ties.append(inv)
                else:
                    p, z, t = port
                    tie = t * inv
                    ties.append(tie)
                    port = [p + t * dv[0], z + t * tie, t * mr[0]]
        ns, nd, nc = [], [], []
        for j in range(half):
            e, o = 2 * j, 2 * j + 1
            sv = s[o] + mr[j] * s[e]
            dn = d[o] + mr[j] * d[e]
            if j + 1 < half:
                sv = sv + ml[j + 1] * s[e + 2]
                dn = dn + ml[j + 1] * d[e + 2]
                nc.append(ml[j + 1] * c[e + 2])
            ns.append(sv)
            nd.append(dn)
        levels.append((dv, ml, mr))
        c, s, d = nc, ns, nd
    return s[0], d[0], levels, port, ties


def expand_chain(u_last, levels, ties, flux):
    u = [u_last]
    for lev in range(len(levels) - 1, -1, -1):
        dv, ml, mr = levels[lev]
        out = []
        for j in range(len(u)):
            even = dv[j] + mr[j] * u[j]
            if j:
                even = even + ml[j] * u[j - 1]
            elif ties is not None:
                even = even + ties[lev] * flux
            out += [even, u[j]]
        u = out
    return u


def merge_ports(a, b):
    kfa, kla, za, ta, ga, pa, qa = a
    kfb, klb, zb, tb, gb, pb, qb = b
    link = R * jnp.minimum(kla, kfb)
    lk = link * recip(1.0 + link * zb)
    inv = recip(ga + lk)
    h = inv * (qa + lk * pb)
    ti = ta * inv
    lt = lk * tb
    w = lt * inv
    merged = (
        kfa,
        klb,
        za + ta * ti,
        ta * w,
        gb + lt * tb * (ga * inv),
        pa + ta * h,
        qb + lt * (h - pb),
    )
    return merged, (h, ti, w, lk, pb, tb)


def descend(saved, flux, u_b):
    h, ti, w, lk, pb, tb = saved
    u_a = h + ti * flux + w * u_b
    flux_b = lk * (u_a - pb - tb * u_b)
    return u_a, flux_b


def film_top(cls):
    total = jnp.zeros(cls.shape, F32)
    for n in range(4):
        total = total + TOPS[n] * (cls == n).astype(F32)
    return total


def node_order(half, lev):
    base, n = 0, half
    for _ in range(lev):
        base += n
        n //= 2
    return base, n


def put_levels(ref, levels):
    half = len(levels[0][0])
    for lev, triple in enumerate(levels):
        base, n = node_order(half, lev)
        for kind in range(3):
            for j in range(n):
                if triple[kind][j] is not None:
                    ref[kind, base + j] = triple[kind][j]


def get_levels(read, half):
    levels, lev = [], 0
    while half >> lev:
        base, n = node_order(half, lev)
        levels.append(
            tuple([None if kind == 1 and j == 0 else read(kind, base + j) for j in range(n)] for kind in range(3))
        )
        lev += 1
    return levels


def first_kernel(
    cot_in, temp_in, sub_in, dep_in, cls_in, ypack, cond, fac, tie_out, cot, sub, dep, cls, temp, mid, tr, sems
):
    me_y = lax.axis_index("gy")
    pairs = ((sub_in, sub), (dep_in, dep), (temp_in, temp), (cls_in, cls), (cot_in, cot))
    copies = [pltpu.make_async_copy(a, b, sems.at[i]) for i, (a, b) in enumerate(pairs)]
    for cp in copies:
        cp.start()
    for cp in copies[:4]:
        cp.wait()
    sub_v, dep_v = sub[...], dep[...]
    top = film_top(cls[...])
    k, cap, s = [], [], []
    for z in range(64):
        under = z < sub_v
        sg = 0.5 + jax.nn.sigmoid(temp[8 * z : 8 * z + 8])
        kz = jnp.where(z < dep_v, jnp.where(under, 1.0, 0.45) * sg, 0.0)
        cond[8 * z : 8 * z + 8] = kz
        k.append(kz)
        cap.append(jnp.where(under, 1.0, 0.6))
        film = top * (dep_v - 1 == z).astype(F32)
        if z == 0:
            film = film + BOTTOM
        s.append(cap[z] + R * film)
    c = [R * jnp.minimum(k[z], k[z + 1]) for z in range(63)] + [None]
    copies[4].wait()
    d = [cot[8 * z : 8 * z + 8] for z in range(64)]
    g, q, levels, _, _ = reduce_chain(c, s, d, False)
    u = expand_chain(q * recip(g), levels, None, None)
    for z in range(64):
        tr[8 * z : 8 * z + 8] = cap[z] * u[z]

    def turned(rows, dst, q):
        block = jnp.transpose(rows)
        for h in range(2):
            dst[pl.ds(4 * h + q, 64, stride=8), :] = block[64 * h : 64 * h + 64]

    subf = sub_v.astype(F32)
    upper = (lax.broadcasted_iota(jnp.int32, (128, 128), 0) & 1) == 1
    for q in range(4):
        turned(cond[pl.ds(q, 128, stride=4), :], mid.at[0], q)
        turned(tr[pl.ds(q, 128, stride=4), :], mid.at[1], q)
        turned(jnp.where(upper, subf[q + 4 : q + 5], subf[q : q + 1]), mid.at[2], q)
    z_lane = (lax.broadcasted_iota(jnp.int32, (8, 128), 1) >> 1).astype(F32)
    row = lax.broadcasted_iota(jnp.int32, (8, 128), 0)
    ky, sy, dy = [], [], []
    for y in range(64):
        ky.append(mid[0, 8 * y : 8 * y + 8])
        dy.append(mid[1, 8 * y : 8 * y + 8])
        sy.append(jnp.where(z_lane < mid[2, 8 * y : 8 * y + 8], 1.0, 0.6))
    cap_first, cap_last = sy[0][0:4], sy[63][4:8]
    low = jnp.where(me_y == 0, R * SIDE, 0.0)
    high = jnp.where(me_y == 7, R * SIDE, 0.0)
    sy[0] = sy[0] + jnp.where(row < 4, low, 0.0)
    sy[63] = sy[63] + jnp.where(row >= 4, high, 0.0)
    cy = [R * jnp.minimum(ky[y], ky[y + 1]) for y in range(63)] + [None]
    g, q, levels, (p, zz, t), ties = reduce_chain(cy, sy, dy, True)
    put_levels(fac, levels)
    for lev in range(NLEV):
        tie_out[lev] = ties[lev]
    kf, kl = ky[0], ky[63]
    side_a = tuple(v[0:4] for v in (kf, kl, zz, t, g, p, q))
    side_b = tuple(v[4:8] for v in (kf, kl, zz, t, g, p, q))
    merged, saved = merge_ports(side_a, side_b)
    for i, v in enumerate(saved):
        tie_out[NLEV + i, 0:4] = v
    pack = jnp.concatenate(list(merged) + [cap_first, cap_last, jnp.zeros((4, 128), F32)], axis=0)
    for n in range(8):
        ypack[n] = pack


def second_kernel(gat, fac, ties, cond, sub, keep, send, xfac, xhfac, a2_out, kh_out, pick, flat, planes, xp):
    me_y = lax.axis_index("gy")
    me_x = lax.axis_index("gx")
    seg = [[gat[n, 4 * i : 4 * i + 4] for i in range(9)] for n in range(8)]
    gam, rhs = seg[0][4], seg[0][6]
    down, links = [None], [None]
    for n in range(1, 8):
        kf, kl, z, t, g, p, q = seg[n][:7]
        link = R * jnp.minimum(seg[n - 1][1], kf)
        lk = link * recip(1.0 + link * z)
        inv = recip(gam + lk)
        h = inv * (rhs + lk * p)
        lt = lk * t
        down.append((h, lt * inv))
        links.append(lk)
        rhs = q + lt * (h - p)
        gam = g + lt * t * (gam * inv)
    u = [None] * 8
    u[7] = rhs * recip(gam)
    for n in range(7, 0, -1):
        u[n - 1] = down[n][0] + down[n][1] * u[n]
    zero4 = jnp.zeros((4, 128), F32)
    fl, uf = [zero4], [None]
    for n in range(1, 8):
        kf, kl, z, t, g, p, q = seg[n][:7]
        fl.append(links[n] * (u[n - 1] - p - t * u[n]))
        uf.append(p + z * fl[n] + t * u[n])
    for n in range(8):
        rows = [fl[n], u[n]]
        if n:
            rows += [seg[n - 1][8] * u[n - 1], seg[n - 1][1], seg[n - 1][8]]
        else:
            rows += [zero4, zero4, zero4 + 1.0]
        if n < 7:
            rows += [seg[n + 1][7] * uf[n + 1], seg[n + 1][0], seg[n + 1][7]]
        else:
            rows += [zero4, zero4, zero4 + 1.0]
        for i, v in enumerate(rows):
            pick[n, 4 * i : 4 * i + 4] = v
    mine = [pick[me_y, 4 * i : 4 * i + 4] for i in range(8)]
    flux, u_b = mine[0], mine[1]
    saved = tuple(ties[NLEV + i, 0:4] for i in range(6))
    u_a, flux_b = descend(saved, flux, u_b)
    flux8 = jnp.concatenate([flux, flux_b], axis=0)
    last8 = jnp.concatenate([u_a, u_b], axis=0)
    levels = get_levels(lambda kind, i: fac[kind, i], 32)
    u_nodes = expand_chain(last8, levels, [ties[i] for i in range(NLEV)], flux8)
    for y in range(64):
        flat[8 * y : 8 * y + 8] = u_nodes[y]
    subf = sub[...]
    for q in range(4):
        planes[pl.ds(q, 128, stride=4), :] = jnp.transpose(
            jnp.concatenate([flat[pl.ds(q, 64, stride=8), :], flat[pl.ds(4 + q, 64, stride=8), :]], axis=0)
        )

    even = (lax.broadcasted_iota(jnp.int32, (4, 128), 1) & 1) == 0

    def both(left, right):
        low = jnp.where(even, left, pltpu.roll(right, 127, 1))
        high = jnp.where(even, pltpu.roll(left, 127, 1), pltpu.roll(right, 126, 1))
        return [low[x : x + 1] for x in range(4)] + [high[x : x + 1] for x in range(4)]

    dh, kh, caph = both(mine[2], mine[5]), both(mine[3], mine[6]), both(mine[4], mine[7])
    for x in range(8):
        kh_out[x : x + 1] = kh[x]

    low = jnp.where(me_x == 0, R * SIDE, 0.0)
    high = jnp.where(me_x == 15, R * SIDE, 0.0)

    def x_chain(k, cap, d):
        s = list(cap)
        s[0] = s[0] + low
        s[7] = s[7] + high
        c = [R * jnp.minimum(k[x], k[x + 1]) for x in range(7)] + [None]
        g, q, levels, (p, z, t), tie = reduce_chain(c, s, d, True)
        return levels, tie, (k[0], k[7], z, t, g, p, q)

    base_z = lax.broadcasted_iota(jnp.int32, (8, 128), 0)
    for chunk in range(8):
        zi = base_z + 8 * chunk
        k, cap, d = [], [], []
        for x in range(8):
            k.append(cond[pl.ds(64 * chunk + x, 8, stride=8), :])
            cap.append(jnp.where(zi < subf[x : x + 1], 1.0, 0.6))
            dx = cap[x] * planes[pl.ds(64 * chunk + x, 8, stride=8), :]
            a2_out[pl.ds(64 * chunk + x, 8, stride=8), :] = dx
            d.append(dx)
        levels, tie, port = x_chain(k, cap, d)
        store_x(xfac.at[chunk], levels, tie)
        for i in range(7):
            xp[i, 8 * chunk : 8 * chunk + 8] = port[i]
    levels, tie, port = x_chain(kh, caph, dh)
    store_x(xhfac, levels, tie)
    core = lax.rem(me_x, 2)
    for i in range(7):
        keep[32 * i : 32 * i + 32] = xp[i, pl.ds(pl.multiple_of(32 * core, 32), 32), :]
        send[32 * i : 32 * i + 32] = xp[i, pl.ds(pl.multiple_of(32 - 32 * core, 32), 32), :]
        keep[224 + i : 225 + i] = port[i]
        send[224 + i : 225 + i] = port[i]


def store_x(ref, levels, tie):
    for lev, triple in enumerate(levels):
        base, n = node_order(4, lev)
        for kind in range(3):
            for j in range(n):
                if triple[kind][j] is not None:
                    ref[7 * kind + base + j] = triple[kind][j]
    for lev in range(3):
        ref[21 + lev] = tie[lev]


def load_x(ref):
    levels = get_levels(lambda kind, i: ref[7 * kind + i], 4)
    return levels, [ref[21 + lev] for lev in range(3)]


def read_pack(ref, n):
    main = tuple(ref[32 * i : 32 * i + 32] for i in range(n))
    edge = tuple(ref[32 * n + i : 32 * n + i + 1] for i in range(n))
    return main, edge


def write_pack(ref, main, edge):
    n = len(main)
    for i in range(n):
        ref[32 * i : 32 * i + 32] = main[i]
        ref[32 * n + i : 32 * n + i + 1] = edge[i]


def order(right, mine, theirs):
    a = tuple(jnp.where(right, t, m) for m, t in zip(mine, theirs))
    b = tuple(jnp.where(right, m, t) for m, t in zip(mine, theirs))
    return a, b


def core_kernel(mine, theirs, merged_out, saved_out):
    right = lax.rem(lax.axis_index("gx"), 2) == 1
    m, t = read_pack(mine, 7), read_pack(theirs, 7)
    done = [merge_ports(*order(right, m[part], t[part])) for part in range(2)]
    write_pack(merged_out, done[0][0], done[1][0])
    write_pack(saved_out, done[0][1], done[1][1])


def ring_kernel(own, near, far, mid, merged_out, pair_out, saved_out, top_out):
    me_x = lax.axis_index("gx")
    right = lax.rem(lax.div(me_x, 2), 2) == 1
    upper = lax.rem(lax.div(me_x, 4), 2) == 1
    last = lax.div(me_x, 8) == 1
    packs = [read_pack(r, 7) for r in (own, near, mid, far)]
    pairs, saves, outs, tops = [], [], [], []
    for part in range(2):
        mine, keep = merge_ports(*order(right, packs[0][part], packs[1][part]))
        other, _ = merge_ports(*order(right, packs[2][part], packs[3][part]))
        merged, saved = merge_ports(*order(upper, mine, other))
        pairs.append(keep)
        saves.append(saved)
        outs.append(merged)
        kf, kl, z, tt, g, p, q = merged
        tg = tt * recip(g)
        tops.append((jnp.where(last, z + tt * tg, g), jnp.where(last, p + tg * q, q), jnp.where(last, kf, kl)))
    write_pack(merged_out, *outs)
    write_pack(pair_out, *pairs)
    write_pack(saved_out, *saves)
    write_pack(top_out, *tops)


def top_kernel(merged, near, theirs, sv1, sv2, sv3, own, send):
    me_x = lax.axis_index("gx")
    far = lax.div(me_x, 8) == 1
    mm = read_pack(merged, 7)
    n, t = read_pack(near, 3), read_pack(theirs, 3)
    saved = [read_pack(r, 6) for r in (sv1, sv2, sv3)]
    final = []
    for part in range(2):
        (ga, qa, ka), (zb, pb, kb) = order(far, n[part], t[part])
        link = R * jnp.minimum(ka, kb)
        lk = link * recip(1.0 + link * zb)
        u_a = (qa + lk * pb) * recip(ga + lk)
        kf, kl, z, tt, g, p, q = mm[part]
        flux = jnp.where(far, lk * (u_a - pb), 0.0)
        u = jnp.where(far, (q + tt * flux) * recip(g), u_a)
        for bit, lev in ((4, 2), (2, 1)):
            right = lax.rem(lax.div(me_x, bit), 2) == 1
            ua, fb = descend(saved[lev][part], flux, u)
            flux = jnp.where(right, fb, flux)
            u = jnp.where(right, u, ua)
        ua, fb = descend(saved[0][part], flux, u)
        odd = lax.rem(me_x, 2) == 1
        final.append((jnp.where(odd, fb, flux), jnp.where(odd, u, ua), jnp.where(odd, flux, fb), jnp.where(odd, ua, u)))
    write_pack(own, final[0][:2], final[1][:2])
    send[0:32] = final[0][2]
    send[32:64] = final[0][3]


def coef_kernel(cond, kh, a2, cot, sub, dep, cls, k_y, k_l, k_z, k_s, base):
    me_y = lax.axis_index("gy")
    sub_v, dep_v, kh_v = sub[...], dep[...], kh[...]
    top = film_top(cls[...])
    lane = lax.broadcasted_iota(jnp.int32, (8, 128), 1)
    first, final = lane == 0, lane == 127
    film_y = jnp.where(first & (me_y == 0), SIDE, 0.0) + jnp.where(final & (me_y == 7), SIDE, 0.0)
    for z in range(64):
        rows = slice(8 * z, 8 * z + 8)
        k = cond[rows]
        k_h = pltpu.roll(kh_v, 128 - 2 * z, 1) if z else kh_v
        k_y[rows] = (2.0 * R) * jnp.minimum(k, jnp.where(final, k_h, pltpu.roll(k, 127, 1)))
        k_l[rows] = (2.0 * R) * jnp.minimum(k, k_h)
        if z < 63:
            k_z[rows] = (2.0 * R) * jnp.minimum(k, cond[8 * z + 8 : 8 * z + 16])
        film = film_y + top * (dep_v - 1 == z).astype(F32)
        if z == 0:
            film = film + BOTTOM
        k_s[rows] = 2.0 * jnp.where(z < sub_v, 1.0, 0.6) - (2.0 * R) * film
        base[rows] = cot[rows] - 2.0 * a2[rows]


def last_kernel(
    own, got, xfac, xhfac, k_y, k_l, k_z, k_s, base, sub, temp_out, src_out, s1, fu, t_buf, s_buf, sems
):
    core = lax.rem(lax.axis_index("gx"), 2)
    for i in range(2):
        fu[i, pl.ds(pl.multiple_of(32 * core, 32), 32), :] = own[32 * i : 32 * i + 32]
        fu[i, pl.ds(pl.multiple_of(32 - 32 * core, 32), 32), :] = got[32 * i : 32 * i + 32]
    levels, tie = load_x(xhfac)
    uh = jnp.concatenate(expand_chain(own[65:66], levels, tie, own[64:65]), axis=0)
    sub_v = sub[...]
    lane = lax.broadcasted_iota(jnp.int32, (8, 128), 1)
    first, final = lane == 0, lane == 127
    up, copies = None, []

    def expand(chunk):
        rows = slice(8 * chunk, 8 * chunk + 8)
        levels, tie = load_x(xfac.at[chunk])
        u = expand_chain(fu[1, rows], levels, tie, fu[0, rows])
        for x in range(8):
            s1[pl.ds(64 * chunk + x, 8, stride=8), :] = u[x]

    expand(0)
    for z in range(64):
        if z & 7 == 0 and z < 56:
            expand(z // 8 + 1)
        rows = slice(8 * z, 8 * z + 8)
        s = s1[rows]
        s_h = pltpu.roll(uh, 128 - 2 * z, 1) if z else uh
        f_y = k_y[rows] * (jnp.where(final, s_h, pltpu.roll(s, 127, 1)) - s)
        f_l = k_l[rows] * (s - s_h)
        total = f_y - jnp.where(first, f_l, pltpu.roll(f_y, 1, 1))
        if z < 63:
            f_z = k_z[rows] * (s1[8 * z + 8 : 8 * z + 16] - s)
            total = total + f_z
        if z:
            total = total - up
        up = f_z
        s_buf[rows] = jnp.where(z < sub_v, 1.0, 0.6) * s
        t_buf[rows] = base[rows] + k_s[rows] * s + total
        if z & 7 == 7:
            part = slice(8 * z - 56, 8 * z + 8)
            for i, (buf, out) in enumerate(((s_buf, src_out), (t_buf, temp_out))):
                cp = pltpu.make_async_copy(buf.at[part], out.at[part], sems.at[2 * (z // 8) + i])
                cp.start()
                copies.append(cp)
    for cp in copies:
        cp.wait()


VMEM = pl.BlockSpec(memory_space=pltpu.VMEM)
HBM = pl.BlockSpec(memory_space=pltpu.MemorySpace.HBM)


def call(kernel, outs, scratch, name, *args, far_in=0, far_out=0, sems=0):
    shapes = [s if isinstance(s, jax.ShapeDtypeStruct) else jax.ShapeDtypeStruct(s, F32) for s in outs]
    scr = [pltpu.VMEM(s, F32) for s in scratch]
    args = [pltpu.with_memory_space_constraint(a, pltpu.MemorySpace.HBM) if i < far_in else a for i, a in enumerate(args)]
    if sems:
        scr.append(pltpu.SemaphoreType.DMA((sems,)))
    return pl.pallas_call(
        kernel,
        out_shape=shapes,
        in_specs=[HBM if i < far_in else VMEM for i in range(len(args))],
        out_specs=[HBM if i < far_out else VMEM for i in range(len(outs))],
        scratch_shapes=scr,
        compiler_params=pltpu.CompilerParams(vmem_limit_bytes=40 * 1024 * 1024),
        name=name,
    )(*args)


def swap(v, bit):
    return lax.ppermute(v, "gx", [(i, i ^ bit) for i in range(16)])


def body(cotangent, saved_temp, substrate_top, deposit_top, top_class):
    cot = cotangent.reshape(512, 128)
    temp = saved_temp.reshape(512, 128)
    small = jax.ShapeDtypeStruct((8, 128), jnp.int32)
    ypack, cond, fac, ties, cot, sub, dep, cls = call(
        first_kernel,
        [(8, 40, 128), (512, 128), (3, 63, 8, 128), (12, 8, 128), (512, 128), small, small, small],
        [(512, 128), (3, 512, 128), (512, 128)],
        "first",
        cot, temp, substrate_top, deposit_top, top_class,
        far_in=5, sems=5,
    )
    gat = lax.all_to_all(ypack, "gy", split_axis=0, concat_axis=0, tiled=True)
    keep, send, xfac, xhfac, a2, kh = call(
        second_kernel,
        [(232, 128), (232, 128), (8, 24, 8, 128), (24, 1, 128), (512, 128), (8, 128)],
        [(8, 32, 128), (512, 128), (512, 128), (7, 64, 128)],
        "second",
        gat, fac, ties, cond, sub,
    )
    m1, sv1 = call(core_kernel, [(232, 128), (200, 128)], [], "merge_core", keep, swap(send, 1))
    near_z = swap(m1, 2)
    far = swap(m1, 6)
    mid = swap(m1, 4)
    m3, sv2, sv3, near = call(
        ring_kernel,
        [(232, 128), (200, 128), (200, 128), (104, 128)],
        [],
        "merge_ring",
        m1, near_z, far, mid,
    )
    sv3, kh = lax.optimization_barrier((sv3, kh))
    coefs = call(coef_kernel, [(512, 128)] * 5, [], "coef", cond, kh, a2, cot, sub, dep, cls)
    opposite = swap(near, 8)
    sv3, coefs = lax.optimization_barrier((sv3, coefs))
    own, out = call(top_kernel, [(72, 128), (64, 128)], [], "top", m3, near, opposite, sv1, sv2, sv3)
    got = swap(out, 1)
    grad_temp, grad_source = call(
        last_kernel,
        [(512, 128), (512, 128)],
        [(512, 128), (2, 64, 128), (512, 128), (512, 128)],
        "last",
        own, got, xfac, xhfac, *coefs, sub,
        far_out=2, sems=16,
    )
    return grad_temp.reshape(cotangent.shape), grad_source.reshape(cotangent.shape)


def solution(mesh):
    in_specs = (
        P(None, "gx", "gy"),
        P(None, "gx", "gy"),
        P("gx", "gy"),
        P("gx", "gy"),
        P("gx", "gy"),
    )
    out_specs = (P(None, "gx", "gy"), P(None, "gx", "gy"))
    return jax.shard_map(body, mesh=mesh, in_specs=in_specs, out_specs=out_specs, check_vma=False)
```

```python
import jax
import jax.numpy as jnp
from jax import lax
from jax.experimental import pallas as pl
from jax.experimental.pallas import tpu as pltpu
from jax.sharding import PartitionSpec as P

R = 1000.0
SIDE = 0.3
BOTTOM = 0.5
TOPS = (0.05, 0.25, 0.8, 2.0)
F32 = jnp.float32
NLEV = 6


def recip(v):
    return 1.0 / v


def reduce_chain(c, s, d, track):
    levels, port, ties = [], None, []
    while len(s) > 1:
        half = len(s) // 2
        ml, mr, dv = [], [], []
        for j in range(half):
            i = 2 * j
            total = s[i] + c[i]
            if j:
                total = total + c[i - 1]
            inv = recip(total)
            mr.append(c[i] * inv)
            ml.append(c[i - 1] * inv if j else None)
            dv.append(d[i] * inv)
            if track and j == 0:
                if port is None:
                    port = [dv[0], inv, mr[0]]
                    ties.append(inv)
                else:
                    p, z, t = port
                    tie = t * inv
                    ties.append(tie)
                    port = [p + t * dv[0], z + t * tie, t * mr[0]]
        ns, nd, nc = [], [], []
        for j in range(half):
            e, o = 2 * j, 2 * j + 1
            sv = s[o] + mr[j] * s[e]
            dn = d[o] + mr[j] * d[e]
            if j + 1 < half:
                sv = sv + ml[j + 1] * s[e + 2]
                dn = dn + ml[j + 1] * d[e + 2]
                nc.append(ml[j + 1] * c[e + 2])
            ns.append(sv)
            nd.append(dn)
        levels.append((dv, ml, mr))
        c, s, d = nc, ns, nd
    return s[0], d[0], levels, port, ties


def expand_chain(u_last, levels, ties, flux):
    u = [u_last]
    for lev in range(len(levels) - 1, -1, -1):
        dv, ml, mr = levels[lev]
        out = []
        for j in range(len(u)):
            even = dv[j] + mr[j] * u[j]
            if j:
                even = even + ml[j] * u[j - 1]
            elif ties is not None:
                even = even + ties[lev] * flux
            out += [even, u[j]]
        u = out
    return u


def port_coefs(a, b):
    kfa, kla, za, ta, ga = a
    kfb, klb, zb, tb, gb = b
    link = R * jnp.minimum(kla, kfb)
    lk = link * recip(1.0 + link * zb)
    inv = recip(ga + lk)
    ti = ta * inv
    lt = lk * tb
    w = lt * inv
    merged = (kfa, klb, za + ta * ti, ta * w, gb + lt * tb * (ga * inv))
    return merged, (inv, lk, ta, lt, ti, w, tb)


def port_values(coefs, a, b):
    inv, lk, ta, lt, ti, w, tb = coefs
    pa, qa = a
    pb, qb = b
    h = inv * (qa + lk * pb)
    return (pa + ta * h, qb + lt * (h - pb)), (h, ti, w, lk, pb, tb)


def merge_ports(a, b):
    matrix, coefs = port_coefs(a[:5], b[:5])
    values, saved = port_values(coefs, a[5:], b[5:])
    return matrix + values, saved


def descend(saved, flux, u_b):
    h, ti, w, lk, pb, tb = saved
    u_a = h + ti * flux + w * u_b
    flux_b = lk * (u_a - pb - tb * u_b)
    return u_a, flux_b


def film_top(cls):
    total = jnp.zeros(cls.shape, F32)
    for n in range(4):
        total = total + TOPS[n] * (cls == n).astype(F32)
    return total


def node_order(half, lev):
    base, n = 0, half
    for _ in range(lev):
        base += n
        n //= 2
    return base, n


def put_levels(ref, levels):
    half = len(levels[0][0])
    for lev, triple in enumerate(levels):
        base, n = node_order(half, lev)
        for kind in range(3):
            for j in range(n):
                if triple[kind][j] is not None:
                    ref[kind, base + j] = triple[kind][j]


def get_levels(read, half):
    levels, lev = [], 0
    while half >> lev:
        base, n = node_order(half, lev)
        levels.append(
            tuple([None if kind == 1 and j == 0 else read(kind, base + j) for j in range(n)] for kind in range(3))
        )
        lev += 1
    return levels


def chain_matrix(c, s):
    z = t = None
    while len(s) > 1:
        half = len(s) // 2
        ml, mr = [None] * half, [None] * half
        for j in range(half):
            i = 2 * j
            inv = recip(s[i] + c[i] + c[i - 1] if j else s[i] + c[i])
            mr[j] = c[i] * inv
            if j:
                ml[j] = c[i - 1] * inv
            elif z is None:
                z, t = inv, mr[0]
            else:
                z, t = z + t * (t * inv), t * mr[0]
        ns, nc = [], []
        for j in range(half):
            e = 2 * j
            sv = s[e + 1] + mr[j] * s[e]
            if j + 1 < half:
                sv = sv + ml[j + 1] * s[e + 2]
                nc.append(ml[j + 1] * c[e + 2])
            ns.append(sv)
        c, s = nc, ns
    return z, t, s[0]


def wall_terms():
    me_x = lax.axis_index("gx")
    return jnp.where(me_x == 0, R * SIDE, 0.0), jnp.where(me_x == 15, R * SIDE, 0.0)


def split_halves(planes, keep, send):
    core = lax.rem(lax.axis_index("gx"), 2)
    for i in range(planes.shape[0]):
        keep[32 * i : 32 * i + 32] = planes[i, pl.ds(pl.multiple_of(32 * core, 32), 32), :]
        send[32 * i : 32 * i + 32] = planes[i, pl.ds(pl.multiple_of(32 - 32 * core, 32), 32), :]


def fields_kernel(cot_in, temp_in, sub_in, dep_in, cls_in, cond, keep, send, cot, sub, dep, cls, temp, planes, sems):
    pairs = ((sub_in, sub), (dep_in, dep), (temp_in, temp), (cls_in, cls), (cot_in, cot))
    copies = [pltpu.make_async_copy(a, b, sems.at[i]) for i, (a, b) in enumerate(pairs)]
    for cp in copies:
        cp.start()
    for cp in copies[:3]:
        cp.wait()
    sub_v, dep_v = sub[...], dep[...]
    for z in range(64):
        base = jnp.where(z < sub_v, 1.0, 0.45)
        sg = 0.5 + jax.nn.sigmoid(temp[8 * z : 8 * z + 8])
        cond[8 * z : 8 * z + 8] = jnp.where(z < dep_v, base * sg, 0.0)
    low, high = wall_terms()
    base_z = lax.broadcasted_iota(jnp.int32, (8, 128), 0)
    for chunk in range(8):
        zi = base_z + 8 * chunk
        k = [cond[pl.ds(64 * chunk + x, 8, stride=8), :] for x in range(8)]
        s = [jnp.where(zi < sub_v[x : x + 1], 1.0, 0.6) for x in range(8)]
        s[0] = s[0] + low
        s[7] = s[7] + high
        c = [R * jnp.minimum(k[x], k[x + 1]) for x in range(7)] + [None]
        for i, v in enumerate((k[0], k[7]) + chain_matrix(c, s)):
            planes[i, 8 * chunk : 8 * chunk + 8] = v
    split_halves(planes, keep, send)
    for cp in copies[3:]:
        cp.wait()


def first_kernel(cot, sub, dep, cls, cond, ypack, fac, tie_out, mid, tr):
    me_y = lax.axis_index("gy")
    sub_v, dep_v = sub[...], dep[...]
    top = film_top(cls[...])
    k, cap, s = [], [], []
    for z in range(64):
        k.append(cond[8 * z : 8 * z + 8])
        cap.append(jnp.where(z < sub_v, 1.0, 0.6))
        film = top * (dep_v - 1 == z).astype(F32)
        if z == 0:
            film = film + BOTTOM
        s.append(cap[z] + R * film)
    c = [R * jnp.minimum(k[z], k[z + 1]) for z in range(63)] + [None]
    d = [cot[8 * z : 8 * z + 8] for z in range(64)]
    g, q, levels, _, _ = reduce_chain(c, s, d, False)
    u = expand_chain(q * recip(g), levels, None, None)
    for z in range(64):
        tr[8 * z : 8 * z + 8] = cap[z] * u[z]

    def turned(rows, dst, q):
        block = jnp.transpose(rows)
        for h in range(2):
            dst[pl.ds(4 * h + q, 64, stride=8), :] = block[64 * h : 64 * h + 64]

    subf = sub_v.astype(F32)
    upper = (lax.broadcasted_iota(jnp.int32, (128, 128), 0) & 1) == 1
    for q in range(4):
        turned(cond[pl.ds(q, 128, stride=4), :], mid.at[0], q)
        turned(tr[pl.ds(q, 128, stride=4), :], mid.at[1], q)
        turned(jnp.where(upper, subf[q + 4 : q + 5], subf[q : q + 1]), mid.at[2], q)
    z_lane = (lax.broadcasted_iota(jnp.int32, (8, 128), 1) >> 1).astype(F32)
    row = lax.broadcasted_iota(jnp.int32, (8, 128), 0)
    ky, sy, dy = [], [], []
    for y in range(64):
        ky.append(mid[0, 8 * y : 8 * y + 8])
        dy.append(mid[1, 8 * y : 8 * y + 8])
        sy.append(jnp.where(z_lane < mid[2, 8 * y : 8 * y + 8], 1.0, 0.6))
    cap_first, cap_last = sy[0][0:4], sy[63][4:8]
    low = jnp.where(me_y == 0, R * SIDE, 0.0)
    high = jnp.where(me_y == 7, R * SIDE, 0.0)
    sy[0] = sy[0] + jnp.where(row < 4, low, 0.0)
    sy[63] = sy[63] + jnp.where(row >= 4, high, 0.0)
    cy = [R * jnp.minimum(ky[y], ky[y + 1]) for y in range(63)] + [None]
    g, q, levels, (p, zz, t), ties = reduce_chain(cy, sy, dy, True)
    put_levels(fac, levels)
    for lev in range(NLEV):
        tie_out[lev] = ties[lev]
    kf, kl = ky[0], ky[63]
    side_a = tuple(v[0:4] for v in (kf, kl, zz, t, g, p, q))
    side_b = tuple(v[4:8] for v in (kf, kl, zz, t, g, p, q))
    merged, saved = merge_ports(side_a, side_b)
    for i, v in enumerate(saved):
        tie_out[NLEV + i, 0:4] = v
    pack = jnp.concatenate(list(merged) + [cap_first, cap_last, jnp.zeros((4, 128), F32)], axis=0)
    for n in range(8):
        ypack[n] = pack


def second_kernel(gat, fac, ties, cond, sub, keep, send, xfac, xhfac, a2_out, kh_out, pick, flat, planes, xp):
    me_y = lax.axis_index("gy")
    seg = [[gat[n, 4 * i : 4 * i + 4] for i in range(9)] for n in range(8)]
    gam, rhs = seg[0][4], seg[0][6]
    down, links = [None], [None]
    for n in range(1, 8):
        kf, kl, z, t, g, p, q = seg[n][:7]
        link = R * jnp.minimum(seg[n - 1][1], kf)
        lk = link * recip(1.0 + link * z)
        inv = recip(gam + lk)
        h = inv * (rhs + lk * p)
        lt = lk * t
        down.append((h, lt * inv))
        links.append(lk)
        rhs = q + lt * (h - p)
        gam = g + lt * t * (gam * inv)
    u = [None] * 8
    u[7] = rhs * recip(gam)
    for n in range(7, 0, -1):
        u[n - 1] = down[n][0] + down[n][1] * u[n]
    zero4 = jnp.zeros((4, 128), F32)
    fl, uf = [zero4], [None]
    for n in range(1, 8):
        kf, kl, z, t, g, p, q = seg[n][:7]
        fl.append(links[n] * (u[n - 1] - p - t * u[n]))
        uf.append(p + z * fl[n] + t * u[n])
    for n in range(8):
        rows = [fl[n], u[n]]
        if n:
            rows += [seg[n - 1][8] * u[n - 1], seg[n - 1][1], seg[n - 1][8]]
        else:
            rows += [zero4, zero4, zero4 + 1.0]
        if n < 7:
            rows += [seg[n + 1][7] * uf[n + 1], seg[n + 1][0], seg[n + 1][7]]
        else:
            rows += [zero4, zero4, zero4 + 1.0]
        for i, v in enumerate(rows):
            pick[n, 4 * i : 4 * i + 4] = v
    mine = [pick[me_y, 4 * i : 4 * i + 4] for i in range(8)]
    flux, u_b = mine[0], mine[1]
    saved = tuple(ties[NLEV + i, 0:4] for i in range(6))
    u_a, flux_b = descend(saved, flux, u_b)
    flux8 = jnp.concatenate([flux, flux_b], axis=0)
    last8 = jnp.concatenate([u_a, u_b], axis=0)
    levels = get_levels(lambda kind, i: fac[kind, i], 32)
    u_nodes = expand_chain(last8, levels, [ties[i] for i in range(NLEV)], flux8)
    for y in range(64):
        flat[8 * y : 8 * y + 8] = u_nodes[y]
    subf = sub[...]
    for q in range(4):
        planes[pl.ds(q, 128, stride=4), :] = jnp.transpose(
            jnp.concatenate([flat[pl.ds(q, 64, stride=8), :], flat[pl.ds(4 + q, 64, stride=8), :]], axis=0)
        )

    even = (lax.broadcasted_iota(jnp.int32, (4, 128), 1) & 1) == 0

    def both(left, right):
        low = jnp.where(even, left, pltpu.roll(right, 127, 1))
        high = jnp.where(even, pltpu.roll(left, 127, 1), pltpu.roll(right, 126, 1))
        return [low[x : x + 1] for x in range(4)] + [high[x : x + 1] for x in range(4)]

    dh, kh, caph = both(mine[2], mine[5]), both(mine[3], mine[6]), both(mine[4], mine[7])
    for x in range(8):
        kh_out[x : x + 1] = kh[x]

    low, high = wall_terms()

    def x_chain(k, cap, d):
        s = list(cap)
        s[0] = s[0] + low
        s[7] = s[7] + high
        c = [R * jnp.minimum(k[x], k[x + 1]) for x in range(7)] + [None]
        g, q, levels, (p, z, t), tie = reduce_chain(c, s, d, True)
        return levels, tie, (k[0], k[7], z, t, g, p, q)

    base_z = lax.broadcasted_iota(jnp.int32, (8, 128), 0)
    for chunk in range(8):
        zi = base_z + 8 * chunk
        k, cap, d = [], [], []
        for x in range(8):
            k.append(cond[pl.ds(64 * chunk + x, 8, stride=8), :])
            cap.append(jnp.where(zi < subf[x : x + 1], 1.0, 0.6))
            dx = cap[x] * planes[pl.ds(64 * chunk + x, 8, stride=8), :]
            a2_out[pl.ds(64 * chunk + x, 8, stride=8), :] = dx
            d.append(dx)
        levels, tie, port = x_chain(k, cap, d)
        store_x(xfac.at[chunk], levels, tie)
        for i in range(2):
            xp[i, 8 * chunk : 8 * chunk + 8] = port[5 + i]
    levels, tie, port = x_chain(kh, caph, dh)
    store_x(xhfac, levels, tie)
    split_halves(xp, keep, send)
    for i in range(7):
        keep[64 + i : 65 + i] = port[i]
        send[64 + i : 65 + i] = port[i]


def store_x(ref, levels, tie):
    for lev, triple in enumerate(levels):
        base, n = node_order(4, lev)
        for kind in range(3):
            for j in range(n):
                if triple[kind][j] is not None:
                    ref[7 * kind + base + j] = triple[kind][j]
    for lev in range(3):
        ref[21 + lev] = tie[lev]


def load_x(ref):
    levels = get_levels(lambda kind, i: ref[7 * kind + i], 4)
    return levels, [ref[21 + lev] for lev in range(3)]


def read_pack(ref, n):
    main = tuple(ref[32 * i : 32 * i + 32] for i in range(n))
    edge = tuple(ref[32 * n + i : 32 * n + i + 1] for i in range(n))
    return main, edge


def write_pack(ref, main, edge):
    n = len(main)
    for i in range(n):
        ref[32 * i : 32 * i + 32] = main[i]
        ref[32 * n + i : 32 * n + i + 1] = edge[i]


def order(right, mine, theirs):
    a = tuple(jnp.where(right, t, m) for m, t in zip(mine, theirs))
    b = tuple(jnp.where(right, m, t) for m, t in zip(mine, theirs))
    return a, b


def planes_of(ref, n):
    return tuple(ref[32 * i : 32 * i + 32] for i in range(n))


def put_planes(ref, values):
    for i, v in enumerate(values):
        ref[32 * i : 32 * i + 32] = v


def spots():
    me_x = lax.axis_index("gx")
    return [lax.rem(lax.div(me_x, bit), 2) == 1 for bit in (1, 2, 4)]


def core_matrix_kernel(mine, theirs, merged_out, coef_out):
    odd, _, _ = spots()
    merged, coefs = port_coefs(*order(odd, planes_of(mine, 5), planes_of(theirs, 5)))
    put_planes(merged_out, merged)
    put_planes(coef_out, coefs)


def ring_matrix_kernel(own, near, far, mid, merged_out, mine_out, other_out, ring_out):
    _, right, upper = spots()
    packs = [planes_of(r, 5) for r in (own, near, mid, far)]
    mine, mine_c = port_coefs(*order(right, packs[0], packs[1]))
    other, other_c = port_coefs(*order(right, packs[2], packs[3]))
    merged, ring_c = port_coefs(*order(upper, mine, other))
    put_planes(merged_out, merged)
    put_planes(mine_out, mine_c)
    put_planes(other_out, other_c)
    put_planes(ring_out, ring_c)


def read_sides(ref):
    main = (ref[0:32], ref[32:64])
    edge = tuple(ref[64 + i : 65 + i] for i in range(7))
    return main, edge


def core_kernel(mine, theirs, coefs, merged_out, saved_out):
    odd, _, _ = spots()
    m, t = read_sides(mine), read_sides(theirs)
    values, saved = port_values(planes_of(coefs, 7), *order(odd, m[0], t[0]))
    edge, edge_saved = merge_ports(*order(odd, m[1], t[1]))
    put_planes(merged_out, values)
    for i in range(7):
        merged_out[64 + i : 65 + i] = edge[i]
    write_pack(saved_out, saved, edge_saved)


def ring_kernel(own, near, far, mid, matrix, mine_c, other_c, ring_c, merged_out, pair_out, saved_out, top_out):
    _, right, upper = spots()
    last = lax.div(lax.axis_index("gx"), 8) == 1
    main, edge = zip(*[read_sides(r) for r in (own, near, mid, far)])
    mine, pair = port_values(planes_of(mine_c, 7), *order(right, main[0], main[1]))
    other, _ = port_values(planes_of(other_c, 7), *order(right, main[2], main[3]))
    values, saved = port_values(planes_of(ring_c, 7), *order(upper, mine, other))
    e_mine, e_pair = merge_ports(*order(right, edge[0], edge[1]))
    e_other, _ = merge_ports(*order(right, edge[2], edge[3]))
    e_merged, e_saved = merge_ports(*order(upper, e_mine, e_other))
    outs = [planes_of(matrix, 5) + values, e_merged]
    tops = []
    for kf, kl, z, tt, g, p, q in outs:
        tg = tt * recip(g)
        tops.append((jnp.where(last, z + tt * tg, g), jnp.where(last, p + tg * q, q), jnp.where(last, kf, kl)))
    write_pack(merged_out, *outs)
    write_pack(pair_out, pair, e_pair)
    write_pack(saved_out, saved, e_saved)
    write_pack(top_out, *tops)


def top_kernel(merged, near, theirs, sv1, sv2, sv3, own, send):
    me_x = lax.axis_index("gx")
    far = lax.div(me_x, 8) == 1
    mm = read_pack(merged, 7)
    n, t = read_pack(near, 3), read_pack(theirs, 3)
    saved = [read_pack(r, 6) for r in (sv1, sv2, sv3)]
    final = []
    for part in range(2):
        (ga, qa, ka), (zb, pb, kb) = order(far, n[part], t[part])
        link = R * jnp.minimum(ka, kb)
        lk = link * recip(1.0 + link * zb)
        u_a = (qa + lk * pb) * recip(ga + lk)
        kf, kl, z, tt, g, p, q = mm[part]
        flux = jnp.where(far, lk * (u_a - pb), 0.0)
        u = jnp.where(far, (q + tt * flux) * recip(g), u_a)
        for bit, lev in ((4, 2), (2, 1)):
            right = lax.rem(lax.div(me_x, bit), 2) == 1
            ua, fb = descend(saved[lev][part], flux, u)
            flux = jnp.where(right, fb, flux)
            u = jnp.where(right, u, ua)
        ua, fb = descend(saved[0][part], flux, u)
        odd = lax.rem(me_x, 2) == 1
        final.append((jnp.where(odd, fb, flux), jnp.where(odd, u, ua), jnp.where(odd, flux, fb), jnp.where(odd, ua, u)))
    write_pack(own, final[0][:2], final[1][:2])
    send[0:32] = final[0][2]
    send[32:64] = final[0][3]


def coef_kernel(cond, kh, a2, cot, sub, dep, cls, k_y, k_l, k_z, k_s, base):
    me_y = lax.axis_index("gy")
    sub_v, dep_v, kh_v = sub[...], dep[...], kh[...]
    top = film_top(cls[...])
    lane = lax.broadcasted_iota(jnp.int32, (8, 128), 1)
    first, final = lane == 0, lane == 127
    film_y = jnp.where(first & (me_y == 0), SIDE, 0.0) + jnp.where(final & (me_y == 7), SIDE, 0.0)
    for z in range(64):
        rows = slice(8 * z, 8 * z + 8)
        k = cond[rows]
        k_h = pltpu.roll(kh_v, 128 - 2 * z, 1) if z else kh_v
        k_y[rows] = (2.0 * R) * jnp.minimum(k, jnp.where(final, k_h, pltpu.roll(k, 127, 1)))
        k_l[rows] = (2.0 * R) * jnp.minimum(k, k_h)
        if z < 63:
            k_z[rows] = (2.0 * R) * jnp.minimum(k, cond[8 * z + 8 : 8 * z + 16])
        film = film_y + top * (dep_v - 1 == z).astype(F32)
        if z == 0:
            film = film + BOTTOM
        k_s[rows] = 2.0 * jnp.where(z < sub_v, 1.0, 0.6) - (2.0 * R) * film
        base[rows] = cot[rows] - 2.0 * a2[rows]


def last_kernel(
    own, got, xfac, xhfac, k_y, k_l, k_z, k_s, base, sub, temp_out, src_out, s1, fu, t_buf, s_buf, sems
):
    core = lax.rem(lax.axis_index("gx"), 2)
    for i in range(2):
        fu[i, pl.ds(pl.multiple_of(32 * core, 32), 32), :] = own[32 * i : 32 * i + 32]
        fu[i, pl.ds(pl.multiple_of(32 - 32 * core, 32), 32), :] = got[32 * i : 32 * i + 32]
    levels, tie = load_x(xhfac)
    uh = jnp.concatenate(expand_chain(own[65:66], levels, tie, own[64:65]), axis=0)
    sub_v = sub[...]
    lane = lax.broadcasted_iota(jnp.int32, (8, 128), 1)
    first, final = lane == 0, lane == 127
    up, copies = None, []

    def expand(chunk):
        rows = slice(8 * chunk, 8 * chunk + 8)
        levels, tie = load_x(xfac.at[chunk])
        u = expand_chain(fu[1, rows], levels, tie, fu[0, rows])
        for x in range(8):
            s1[pl.ds(64 * chunk + x, 8, stride=8), :] = u[x]

    expand(0)
    for z in range(64):
        if z & 7 == 0 and z < 56:
            expand(z // 8 + 1)
        rows = slice(8 * z, 8 * z + 8)
        s = s1[rows]
        s_h = pltpu.roll(uh, 128 - 2 * z, 1) if z else uh
        f_y = k_y[rows] * (jnp.where(final, s_h, pltpu.roll(s, 127, 1)) - s)
        f_l = k_l[rows] * (s - s_h)
        total = f_y - jnp.where(first, f_l, pltpu.roll(f_y, 1, 1))
        if z < 63:
            f_z = k_z[rows] * (s1[8 * z + 8 : 8 * z + 16] - s)
            total = total + f_z
        if z:
            total = total - up
        up = f_z
        s_buf[rows] = jnp.where(z < sub_v, 1.0, 0.6) * s
        t_buf[rows] = base[rows] + k_s[rows] * s + total
        if z & 7 == 7:
            part = slice(8 * z - 56, 8 * z + 8)
            for i, (buf, out) in enumerate(((s_buf, src_out), (t_buf, temp_out))):
                cp = pltpu.make_async_copy(buf.at[part], out.at[part], sems.at[2 * (z // 8) + i])
                cp.start()
                copies.append(cp)
    for cp in copies:
        cp.wait()


VMEM = pl.BlockSpec(memory_space=pltpu.VMEM)
HBM = pl.BlockSpec(memory_space=pltpu.MemorySpace.HBM)


def call(kernel, outs, scratch, name, *args, far_in=0, far_out=0, sems=0):
    shapes = [s if isinstance(s, jax.ShapeDtypeStruct) else jax.ShapeDtypeStruct(s, F32) for s in outs]
    scr = [pltpu.VMEM(s, F32) for s in scratch]
    args = [pltpu.with_memory_space_constraint(a, pltpu.MemorySpace.HBM) if i < far_in else a for i, a in enumerate(args)]
    if sems:
        scr.append(pltpu.SemaphoreType.DMA((sems,)))
    return pl.pallas_call(
        kernel,
        out_shape=shapes,
        in_specs=[HBM if i < far_in else VMEM for i in range(len(args))],
        out_specs=[HBM if i < far_out else VMEM for i in range(len(outs))],
        scratch_shapes=scr,
        compiler_params=pltpu.CompilerParams(vmem_limit_bytes=40 * 1024 * 1024),
        name=name,
    )(*args)


def swap(v, bit):
    return lax.ppermute(v, "gx", [(i, i ^ bit) for i in range(16)])


def body(cotangent, saved_temp, substrate_top, deposit_top, top_class):
    cot = cotangent.reshape(512, 128)
    temp = saved_temp.reshape(512, 128)
    small = jax.ShapeDtypeStruct((8, 128), jnp.int32)
    cond, keep_m, send_m, cot, sub, dep, cls = call(
        fields_kernel,
        [(512, 128), (160, 128), (160, 128), (512, 128), small, small, small],
        [(512, 128), (5, 64, 128)],
        "fields",
        cot, temp, substrate_top, deposit_top, top_class,
        far_in=5, sems=5,
    )
    other_m = swap(send_m, 1)
    ypack, fac, ties = call(
        first_kernel,
        [(8, 40, 128), (3, 63, 8, 128), (12, 8, 128)],
        [(3, 512, 128), (512, 128)],
        "first",
        cot, sub, dep, cls, cond,
    )
    gat = lax.all_to_all(ypack, "gy", split_axis=0, concat_axis=0, tiled=True)
    mm, core_c = call(core_matrix_kernel, [(160, 128), (224, 128)], [], "matrix_core", keep_m, other_m)
    ring_m = [swap(mm, bit) for bit in (2, 6, 4)]
    keep, send, xfac, xhfac, a2, kh = call(
        second_kernel,
        [(72, 128), (72, 128), (8, 24, 8, 128), (24, 1, 128), (512, 128), (8, 128)],
        [(8, 32, 128), (512, 128), (512, 128), (2, 64, 128)],
        "second",
        gat, fac, ties, cond, sub,
    )
    m1, sv1 = call(core_kernel, [(72, 128), (200, 128)], [], "merge_core", keep, swap(send, 1), core_c)
    ring_v = [swap(m1, bit) for bit in (2, 6, 4)]
    matrix, mine_c, other_c, ring_c = call(
        ring_matrix_kernel, [(160, 128)] + [(224, 128)] * 3, [], "matrix_ring", mm, *ring_m
    )
    m3, sv2, sv3, near = call(
        ring_kernel,
        [(232, 128), (200, 128), (200, 128), (104, 128)],
        [],
        "merge_ring",
        m1, *ring_v, matrix, mine_c, other_c, ring_c,
    )
    sv3, kh = lax.optimization_barrier((sv3, kh))
    coefs = call(coef_kernel, [(512, 128)] * 5, [], "coef", cond, kh, a2, cot, sub, dep, cls)
    opposite = swap(near, 8)
    sv3, coefs = lax.optimization_barrier((sv3, coefs))
    own, out = call(top_kernel, [(72, 128), (64, 128)], [], "top", m3, near, opposite, sv1, sv2, sv3)
    got = swap(out, 1)
    grad_temp, grad_source = call(
        last_kernel,
        [(512, 128), (512, 128)],
        [(512, 128), (2, 64, 128), (512, 128), (512, 128)],
        "last",
        own, got, xfac, xhfac, *coefs, sub,
        far_out=2, sems=16,
    )
    return grad_temp.reshape(cotangent.shape), grad_source.reshape(cotangent.shape)


def solution(mesh):
    in_specs = (
        P(None, "gx", "gy"),
        P(None, "gx", "gy"),
        P("gx", "gy"),
        P("gx", "gy"),
        P("gx", "gy"),
    )
    out_specs = (P(None, "gx", "gy"), P(None, "gx", "gy"))
    return jax.shard_map(body, mesh=mesh, in_specs=in_specs, out_specs=out_specs, check_vma=False)
```

```python
import jax
import jax.numpy as jnp
from jax import lax
from jax.experimental import pallas as pl
from jax.experimental.pallas import tpu as pltpu
from jax.sharding import PartitionSpec as P

R = 1000.0
SIDE = 0.3
BOTTOM = 0.5
TOPS = (0.05, 0.25, 0.8, 2.0)
F32 = jnp.float32
NLEV = 6


def recip(v):
    return 1.0 / v


def reduce_chain(c, s, d, track):
    levels, port, ties = [], None, []
    while len(s) > 1:
        half = len(s) // 2
        ml, mr, dv = [], [], []
        for j in range(half):
            i = 2 * j
            total = s[i] + c[i]
            if j:
                total = total + c[i - 1]
            inv = recip(total)
            mr.append(c[i] * inv)
            ml.append(c[i - 1] * inv if j else None)
            dv.append(d[i] * inv)
            if track and j == 0:
                if port is None:
                    port = [dv[0], inv, mr[0]]
                    ties.append(inv)
                else:
                    p, z, t = port
                    tie = t * inv
                    ties.append(tie)
                    port = [p + t * dv[0], z + t * tie, t * mr[0]]
        ns, nd, nc = [], [], []
        for j in range(half):
            e, o = 2 * j, 2 * j + 1
            sv = s[o] + mr[j] * s[e]
            dn = d[o] + mr[j] * d[e]
            if j + 1 < half:
                sv = sv + ml[j + 1] * s[e + 2]
                dn = dn + ml[j + 1] * d[e + 2]
                nc.append(ml[j + 1] * c[e + 2])
            ns.append(sv)
            nd.append(dn)
        levels.append((dv, ml, mr))
        c, s, d = nc, ns, nd
    return s[0], d[0], levels, port, ties


def expand_chain(u_last, levels, ties, flux):
    u = [u_last]
    for lev in range(len(levels) - 1, -1, -1):
        dv, ml, mr = levels[lev]
        out = []
        for j in range(len(u)):
            even = dv[j] + mr[j] * u[j]
            if j:
                even = even + ml[j] * u[j - 1]
            elif ties is not None:
                even = even + ties[lev] * flux
            out += [even, u[j]]
        u = out
    return u


def port_coefs(a, b):
    kfa, kla, za, ta, ga = a
    kfb, klb, zb, tb, gb = b
    link = R * jnp.minimum(kla, kfb)
    lk = link * recip(1.0 + link * zb)
    inv = recip(ga + lk)
    ti = ta * inv
    lt = lk * tb
    w = lt * inv
    merged = (kfa, klb, za + ta * ti, ta * w, gb + lt * tb * (ga * inv))
    return merged, (inv, lk, ta, lt, ti, w, tb)


def port_values(coefs, a, b):
    inv, lk, ta, lt, ti, w, tb = coefs
    pa, qa = a
    pb, qb = b
    h = inv * (qa + lk * pb)
    return (pa + ta * h, qb + lt * (h - pb)), (h, ti, w, lk, pb, tb)


def merge_ports(a, b):
    matrix, coefs = port_coefs(a[:5], b[:5])
    values, saved = port_values(coefs, a[5:], b[5:])
    return matrix + values, saved


def descend(saved, flux, u_b):
    h, ti, w, lk, pb, tb = saved
    u_a = h + ti * flux + w * u_b
    flux_b = lk * (u_a - pb - tb * u_b)
    return u_a, flux_b


def film_top(cls):
    total = jnp.zeros(cls.shape, F32)
    for n in range(4):
        total = total + TOPS[n] * (cls == n).astype(F32)
    return total


def node_order(half, lev):
    base, n = 0, half
    for _ in range(lev):
        base += n
        n //= 2
    return base, n


def put_levels(ref, levels):
    half = len(levels[0][0])
    for lev, triple in enumerate(levels):
        base, n = node_order(half, lev)
        for kind in range(3):
            for j in range(n):
                if triple[kind][j] is not None:
                    ref[kind, base + j] = triple[kind][j]


def get_levels(read, half):
    levels, lev = [], 0
    while half >> lev:
        base, n = node_order(half, lev)
        levels.append(
            tuple([None if kind == 1 and j == 0 else read(kind, base + j) for j in range(n)] for kind in range(3))
        )
        lev += 1
    return levels


def chain_matrix(c, s):
    z = t = None
    while len(s) > 1:
        half = len(s) // 2
        ml, mr = [None] * half, [None] * half
        for j in range(half):
            i = 2 * j
            inv = recip(s[i] + c[i] + c[i - 1] if j else s[i] + c[i])
            mr[j] = c[i] * inv
            if j:
                ml[j] = c[i - 1] * inv
            elif z is None:
                z, t = inv, mr[0]
            else:
                z, t = z + t * (t * inv), t * mr[0]
        ns, nc = [], []
        for j in range(half):
            e = 2 * j
            sv = s[e + 1] + mr[j] * s[e]
            if j + 1 < half:
                sv = sv + ml[j + 1] * s[e + 2]
                nc.append(ml[j + 1] * c[e + 2])
            ns.append(sv)
        c, s = nc, ns
    return z, t, s[0]


def wall_terms():
    me_x = lax.axis_index("gx")
    return jnp.where(me_x == 0, R * SIDE, 0.0), jnp.where(me_x == 15, R * SIDE, 0.0)


def own_half():
    me_x = lax.axis_index("gx")
    return lax.rem(me_x + lax.div(me_x, 2) + lax.div(me_x, 8), 2)


def split_halves(planes, keep, send):
    core = own_half()
    for i in range(planes.shape[0]):
        keep[32 * i : 32 * i + 32] = planes[i, pl.ds(pl.multiple_of(32 * core, 32), 32), :]
        send[32 * i : 32 * i + 32] = planes[i, pl.ds(pl.multiple_of(32 - 32 * core, 32), 32), :]


def fields_kernel(cot_in, temp_in, sub_in, dep_in, cls_in, cond, keep, send, cot, sub, dep, cls, temp, planes, sems):
    pairs = ((sub_in, sub), (dep_in, dep), (temp_in, temp), (cls_in, cls), (cot_in, cot))
    copies = [pltpu.make_async_copy(a, b, sems.at[i]) for i, (a, b) in enumerate(pairs)]
    for cp in copies:
        cp.start()
    for cp in copies[:3]:
        cp.wait()
    sub_v, dep_v = sub[...], dep[...]
    for z in range(64):
        base = jnp.where(z < sub_v, 1.0, 0.45)
        sg = 0.5 + jax.nn.sigmoid(temp[8 * z : 8 * z + 8])
        cond[8 * z : 8 * z + 8] = jnp.where(z < dep_v, base * sg, 0.0)
    low, high = wall_terms()
    base_z = lax.broadcasted_iota(jnp.int32, (8, 128), 0)
    for chunk in range(8):
        zi = base_z + 8 * chunk
        k = [cond[pl.ds(64 * chunk + x, 8, stride=8), :] for x in range(8)]
        s = [jnp.where(zi < sub_v[x : x + 1], 1.0, 0.6) for x in range(8)]
        s[0] = s[0] + low
        s[7] = s[7] + high
        c = [R * jnp.minimum(k[x], k[x + 1]) for x in range(7)] + [None]
        for i, v in enumerate((k[0], k[7]) + chain_matrix(c, s)):
            planes[i, 8 * chunk : 8 * chunk + 8] = v
    split_halves(planes, keep, send)
    for cp in copies[3:]:
        cp.wait()


def first_kernel(cot, sub, dep, cls, cond, ypack, fac, tie_out, mid, tr):
    me_y = lax.axis_index("gy")
    sub_v, dep_v = sub[...], dep[...]
    top = film_top(cls[...])
    k, cap, s = [], [], []
    for z in range(64):
        k.append(cond[8 * z : 8 * z + 8])
        cap.append(jnp.where(z < sub_v, 1.0, 0.6))
        film = top * (dep_v - 1 == z).astype(F32)
        if z == 0:
            film = film + BOTTOM
        s.append(cap[z] + R * film)
    c = [R * jnp.minimum(k[z], k[z + 1]) for z in range(63)] + [None]
    d = [cot[8 * z : 8 * z + 8] for z in range(64)]
    g, q, levels, _, _ = reduce_chain(c, s, d, False)
    u = expand_chain(q * recip(g), levels, None, None)
    for z in range(64):
        tr[8 * z : 8 * z + 8] = cap[z] * u[z]

    def turned(rows, dst, q):
        block = jnp.transpose(rows)
        for h in range(2):
            dst[pl.ds(4 * h + q, 64, stride=8), :] = block[64 * h : 64 * h + 64]

    subf = sub_v.astype(F32)
    upper = (lax.broadcasted_iota(jnp.int32, (128, 128), 0) & 1) == 1
    for q in range(4):
        turned(cond[pl.ds(q, 128, stride=4), :], mid.at[0], q)
        turned(tr[pl.ds(q, 128, stride=4), :], mid.at[1], q)
        turned(jnp.where(upper, subf[q + 4 : q + 5], subf[q : q + 1]), mid.at[2], q)
    z_lane = (lax.broadcasted_iota(jnp.int32, (8, 128), 1) >> 1).astype(F32)
    row = lax.broadcasted_iota(jnp.int32, (8, 128), 0)
    ky, sy, dy = [], [], []
    for y in range(64):
        ky.append(mid[0, 8 * y : 8 * y + 8])
        dy.append(mid[1, 8 * y : 8 * y + 8])
        sy.append(jnp.where(z_lane < mid[2, 8 * y : 8 * y + 8], 1.0, 0.6))
    cap_first, cap_last = sy[0][0:4], sy[63][4:8]
    low = jnp.where(me_y == 0, R * SIDE, 0.0)
    high = jnp.where(me_y == 7, R * SIDE, 0.0)
    sy[0] = sy[0] + jnp.where(row < 4, low, 0.0)
    sy[63] = sy[63] + jnp.where(row >= 4, high, 0.0)
    cy = [R * jnp.minimum(ky[y], ky[y + 1]) for y in range(63)] + [None]
    g, q, levels, (p, zz, t), ties = reduce_chain(cy, sy, dy, True)
    put_levels(fac, levels)
    for lev in range(NLEV):
        tie_out[lev] = ties[lev]
    kf, kl = ky[0], ky[63]
    side_a = tuple(v[0:4] for v in (kf, kl, zz, t, g, p, q))
    side_b = tuple(v[4:8] for v in (kf, kl, zz, t, g, p, q))
    merged, saved = merge_ports(side_a, side_b)
    for i, v in enumerate(saved):
        tie_out[NLEV + i, 0:4] = v
    pack = jnp.concatenate(list(merged) + [cap_first, cap_last, jnp.zeros((4, 128), F32)], axis=0)
    for n in range(8):
        ypack[n] = pack


def second_kernel(gat, fac, ties, cond, sub, keep, send, xfac, xhfac, a2_out, kh_out, pick, flat, planes, xp):
    me_y = lax.axis_index("gy")
    seg = [[gat[n, 4 * i : 4 * i + 4] for i in range(9)] for n in range(8)]
    gam, rhs = seg[0][4], seg[0][6]
    down, links = [None], [None]
    for n in range(1, 8):
        kf, kl, z, t, g, p, q = seg[n][:7]
        link = R * jnp.minimum(seg[n - 1][1], kf)
        lk = link * recip(1.0 + link * z)
        inv = recip(gam + lk)
        h = inv * (rhs + lk * p)
        lt = lk * t
        down.append((h, lt * inv))
        links.append(lk)
        rhs = q + lt * (h - p)
        gam = g + lt * t * (gam * inv)
    u = [None] * 8
    u[7] = rhs * recip(gam)
    for n in range(7, 0, -1):
        u[n - 1] = down[n][0] + down[n][1] * u[n]
    zero4 = jnp.zeros((4, 128), F32)
    fl, uf = [zero4], [None]
    for n in range(1, 8):
        kf, kl, z, t, g, p, q = seg[n][:7]
        fl.append(links[n] * (u[n - 1] - p - t * u[n]))
        uf.append(p + z * fl[n] + t * u[n])
    for n in range(8):
        rows = [fl[n], u[n]]
        if n:
            rows += [seg[n - 1][8] * u[n - 1], seg[n - 1][1], seg[n - 1][8]]
        else:
            rows += [zero4, zero4, zero4 + 1.0]
        if n < 7:
            rows += [seg[n + 1][7] * uf[n + 1], seg[n + 1][0], seg[n + 1][7]]
        else:
            rows += [zero4, zero4, zero4 + 1.0]
        for i, v in enumerate(rows):
            pick[n, 4 * i : 4 * i + 4] = v
    mine = [pick[me_y, 4 * i : 4 * i + 4] for i in range(8)]
    flux, u_b = mine[0], mine[1]
    saved = tuple(ties[NLEV + i, 0:4] for i in range(6))
    u_a, flux_b = descend(saved, flux, u_b)
    flux8 = jnp.concatenate([flux, flux_b], axis=0)
    last8 = jnp.concatenate([u_a, u_b], axis=0)
    levels = get_levels(lambda kind, i: fac[kind, i], 32)
    u_nodes = expand_chain(last8, levels, [ties[i] for i in range(NLEV)], flux8)
    for y in range(64):
        flat[8 * y : 8 * y + 8] = u_nodes[y]
    subf = sub[...]
    for q in range(4):
        planes[pl.ds(q, 128, stride=4), :] = jnp.transpose(
            jnp.concatenate([flat[pl.ds(q, 64, stride=8), :], flat[pl.ds(4 + q, 64, stride=8), :]], axis=0)
        )

    even = (lax.broadcasted_iota(jnp.int32, (4, 128), 1) & 1) == 0

    def both(left, right):
        low = jnp.where(even, left, pltpu.roll(right, 127, 1))
        high = jnp.where(even, pltpu.roll(left, 127, 1), pltpu.roll(right, 126, 1))
        return [low[x : x + 1] for x in range(4)] + [high[x : x + 1] for x in range(4)]

    dh, kh, caph = both(mine[2], mine[5]), both(mine[3], mine[6]), both(mine[4], mine[7])
    for x in range(8):
        kh_out[x : x + 1] = kh[x]

    low, high = wall_terms()

    def x_chain(k, cap, d):
        s = list(cap)
        s[0] = s[0] + low
        s[7] = s[7] + high
        c = [R * jnp.minimum(k[x], k[x + 1]) for x in range(7)] + [None]
        g, q, levels, (p, z, t), tie = reduce_chain(c, s, d, True)
        return levels, tie, (k[0], k[7], z, t, g, p, q)

    base_z = lax.broadcasted_iota(jnp.int32, (8, 128), 0)
    for chunk in range(8):
        zi = base_z + 8 * chunk
        k, cap, d = [], [], []
        for x in range(8):
            k.append(cond[pl.ds(64 * chunk + x, 8, stride=8), :])
            cap.append(jnp.where(zi < subf[x : x + 1], 1.0, 0.6))
            dx = cap[x] * planes[pl.ds(64 * chunk + x, 8, stride=8), :]
            a2_out[pl.ds(64 * chunk + x, 8, stride=8), :] = dx
            d.append(dx)
        levels, tie, port = x_chain(k, cap, d)
        store_x(xfac.at[chunk], levels, tie)
        for i in range(2):
            xp[i, 8 * chunk : 8 * chunk + 8] = port[5 + i]
    levels, tie, port = x_chain(kh, caph, dh)
    store_x(xhfac, levels, tie)
    split_halves(xp, keep, send)
    for i in range(7):
        keep[64 + i : 65 + i] = port[i]
        send[64 + i : 65 + i] = port[i]


def store_x(ref, levels, tie):
    for lev, triple in enumerate(levels):
        base, n = node_order(4, lev)
        for kind in range(3):
            for j in range(n):
                if triple[kind][j] is not None:
                    ref[7 * kind + base + j] = triple[kind][j]
    for lev in range(3):
        ref[21 + lev] = tie[lev]


def load_x(ref):
    levels = get_levels(lambda kind, i: ref[7 * kind + i], 4)
    return levels, [ref[21 + lev] for lev in range(3)]


def read_pack(ref, n):
    main = tuple(ref[32 * i : 32 * i + 32] for i in range(n))
    edge = tuple(ref[32 * n + i : 32 * n + i + 1] for i in range(n))
    return main, edge


def write_pack(ref, main, edge):
    n = len(main)
    for i in range(n):
        ref[32 * i : 32 * i + 32] = main[i]
        ref[32 * n + i : 32 * n + i + 1] = edge[i]


def order(right, mine, theirs):
    a = tuple(jnp.where(right, t, m) for m, t in zip(mine, theirs))
    b = tuple(jnp.where(right, m, t) for m, t in zip(mine, theirs))
    return a, b


def planes_of(ref, n):
    return tuple(ref[32 * i : 32 * i + 32] for i in range(n))


def put_planes(ref, values):
    for i, v in enumerate(values):
        ref[32 * i : 32 * i + 32] = v


def spots():
    me_x = lax.axis_index("gx")
    return [lax.rem(lax.div(me_x, bit), 2) == 1 for bit in (1, 2, 4)]


def core_matrix_kernel(mine, theirs, merged_out, coef_out):
    odd, _, _ = spots()
    merged, coefs = port_coefs(*order(odd, planes_of(mine, 5), planes_of(theirs, 5)))
    put_planes(merged_out, merged)
    put_planes(coef_out, coefs)


def ring_matrix_kernel(own, near, far, mid, merged_out, mine_out, other_out, ring_out):
    _, right, upper = spots()
    packs = [planes_of(r, 5) for r in (own, near, mid, far)]
    mine, mine_c = port_coefs(*order(right, packs[0], packs[1]))
    other, other_c = port_coefs(*order(right, packs[2], packs[3]))
    merged, ring_c = port_coefs(*order(upper, mine, other))
    put_planes(merged_out, merged)
    put_planes(mine_out, mine_c)
    put_planes(other_out, other_c)
    put_planes(ring_out, ring_c)


def read_sides(ref):
    main = (ref[0:32], ref[32:64])
    edge = tuple(ref[64 + i : 65 + i] for i in range(7))
    return main, edge


def core_kernel(mine, theirs, coefs, merged_out, saved_out):
    odd, _, _ = spots()
    m, t = read_sides(mine), read_sides(theirs)
    values, saved = port_values(planes_of(coefs, 7), *order(odd, m[0], t[0]))
    edge, edge_saved = merge_ports(*order(odd, m[1], t[1]))
    put_planes(merged_out, values)
    for i in range(7):
        merged_out[64 + i : 65 + i] = edge[i]
    write_pack(saved_out, saved, edge_saved)


def ring_kernel(own, near, far, mid, matrix, mine_c, other_c, ring_c, merged_out, pair_out, saved_out, top_out):
    _, right, upper = spots()
    last = lax.div(lax.axis_index("gx"), 8) == 1
    main, edge = zip(*[read_sides(r) for r in (own, near, mid, far)])
    mine, pair = port_values(planes_of(mine_c, 7), *order(right, main[0], main[1]))
    other, _ = port_values(planes_of(other_c, 7), *order(right, main[2], main[3]))
    values, saved = port_values(planes_of(ring_c, 7), *order(upper, mine, other))
    e_mine, e_pair = merge_ports(*order(right, edge[0], edge[1]))
    e_other, _ = merge_ports(*order(right, edge[2], edge[3]))
    e_merged, e_saved = merge_ports(*order(upper, e_mine, e_other))
    outs = [planes_of(matrix, 5) + values, e_merged]
    tops = []
    for kf, kl, z, tt, g, p, q in outs:
        tg = tt * recip(g)
        tops.append((jnp.where(last, z + tt * tg, g), jnp.where(last, p + tg * q, q), jnp.where(last, kf, kl)))
    write_pack(merged_out, *outs)
    write_pack(pair_out, pair, e_pair)
    write_pack(saved_out, saved, e_saved)
    write_pack(top_out, *tops)


def top_kernel(merged, near, theirs, sv1, sv2, sv3, own, send):
    me_x = lax.axis_index("gx")
    far = lax.div(me_x, 8) == 1
    mm = read_pack(merged, 7)
    n, t = read_pack(near, 3), read_pack(theirs, 3)
    saved = [read_pack(r, 6) for r in (sv1, sv2, sv3)]
    final = []
    for part in range(2):
        (ga, qa, ka), (zb, pb, kb) = order(far, n[part], t[part])
        link = R * jnp.minimum(ka, kb)
        lk = link * recip(1.0 + link * zb)
        u_a = (qa + lk * pb) * recip(ga + lk)
        kf, kl, z, tt, g, p, q = mm[part]
        flux = jnp.where(far, lk * (u_a - pb), 0.0)
        u = jnp.where(far, (q + tt * flux) * recip(g), u_a)
        for bit, lev in ((4, 2), (2, 1)):
            right = lax.rem(lax.div(me_x, bit), 2) == 1
            ua, fb = descend(saved[lev][part], flux, u)
            flux = jnp.where(right, fb, flux)
            u = jnp.where(right, u, ua)
        ua, fb = descend(saved[0][part], flux, u)
        odd = lax.rem(me_x, 2) == 1
        final.append((jnp.where(odd, fb, flux), jnp.where(odd, u, ua), jnp.where(odd, flux, fb), jnp.where(odd, ua, u)))
    write_pack(own, final[0][:2], final[1][:2])
    send[0:32] = final[0][2]
    send[32:64] = final[0][3]


def coef_kernel(cond, kh, a2, cot, sub, dep, cls, k_y, k_l, k_z, k_s, base):
    me_y = lax.axis_index("gy")
    sub_v, dep_v, kh_v = sub[...], dep[...], kh[...]
    top = film_top(cls[...])
    lane = lax.broadcasted_iota(jnp.int32, (8, 128), 1)
    first, final = lane == 0, lane == 127
    film_y = jnp.where(first & (me_y == 0), SIDE, 0.0) + jnp.where(final & (me_y == 7), SIDE, 0.0)
    for z in range(64):
        rows = slice(8 * z, 8 * z + 8)
        k = cond[rows]
        k_h = pltpu.roll(kh_v, 128 - 2 * z, 1) if z else kh_v
        k_y[rows] = (2.0 * R) * jnp.minimum(k, jnp.where(final, k_h, pltpu.roll(k, 127, 1)))
        k_l[rows] = (2.0 * R) * jnp.minimum(k, k_h)
        if z < 63:
            k_z[rows] = (2.0 * R) * jnp.minimum(k, cond[8 * z + 8 : 8 * z + 16])
        film = film_y + top * (dep_v - 1 == z).astype(F32)
        if z == 0:
            film = film + BOTTOM
        k_s[rows] = 2.0 * jnp.where(z < sub_v, 1.0, 0.6) - (2.0 * R) * film
        base[rows] = cot[rows] - 2.0 * a2[rows]


def last_kernel(
    own, got, xfac, xhfac, k_y, k_l, k_z, k_s, base, sub, temp_out, src_out, s1, fu, t_buf, s_buf, sems
):
    core = own_half()
    for i in range(2):
        fu[i, pl.ds(pl.multiple_of(32 * core, 32), 32), :] = own[32 * i : 32 * i + 32]
        fu[i, pl.ds(pl.multiple_of(32 - 32 * core, 32), 32), :] = got[32 * i : 32 * i + 32]
    levels, tie = load_x(xhfac)
    uh = jnp.concatenate(expand_chain(own[65:66], levels, tie, own[64:65]), axis=0)
    sub_v = sub[...]
    lane = lax.broadcasted_iota(jnp.int32, (8, 128), 1)
    first, final = lane == 0, lane == 127
    up, copies = None, []

    def expand(chunk):
        rows = slice(8 * chunk, 8 * chunk + 8)
        levels, tie = load_x(xfac.at[chunk])
        u = expand_chain(fu[1, rows], levels, tie, fu[0, rows])
        for x in range(8):
            s1[pl.ds(64 * chunk + x, 8, stride=8), :] = u[x]

    expand(0)
    for z in range(64):
        if z & 7 == 0 and z < 56:
            expand(z // 8 + 1)
        rows = slice(8 * z, 8 * z + 8)
        s = s1[rows]
        s_h = pltpu.roll(uh, 128 - 2 * z, 1) if z else uh
        f_y = k_y[rows] * (jnp.where(final, s_h, pltpu.roll(s, 127, 1)) - s)
        f_l = k_l[rows] * (s - s_h)
        total = f_y - jnp.where(first, f_l, pltpu.roll(f_y, 1, 1))
        if z < 63:
            f_z = k_z[rows] * (s1[8 * z + 8 : 8 * z + 16] - s)
            total = total + f_z
        if z:
            total = total - up
        up = f_z
        s_buf[rows] = jnp.where(z < sub_v, 1.0, 0.6) * s
        t_buf[rows] = base[rows] + k_s[rows] * s + total
        if z & 7 == 7:
            part = slice(8 * z - 56, 8 * z + 8)
            for i, (buf, out) in enumerate(((s_buf, src_out), (t_buf, temp_out))):
                cp = pltpu.make_async_copy(buf.at[part], out.at[part], sems.at[2 * (z // 8) + i])
                cp.start()
                copies.append(cp)
    for cp in copies:
        cp.wait()


VMEM = pl.BlockSpec(memory_space=pltpu.VMEM)
HBM = pl.BlockSpec(memory_space=pltpu.MemorySpace.HBM)


def call(kernel, outs, scratch, name, *args, far_in=0, far_out=0, sems=0):
    shapes = [s if isinstance(s, jax.ShapeDtypeStruct) else jax.ShapeDtypeStruct(s, F32) for s in outs]
    scr = [pltpu.VMEM(s, F32) for s in scratch]
    args = [pltpu.with_memory_space_constraint(a, pltpu.MemorySpace.HBM) if i < far_in else a for i, a in enumerate(args)]
    if sems:
        scr.append(pltpu.SemaphoreType.DMA((sems,)))
    return pl.pallas_call(
        kernel,
        out_shape=shapes,
        in_specs=[HBM if i < far_in else VMEM for i in range(len(args))],
        out_specs=[HBM if i < far_out else VMEM for i in range(len(outs))],
        scratch_shapes=scr,
        compiler_params=pltpu.CompilerParams(vmem_limit_bytes=40 * 1024 * 1024),
        name=name,
    )(*args)


def swap(v, bit):
    return lax.ppermute(v, "gx", [(i, i ^ bit) for i in range(16)])


def body(cotangent, saved_temp, substrate_top, deposit_top, top_class):
    cot = cotangent.reshape(512, 128)
    temp = saved_temp.reshape(512, 128)
    small = jax.ShapeDtypeStruct((8, 128), jnp.int32)
    cond, keep_m, send_m, cot, sub, dep, cls = call(
        fields_kernel,
        [(512, 128), (160, 128), (160, 128), (512, 128), small, small, small],
        [(512, 128), (5, 64, 128)],
        "fields",
        cot, temp, substrate_top, deposit_top, top_class,
        far_in=5, sems=5,
    )
    other_m = swap(send_m, 1)
    ypack, fac, ties = call(
        first_kernel,
        [(8, 40, 128), (3, 63, 8, 128), (12, 8, 128)],
        [(3, 512, 128), (512, 128)],
        "first",
        cot, sub, dep, cls, cond,
    )
    mm, core_c = call(core_matrix_kernel, [(160, 128), (224, 128)], [], "matrix_core", keep_m, other_m)
    mm, ypack = lax.optimization_barrier((mm, ypack))
    gat = lax.all_to_all(ypack, "gy", split_axis=0, concat_axis=0, tiled=True)
    ring_m = [swap(mm, bit) for bit in (3, 7, 4)]
    keep, send, xfac, xhfac, a2, kh = call(
        second_kernel,
        [(72, 128), (72, 128), (8, 24, 8, 128), (24, 1, 128), (512, 128), (8, 128)],
        [(8, 32, 128), (512, 128), (512, 128), (2, 64, 128)],
        "second",
        gat, fac, ties, cond, sub,
    )
    m1, sv1 = call(core_kernel, [(72, 128), (200, 128)], [], "merge_core", keep, swap(send, 1), core_c)
    ring_v = [swap(m1, bit) for bit in (3, 7, 4)]
    matrix, mine_c, other_c, ring_c = call(
        ring_matrix_kernel, [(160, 128)] + [(224, 128)] * 3, [], "matrix_ring", mm, *ring_m
    )
    m3, sv2, sv3, near = call(
        ring_kernel,
        [(232, 128), (200, 128), (200, 128), (104, 128)],
        [],
        "merge_ring",
        m1, *ring_v, matrix, mine_c, other_c, ring_c,
    )
    sv3, kh = lax.optimization_barrier((sv3, kh))
    coefs = call(coef_kernel, [(512, 128)] * 5, [], "coef", cond, kh, a2, cot, sub, dep, cls)
    opposite = swap(near, 9)
    sv3, coefs = lax.optimization_barrier((sv3, coefs))
    own, out = call(top_kernel, [(72, 128), (64, 128)], [], "top", m3, near, opposite, sv1, sv2, sv3)
    got = swap(out, 1)
    grad_temp, grad_source = call(
        last_kernel,
        [(512, 128), (512, 128)],
        [(512, 128), (2, 64, 128), (512, 128), (512, 128)],
        "last",
        own, got, xfac, xhfac, *coefs, sub,
        far_out=2, sems=16,
    )
    return grad_temp.reshape(cotangent.shape), grad_source.reshape(cotangent.shape)


def solution(mesh):
    in_specs = (
        P(None, "gx", "gy"),
        P(None, "gx", "gy"),
        P("gx", "gy"),
        P("gx", "gy"),
        P("gx", "gy"),
    )
    out_specs = (P(None, "gx", "gy"), P(None, "gx", "gy"))
    return jax.shard_map(body, mesh=mesh, in_specs=in_specs, out_specs=out_specs, check_vma=False)
```

```python
import jax
import jax.numpy as jnp
from jax import lax
from jax.experimental import pallas as pl
from jax.experimental.pallas import tpu as pltpu
from jax.sharding import PartitionSpec as P

R = 1000.0
SIDE = 0.3
BOTTOM = 0.5
TOPS = (0.05, 0.25, 0.8, 2.0)
F32 = jnp.float32
NLEV = 6


def recip(v):
    return 1.0 / v


def reduce_chain(c, s, d, track):
    levels, port, ties = [], None, []
    while len(s) > 1:
        half = len(s) // 2
        ml, mr, dv = [], [], []
        for j in range(half):
            i = 2 * j
            total = s[i] + c[i]
            if j:
                total = total + c[i - 1]
            inv = recip(total)
            mr.append(c[i] * inv)
            ml.append(c[i - 1] * inv if j else None)
            dv.append(d[i] * inv)
            if track and j == 0:
                if port is None:
                    port = [dv[0], inv, mr[0]]
                    ties.append(inv)
                else:
                    p, z, t = port
                    tie = t * inv
                    ties.append(tie)
                    port = [p + t * dv[0], z + t * tie, t * mr[0]]
        ns, nd, nc = [], [], []
        for j in range(half):
            e, o = 2 * j, 2 * j + 1
            sv = s[o] + mr[j] * s[e]
            dn = d[o] + mr[j] * d[e]
            if j + 1 < half:
                sv = sv + ml[j + 1] * s[e + 2]
                dn = dn + ml[j + 1] * d[e + 2]
                nc.append(ml[j + 1] * c[e + 2])
            ns.append(sv)
            nd.append(dn)
        levels.append((dv, ml, mr))
        c, s, d = nc, ns, nd
    return s[0], d[0], levels, port, ties


def expand_chain(u_last, levels, ties, flux):
    u = [u_last]
    for lev in range(len(levels) - 1, -1, -1):
        dv, ml, mr = levels[lev]
        out = []
        for j in range(len(u)):
            even = dv[j] + mr[j] * u[j]
            if j:
                even = even + ml[j] * u[j - 1]
            elif ties is not None:
                even = even + ties[lev] * flux
            out += [even, u[j]]
        u = out
    return u


def merge_ports(a, b):
    kfa, kla, za, ta, ga, pa, qa = a
    kfb, klb, zb, tb, gb, pb, qb = b
    link = R * jnp.minimum(kla, kfb)
    lk = link * recip(1.0 + link * zb)
    inv = recip(ga + lk)
    h = inv * (qa + lk * pb)
    ti = ta * inv
    lt = lk * tb
    w = lt * inv
    merged = (
        kfa,
        klb,
        za + ta * ti,
        ta * w,
        gb + lt * tb * (ga * inv),
        pa + ta * h,
        qb + lt * (h - pb),
    )
    return merged, (h, ti, w, lk, pb, tb)


def descend(saved, flux, u_b):
    h, ti, w, lk, pb, tb = saved
    u_a = h + ti * flux + w * u_b
    flux_b = lk * (u_a - pb - tb * u_b)
    return u_a, flux_b


def film_top(cls):
    total = jnp.zeros(cls.shape, F32)
    for n in range(4):
        total = total + TOPS[n] * (cls == n).astype(F32)
    return total


def node_order(half, lev):
    base, n = 0, half
    for _ in range(lev):
        base += n
        n //= 2
    return base, n


def put_levels(ref, levels):
    half = len(levels[0][0])
    for lev, triple in enumerate(levels):
        base, n = node_order(half, lev)
        for kind in range(3):
            for j in range(n):
                if triple[kind][j] is not None:
                    ref[kind, base + j] = triple[kind][j]


def get_levels(read, half):
    levels, lev = [], 0
    while half >> lev:
        base, n = node_order(half, lev)
        levels.append(
            tuple([None if kind == 1 and j == 0 else read(kind, base + j) for j in range(n)] for kind in range(3))
        )
        lev += 1
    return levels


def first_kernel(
    cot_in, temp_in, sub_in, dep_in, cls_in, ypack, cond, fac, tie_out, cot, sub, dep, cls, temp, mid, tr, sems
):
    me_y = lax.axis_index("gy")
    pairs = ((sub_in, sub), (dep_in, dep), (temp_in, temp), (cls_in, cls), (cot_in, cot))
    copies = [pltpu.make_async_copy(a, b, sems.at[i]) for i, (a, b) in enumerate(pairs)]
    for cp in copies:
        cp.start()
    for cp in copies[:4]:
        cp.wait()
    sub_v, dep_v = sub[...], dep[...]
    top = film_top(cls[...])
    k, cap, s = [], [], []
    for z in range(64):
        under = z < sub_v
        sg = 0.5 + jax.nn.sigmoid(temp[8 * z : 8 * z + 8])
        kz = jnp.where(z < dep_v, jnp.where(under, 1.0, 0.45) * sg, 0.0)
        cond[8 * z : 8 * z + 8] = kz
        k.append(kz)
        cap.append(jnp.where(under, 1.0, 0.6))
        film = top * (dep_v - 1 == z).astype(F32)
        if z == 0:
            film = film + BOTTOM
        s.append(cap[z] + R * film)
    c = [R * jnp.minimum(k[z], k[z + 1]) for z in range(63)] + [None]
    copies[4].wait()
    d = [cot[8 * z : 8 * z + 8] for z in range(64)]
    g, q, levels, _, _ = reduce_chain(c, s, d, False)
    u = expand_chain(q * recip(g), levels, None, None)
    for z in range(64):
        tr[8 * z : 8 * z + 8] = cap[z] * u[z]

    def turned(rows, dst, q):
        block = jnp.transpose(rows)
        for h in range(2):
            dst[pl.ds(4 * h + q, 64, stride=8), :] = block[64 * h : 64 * h + 64]

    subf = sub_v.astype(F32)
    upper = (lax.broadcasted_iota(jnp.int32, (128, 128), 0) & 1) == 1
    for q in range(4):
        turned(cond[pl.ds(q, 128, stride=4), :], mid.at[0], q)
        turned(tr[pl.ds(q, 128, stride=4), :], mid.at[1], q)
        turned(jnp.where(upper, subf[q + 4 : q + 5], subf[q : q + 1]), mid.at[2], q)
    z_lane = (lax.broadcasted_iota(jnp.int32, (8, 128), 1) >> 1).astype(F32)
    row = lax.broadcasted_iota(jnp.int32, (8, 128), 0)
    ky, sy, dy = [], [], []
    for y in range(64):
        ky.append(mid[0, 8 * y : 8 * y + 8])
        dy.append(mid[1, 8 * y : 8 * y + 8])
        sy.append(jnp.where(z_lane < mid[2, 8 * y : 8 * y + 8], 1.0, 0.6))
    cap_first, cap_last = sy[0][0:4], sy[63][4:8]
    low = jnp.where(me_y == 0, R * SIDE, 0.0)
    high = jnp.where(me_y == 7, R * SIDE, 0.0)
    sy[0] = sy[0] + jnp.where(row < 4, low, 0.0)
    sy[63] = sy[63] + jnp.where(row >= 4, high, 0.0)
    cy = [R * jnp.minimum(ky[y], ky[y + 1]) for y in range(63)] + [None]
    g, q, levels, (p, zz, t), ties = reduce_chain(cy, sy, dy, True)
    put_levels(fac, levels)
    for lev in range(NLEV):
        tie_out[lev] = ties[lev]
    kf, kl = ky[0], ky[63]
    side_a = tuple(v[0:4] for v in (kf, kl, zz, t, g, p, q))
    side_b = tuple(v[4:8] for v in (kf, kl, zz, t, g, p, q))
    merged, saved = merge_ports(side_a, side_b)
    for i, v in enumerate(saved):
        tie_out[NLEV + i, 0:4] = v
    pack = jnp.concatenate(list(merged) + [cap_first, cap_last, jnp.zeros((4, 128), F32)], axis=0)
    for n in range(8):
        ypack[n] = pack


def own_half():
    me_x = lax.axis_index("gx")
    return lax.rem(me_x + lax.div(me_x, 2) + lax.div(me_x, 8), 2)


def second_kernel(gat, fac, ties, cond, sub, keep, send, xfac, xhfac, a2_out, kh_out, pick, flat, planes, xp):
    me_y = lax.axis_index("gy")
    me_x = lax.axis_index("gx")
    seg = [[gat[n, 4 * i : 4 * i + 4] for i in range(9)] for n in range(8)]
    gam, rhs = seg[0][4], seg[0][6]
    down, links = [None], [None]
    for n in range(1, 8):
        kf, kl, z, t, g, p, q = seg[n][:7]
        link = R * jnp.minimum(seg[n - 1][1], kf)
        lk = link * recip(1.0 + link * z)
        inv = recip(gam + lk)
        h = inv * (rhs + lk * p)
        lt = lk * t
        down.append((h, lt * inv))
        links.append(lk)
        rhs = q + lt * (h - p)
        gam = g + lt * t * (gam * inv)
    u = [None] * 8
    u[7] = rhs * recip(gam)
    for n in range(7, 0, -1):
        u[n - 1] = down[n][0] + down[n][1] * u[n]
    zero4 = jnp.zeros((4, 128), F32)
    fl, uf = [zero4], [None]
    for n in range(1, 8):
        kf, kl, z, t, g, p, q = seg[n][:7]
        fl.append(links[n] * (u[n - 1] - p - t * u[n]))
        uf.append(p + z * fl[n] + t * u[n])
    for n in range(8):
        rows = [fl[n], u[n]]
        if n:
            rows += [seg[n - 1][8] * u[n - 1], seg[n - 1][1], seg[n - 1][8]]
        else:
            rows += [zero4, zero4, zero4 + 1.0]
        if n < 7:
            rows += [seg[n + 1][7] * uf[n + 1], seg[n + 1][0], seg[n + 1][7]]
        else:
            rows += [zero4, zero4, zero4 + 1.0]
        for i, v in enumerate(rows):
            pick[n, 4 * i : 4 * i + 4] = v
    mine = [pick[me_y, 4 * i : 4 * i + 4] for i in range(8)]
    flux, u_b = mine[0], mine[1]
    saved = tuple(ties[NLEV + i, 0:4] for i in range(6))
    u_a, flux_b = descend(saved, flux, u_b)
    flux8 = jnp.concatenate([flux, flux_b], axis=0)
    last8 = jnp.concatenate([u_a, u_b], axis=0)
    levels = get_levels(lambda kind, i: fac[kind, i], 32)
    u_nodes = expand_chain(last8, levels, [ties[i] for i in range(NLEV)], flux8)
    for y in range(64):
        flat[8 * y : 8 * y + 8] = u_nodes[y]
    subf = sub[...]
    for q in range(4):
        planes[pl.ds(q, 128, stride=4), :] = jnp.transpose(
            jnp.concatenate([flat[pl.ds(q, 64, stride=8), :], flat[pl.ds(4 + q, 64, stride=8), :]], axis=0)
        )

    even = (lax.broadcasted_iota(jnp.int32, (4, 128), 1) & 1) == 0

    def both(left, right):
        low = jnp.where(even, left, pltpu.roll(right, 127, 1))
        high = jnp.where(even, pltpu.roll(left, 127, 1), pltpu.roll(right, 126, 1))
        return [low[x : x + 1] for x in range(4)] + [high[x : x + 1] for x in range(4)]

    dh, kh, caph = both(mine[2], mine[5]), both(mine[3], mine[6]), both(mine[4], mine[7])
    for x in range(8):
        kh_out[x : x + 1] = kh[x]

    low = jnp.where(me_x == 0, R * SIDE, 0.0)
    high = jnp.where(me_x == 15, R * SIDE, 0.0)

    def x_chain(k, cap, d):
        s = list(cap)
        s[0] = s[0] + low
        s[7] = s[7] + high
        c = [R * jnp.minimum(k[x], k[x + 1]) for x in range(7)] + [None]
        g, q, levels, (p, z, t), tie = reduce_chain(c, s, d, True)
        return levels, tie, (k[0], k[7], z, t, g, p, q)

    base_z = lax.broadcasted_iota(jnp.int32, (8, 128), 0)
    for chunk in range(8):
        zi = base_z + 8 * chunk
        k, cap, d = [], [], []
        for x in range(8):
            k.append(cond[pl.ds(64 * chunk + x, 8, stride=8), :])
            cap.append(jnp.where(zi < subf[x : x + 1], 1.0, 0.6))
            dx = cap[x] * planes[pl.ds(64 * chunk + x, 8, stride=8), :]
            a2_out[pl.ds(64 * chunk + x, 8, stride=8), :] = dx
            d.append(dx)
        levels, tie, port = x_chain(k, cap, d)
        store_x(xfac.at[chunk], levels, tie)
        for i in range(7):
            xp[i, 8 * chunk : 8 * chunk + 8] = port[i]
    levels, tie, port = x_chain(kh, caph, dh)
    store_x(xhfac, levels, tie)
    core = own_half()
    for i in range(7):
        keep[32 * i : 32 * i + 32] = xp[i, pl.ds(pl.multiple_of(32 * core, 32), 32), :]
        send[32 * i : 32 * i + 32] = xp[i, pl.ds(pl.multiple_of(32 - 32 * core, 32), 32), :]
        keep[224 + i : 225 + i] = port[i]
        send[224 + i : 225 + i] = port[i]


def store_x(ref, levels, tie):
    for lev, triple in enumerate(levels):
        base, n = node_order(4, lev)
        for kind in range(3):
            for j in range(n):
                if triple[kind][j] is not None:
                    ref[7 * kind + base + j] = triple[kind][j]
    for lev in range(3):
        ref[21 + lev] = tie[lev]


def load_x(ref):
    levels = get_levels(lambda kind, i: ref[7 * kind + i], 4)
    return levels, [ref[21 + lev] for lev in range(3)]


def read_pack(ref, n):
    main = tuple(ref[32 * i : 32 * i + 32] for i in range(n))
    edge = tuple(ref[32 * n + i : 32 * n + i + 1] for i in range(n))
    return main, edge


def write_pack(ref, main, edge):
    n = len(main)
    for i in range(n):
        ref[32 * i : 32 * i + 32] = main[i]
        ref[32 * n + i : 32 * n + i + 1] = edge[i]


def order(right, mine, theirs):
    a = tuple(jnp.where(right, t, m) for m, t in zip(mine, theirs))
    b = tuple(jnp.where(right, m, t) for m, t in zip(mine, theirs))
    return a, b


def core_kernel(mine, theirs, merged_out, saved_out):
    right = lax.rem(lax.axis_index("gx"), 2) == 1
    m, t = read_pack(mine, 7), read_pack(theirs, 7)
    done = [merge_ports(*order(right, m[part], t[part])) for part in range(2)]
    write_pack(merged_out, done[0][0], done[1][0])
    write_pack(saved_out, done[0][1], done[1][1])


def ring_kernel(own, near, far, mid, merged_out, pair_out, saved_out, top_out):
    me_x = lax.axis_index("gx")
    right = lax.rem(lax.div(me_x, 2), 2) == 1
    upper = lax.rem(lax.div(me_x, 4), 2) == 1
    last = lax.div(me_x, 8) == 1
    packs = [read_pack(r, 7) for r in (own, near, mid, far)]
    pairs, saves, outs, tops = [], [], [], []
    for part in range(2):
        mine, keep = merge_ports(*order(right, packs[0][part], packs[1][part]))
        other, _ = merge_ports(*order(right, packs[2][part], packs[3][part]))
        merged, saved = merge_ports(*order(upper, mine, other))
        pairs.append(keep)
        saves.append(saved)
        outs.append(merged)
        kf, kl, z, tt, g, p, q = merged
        tg = tt * recip(g)
        tops.append((jnp.where(last, z + tt * tg, g), jnp.where(last, p + tg * q, q), jnp.where(last, kf, kl)))
    write_pack(merged_out, *outs)
    write_pack(pair_out, *pairs)
    write_pack(saved_out, *saves)
    write_pack(top_out, *tops)


def top_kernel(merged, near, theirs, sv1, sv2, sv3, own, send):
    me_x = lax.axis_index("gx")
    far = lax.div(me_x, 8) == 1
    mm = read_pack(merged, 7)
    n, t = read_pack(near, 3), read_pack(theirs, 3)
    saved = [read_pack(r, 6) for r in (sv1, sv2, sv3)]
    final = []
    for part in range(2):
        (ga, qa, ka), (zb, pb, kb) = order(far, n[part], t[part])
        link = R * jnp.minimum(ka, kb)
        lk = link * recip(1.0 + link * zb)
        u_a = (qa + lk * pb) * recip(ga + lk)
        kf, kl, z, tt, g, p, q = mm[part]
        flux = jnp.where(far, lk * (u_a - pb), 0.0)
        u = jnp.where(far, (q + tt * flux) * recip(g), u_a)
        for bit, lev in ((4, 2), (2, 1)):
            right = lax.rem(lax.div(me_x, bit), 2) == 1
            ua, fb = descend(saved[lev][part], flux, u)
            flux = jnp.where(right, fb, flux)
            u = jnp.where(right, u, ua)
        ua, fb = descend(saved[0][part], flux, u)
        odd = lax.rem(me_x, 2) == 1
        final.append((jnp.where(odd, fb, flux), jnp.where(odd, u, ua), jnp.where(odd, flux, fb), jnp.where(odd, ua, u)))
    write_pack(own, final[0][:2], final[1][:2])
    send[0:32] = final[0][2]
    send[32:64] = final[0][3]


def coef_kernel(cond, kh, a2, cot, sub, dep, cls, k_y, k_l, k_z, k_s, base):
    me_y = lax.axis_index("gy")
    sub_v, dep_v, kh_v = sub[...], dep[...], kh[...]
    top = film_top(cls[...])
    lane = lax.broadcasted_iota(jnp.int32, (8, 128), 1)
    first, final = lane == 0, lane == 127
    film_y = jnp.where(first & (me_y == 0), SIDE, 0.0) + jnp.where(final & (me_y == 7), SIDE, 0.0)
    for z in range(64):
        rows = slice(8 * z, 8 * z + 8)
        k = cond[rows]
        k_h = pltpu.roll(kh_v, 128 - 2 * z, 1) if z else kh_v
        k_y[rows] = (2.0 * R) * jnp.minimum(k, jnp.where(final, k_h, pltpu.roll(k, 127, 1)))
        k_l[rows] = (2.0 * R) * jnp.minimum(k, k_h)
        if z < 63:
            k_z[rows] = (2.0 * R) * jnp.minimum(k, cond[8 * z + 8 : 8 * z + 16])
        film = film_y + top * (dep_v - 1 == z).astype(F32)
        if z == 0:
            film = film + BOTTOM
        k_s[rows] = 2.0 * jnp.where(z < sub_v, 1.0, 0.6) - (2.0 * R) * film
        base[rows] = cot[rows] - 2.0 * a2[rows]


def last_kernel(
    own, got, xfac, xhfac, k_y, k_l, k_z, k_s, base, sub, temp_out, src_out, s1, fu, t_buf, s_buf, sems
):
    core = own_half()
    for i in range(2):
        fu[i, pl.ds(pl.multiple_of(32 * core, 32), 32), :] = own[32 * i : 32 * i + 32]
        fu[i, pl.ds(pl.multiple_of(32 - 32 * core, 32), 32), :] = got[32 * i : 32 * i + 32]
    levels, tie = load_x(xhfac)
    uh = jnp.concatenate(expand_chain(own[65:66], levels, tie, own[64:65]), axis=0)
    sub_v = sub[...]
    lane = lax.broadcasted_iota(jnp.int32, (8, 128), 1)
    first, final = lane == 0, lane == 127
    up, copies = None, []

    def expand(chunk):
        rows = slice(8 * chunk, 8 * chunk + 8)
        levels, tie = load_x(xfac.at[chunk])
        u = expand_chain(fu[1, rows], levels, tie, fu[0, rows])
        for x in range(8):
            s1[pl.ds(64 * chunk + x, 8, stride=8), :] = u[x]

    expand(0)
    for z in range(64):
        if z & 7 == 0 and z < 56:
            expand(z // 8 + 1)
        rows = slice(8 * z, 8 * z + 8)
        s = s1[rows]
        s_h = pltpu.roll(uh, 128 - 2 * z, 1) if z else uh
        f_y = k_y[rows] * (jnp.where(final, s_h, pltpu.roll(s, 127, 1)) - s)
        f_l = k_l[rows] * (s - s_h)
        total = f_y - jnp.where(first, f_l, pltpu.roll(f_y, 1, 1))
        if z < 63:
            f_z = k_z[rows] * (s1[8 * z + 8 : 8 * z + 16] - s)
            total = total + f_z
        if z:
            total = total - up
        up = f_z
        s_buf[rows] = jnp.where(z < sub_v, 1.0, 0.6) * s
        t_buf[rows] = base[rows] + k_s[rows] * s + total
        if z & 7 == 7:
            part = slice(8 * z - 56, 8 * z + 8)
            for i, (buf, out) in enumerate(((s_buf, src_out), (t_buf, temp_out))):
                cp = pltpu.make_async_copy(buf.at[part], out.at[part], sems.at[2 * (z // 8) + i])
                cp.start()
                copies.append(cp)
    for cp in copies:
        cp.wait()


VMEM = pl.BlockSpec(memory_space=pltpu.VMEM)
HBM = pl.BlockSpec(memory_space=pltpu.MemorySpace.HBM)


def call(kernel, outs, scratch, name, *args, far_in=0, far_out=0, sems=0):
    shapes = [s if isinstance(s, jax.ShapeDtypeStruct) else jax.ShapeDtypeStruct(s, F32) for s in outs]
    scr = [pltpu.VMEM(s, F32) for s in scratch]
    args = [pltpu.with_memory_space_constraint(a, pltpu.MemorySpace.HBM) if i < far_in else a for i, a in enumerate(args)]
    if sems:
        scr.append(pltpu.SemaphoreType.DMA((sems,)))
    return pl.pallas_call(
        kernel,
        out_shape=shapes,
        in_specs=[HBM if i < far_in else VMEM for i in range(len(args))],
        out_specs=[HBM if i < far_out else VMEM for i in range(len(outs))],
        scratch_shapes=scr,
        compiler_params=pltpu.CompilerParams(vmem_limit_bytes=40 * 1024 * 1024),
        name=name,
    )(*args)


def swap(v, bit):
    return lax.ppermute(v, "gx", [(i, i ^ bit) for i in range(16)])


def body(cotangent, saved_temp, substrate_top, deposit_top, top_class):
    cot = cotangent.reshape(512, 128)
    temp = saved_temp.reshape(512, 128)
    small = jax.ShapeDtypeStruct((8, 128), jnp.int32)
    ypack, cond, fac, ties, cot, sub, dep, cls = call(
        first_kernel,
        [(8, 40, 128), (512, 128), (3, 63, 8, 128), (12, 8, 128), (512, 128), small, small, small],
        [(512, 128), (3, 512, 128), (512, 128)],
        "first",
        cot, temp, substrate_top, deposit_top, top_class,
        far_in=5, sems=5,
    )
    gat = lax.all_to_all(ypack, "gy", split_axis=0, concat_axis=0, tiled=True)
    keep, send, xfac, xhfac, a2, kh = call(
        second_kernel,
        [(232, 128), (232, 128), (8, 24, 8, 128), (24, 1, 128), (512, 128), (8, 128)],
        [(8, 32, 128), (512, 128), (512, 128), (7, 64, 128)],
        "second",
        gat, fac, ties, cond, sub,
    )
    m1, sv1 = call(core_kernel, [(232, 128), (200, 128)], [], "merge_core", keep, swap(send, 1))
    near_z = swap(m1, 3)
    far = swap(m1, 7)
    mid = swap(m1, 4)
    m3, sv2, sv3, near = call(
        ring_kernel,
        [(232, 128), (200, 128), (200, 128), (104, 128)],
        [],
        "merge_ring",
        m1, near_z, far, mid,
    )
    sv3, kh = lax.optimization_barrier((sv3, kh))
    coefs = call(coef_kernel, [(512, 128)] * 5, [], "coef", cond, kh, a2, cot, sub, dep, cls)
    opposite = swap(near, 9)
    sv3, coefs = lax.optimization_barrier((sv3, coefs))
    own, out = call(top_kernel, [(72, 128), (64, 128)], [], "top", m3, near, opposite, sv1, sv2, sv3)
    got = swap(out, 1)
    grad_temp, grad_source = call(
        last_kernel,
        [(512, 128), (512, 128)],
        [(512, 128), (2, 64, 128), (512, 128), (512, 128)],
        "last",
        own, got, xfac, xhfac, *coefs, sub,
        far_out=2, sems=16,
    )
    return grad_temp.reshape(cotangent.shape), grad_source.reshape(cotangent.shape)


def solution(mesh):
    in_specs = (
        P(None, "gx", "gy"),
        P(None, "gx", "gy"),
        P("gx", "gy"),
        P("gx", "gy"),
        P("gx", "gy"),
    )
    out_specs = (P(None, "gx", "gy"), P(None, "gx", "gy"))
    return jax.shard_map(body, mesh=mesh, in_specs=in_specs, out_specs=out_specs, check_vma=False)
```

```python
import jax
import jax.numpy as jnp
from jax import lax
from jax.experimental import pallas as pl
from jax.experimental.pallas import tpu as pltpu
from jax.sharding import PartitionSpec as P

R = 1000.0
SIDE = 0.3
BOTTOM = 0.5
TOPS = (0.05, 0.25, 0.8, 2.0)
F32 = jnp.float32
NLEV = 6


def recip(v):
    return 1.0 / v


def reduce_chain(c, s, d, track):
    levels, port, ties = [], None, []
    while len(s) > 1:
        half = len(s) // 2
        ml, mr, dv = [], [], []
        for j in range(half):
            i = 2 * j
            total = s[i] + c[i]
            if j:
                total = total + c[i - 1]
            inv = recip(total)
            mr.append(c[i] * inv)
            ml.append(c[i - 1] * inv if j else None)
            dv.append(d[i] * inv)
            if track and j == 0:
                if port is None:
                    port = [dv[0], inv, mr[0]]
                    ties.append(inv)
                else:
                    p, z, t = port
                    tie = t * inv
                    ties.append(tie)
                    port = [p + t * dv[0], z + t * tie, t * mr[0]]
        ns, nd, nc = [], [], []
        for j in range(half):
            e, o = 2 * j, 2 * j + 1
            sv = s[o] + mr[j] * s[e]
            dn = d[o] + mr[j] * d[e]
            if j + 1 < half:
                sv = sv + ml[j + 1] * s[e + 2]
                dn = dn + ml[j + 1] * d[e + 2]
                nc.append(ml[j + 1] * c[e + 2])
            ns.append(sv)
            nd.append(dn)
        levels.append((dv, ml, mr))
        c, s, d = nc, ns, nd
    return s[0], d[0], levels, port, ties


def expand_chain(u_last, levels, ties, flux):
    u = [u_last]
    for lev in range(len(levels) - 1, -1, -1):
        dv, ml, mr = levels[lev]
        out = []
        for j in range(len(u)):
            even = dv[j] + mr[j] * u[j]
            if j:
                even = even + ml[j] * u[j - 1]
            elif ties is not None:
                even = even + ties[lev] * flux
            out += [even, u[j]]
        u = out
    return u


def port_coefs(a, b):
    kfa, kla, za, ta, ga = a
    kfb, klb, zb, tb, gb = b
    link = R * jnp.minimum(kla, kfb)
    lk = link * recip(1.0 + link * zb)
    inv = recip(ga + lk)
    ti = ta * inv
    lt = lk * tb
    w = lt * inv
    merged = (kfa, klb, za + ta * ti, ta * w, gb + lt * tb * (ga * inv))
    return merged, (inv, lk, ta, lt, ti, w, tb)


def port_values(coefs, a, b):
    inv, lk, ta, lt, ti, w, tb = coefs
    pa, qa = a
    pb, qb = b
    h = inv * (qa + lk * pb)
    return (pa + ta * h, qb + lt * (h - pb)), (h, ti, w, lk, pb, tb)


def merge_ports(a, b):
    matrix, coefs = port_coefs(a[:5], b[:5])
    values, saved = port_values(coefs, a[5:], b[5:])
    return matrix + values, saved


def descend(saved, flux, u_b):
    h, ti, w, lk, pb, tb = saved
    u_a = h + ti * flux + w * u_b
    flux_b = lk * (u_a - pb - tb * u_b)
    return u_a, flux_b


def film_top(cls):
    total = jnp.zeros(cls.shape, F32)
    for n in range(4):
        total = total + TOPS[n] * (cls == n).astype(F32)
    return total


def node_order(half, lev):
    base, n = 0, half
    for _ in range(lev):
        base += n
        n //= 2
    return base, n


def put_levels(ref, levels):
    half = len(levels[0][0])
    for lev, triple in enumerate(levels):
        base, n = node_order(half, lev)
        for kind in range(3):
            for j in range(n):
                if triple[kind][j] is not None:
                    ref[kind, base + j] = triple[kind][j]


def get_levels(read, half):
    levels, lev = [], 0
    while half >> lev:
        base, n = node_order(half, lev)
        levels.append(
            tuple([None if kind == 1 and j == 0 else read(kind, base + j) for j in range(n)] for kind in range(3))
        )
        lev += 1
    return levels


def chain_matrix(c, s):
    z = t = None
    while len(s) > 1:
        half = len(s) // 2
        ml, mr = [None] * half, [None] * half
        for j in range(half):
            i = 2 * j
            inv = recip(s[i] + c[i] + c[i - 1] if j else s[i] + c[i])
            mr[j] = c[i] * inv
            if j:
                ml[j] = c[i - 1] * inv
            elif z is None:
                z, t = inv, mr[0]
            else:
                z, t = z + t * (t * inv), t * mr[0]
        ns, nc = [], []
        for j in range(half):
            e = 2 * j
            sv = s[e + 1] + mr[j] * s[e]
            if j + 1 < half:
                sv = sv + ml[j + 1] * s[e + 2]
                nc.append(ml[j + 1] * c[e + 2])
            ns.append(sv)
        c, s = nc, ns
    return z, t, s[0]


def wall_terms():
    me_x = lax.axis_index("gx")
    return jnp.where(me_x == 0, R * SIDE, 0.0), jnp.where(me_x == 15, R * SIDE, 0.0)


def own_half():
    me_x = lax.axis_index("gx")
    return lax.rem(me_x + lax.div(me_x, 2) + lax.div(me_x, 8), 2)


def split_halves(planes, keep, send):
    core = own_half()
    for i in range(planes.shape[0]):
        keep[32 * i : 32 * i + 32] = planes[i, pl.ds(pl.multiple_of(32 * core, 32), 32), :]
        send[32 * i : 32 * i + 32] = planes[i, pl.ds(pl.multiple_of(32 - 32 * core, 32), 32), :]


def fields_kernel(cot_in, temp_in, sub_in, dep_in, cls_in, cond, keep, send, cot, sub, dep, cls, temp, planes, sems):
    pairs = ((sub_in, sub), (dep_in, dep), (temp_in, temp), (cls_in, cls), (cot_in, cot))
    copies = [pltpu.make_async_copy(a, b, sems.at[i]) for i, (a, b) in enumerate(pairs)]
    for cp in copies:
        cp.start()
    for cp in copies[:3]:
        cp.wait()
    sub_v, dep_v = sub[...], dep[...]
    for z in range(64):
        base = jnp.where(z < sub_v, 1.0, 0.45)
        sg = 0.5 + jax.nn.sigmoid(temp[8 * z : 8 * z + 8])
        cond[8 * z : 8 * z + 8] = jnp.where(z < dep_v, base * sg, 0.0)
    low, high = wall_terms()
    base_z = lax.broadcasted_iota(jnp.int32, (8, 128), 0)
    for chunk in range(8):
        zi = base_z + 8 * chunk
        k = [cond[pl.ds(64 * chunk + x, 8, stride=8), :] for x in range(8)]
        s = [jnp.where(zi < sub_v[x : x + 1], 1.0, 0.6) for x in range(8)]
        s[0] = s[0] + low
        s[7] = s[7] + high
        c = [R * jnp.minimum(k[x], k[x + 1]) for x in range(7)] + [None]
        for i, v in enumerate((k[0], k[7]) + chain_matrix(c, s)):
            planes[i, 8 * chunk : 8 * chunk + 8] = v
    split_halves(planes, keep, send)
    for cp in copies[3:]:
        cp.wait()


def first_kernel(cot, sub, dep, cls, cond, ypack, fac, tie_out, mid, tr):
    me_y = lax.axis_index("gy")
    sub_v, dep_v = sub[...], dep[...]
    top = film_top(cls[...])
    k, cap, s = [], [], []
    for z in range(64):
        k.append(cond[8 * z : 8 * z + 8])
        cap.append(jnp.where(z < sub_v, 1.0, 0.6))
        film = top * (dep_v - 1 == z).astype(F32)
        if z == 0:
            film = film + BOTTOM
        s.append(cap[z] + R * film)
    c = [R * jnp.minimum(k[z], k[z + 1]) for z in range(63)] + [None]
    d = [cot[8 * z : 8 * z + 8] for z in range(64)]
    g, q, levels, _, _ = reduce_chain(c, s, d, False)
    u = expand_chain(q * recip(g), levels, None, None)
    for z in range(64):
        tr[8 * z : 8 * z + 8] = cap[z] * u[z]

    def turned(rows, dst, q):
        block = jnp.transpose(rows)
        for h in range(2):
            dst[pl.ds(4 * h + q, 64, stride=8), :] = block[64 * h : 64 * h + 64]

    subf = sub_v.astype(F32)
    upper = (lax.broadcasted_iota(jnp.int32, (128, 128), 0) & 1) == 1
    for q in range(4):
        turned(cond[pl.ds(q, 128, stride=4), :], mid.at[0], q)
        turned(tr[pl.ds(q, 128, stride=4), :], mid.at[1], q)
        turned(jnp.where(upper, subf[q + 4 : q + 5], subf[q : q + 1]), mid.at[2], q)
    z_lane = (lax.broadcasted_iota(jnp.int32, (8, 128), 1) >> 1).astype(F32)
    row = lax.broadcasted_iota(jnp.int32, (8, 128), 0)
    ky, sy, dy = [], [], []
    for y in range(64):
        ky.append(mid[0, 8 * y : 8 * y + 8])
        dy.append(mid[1, 8 * y : 8 * y + 8])
        sy.append(jnp.where(z_lane < mid[2, 8 * y : 8 * y + 8], 1.0, 0.6))
    cap_first, cap_last = sy[0][0:4], sy[63][4:8]
    low = jnp.where(me_y == 0, R * SIDE, 0.0)
    high = jnp.where(me_y == 7, R * SIDE, 0.0)
    sy[0] = sy[0] + jnp.where(row < 4, low, 0.0)
    sy[63] = sy[63] + jnp.where(row >= 4, high, 0.0)
    cy = [R * jnp.minimum(ky[y], ky[y + 1]) for y in range(63)] + [None]
    g, q, levels, (p, zz, t), ties = reduce_chain(cy, sy, dy, True)
    put_levels(fac, levels)
    for lev in range(NLEV):
        tie_out[lev] = ties[lev]
    kf, kl = ky[0], ky[63]
    side_a = tuple(v[0:4] for v in (kf, kl, zz, t, g, p, q))
    side_b = tuple(v[4:8] for v in (kf, kl, zz, t, g, p, q))
    merged, saved = merge_ports(side_a, side_b)
    for i, v in enumerate(saved):
        tie_out[NLEV + i, 0:4] = v
    pack = jnp.concatenate(list(merged) + [cap_first, cap_last, jnp.zeros((4, 128), F32)], axis=0)
    for n in range(8):
        ypack[n] = pack


def second_kernel(gat, fac, ties, cond, sub, keep, send, xfac, xhfac, a2_out, kh_out, pick, flat, planes, xp):
    me_y = lax.axis_index("gy")
    seg = [[gat[n, 4 * i : 4 * i + 4] for i in range(9)] for n in range(8)]
    gam, rhs = seg[0][4], seg[0][6]
    down, links = [None], [None]
    for n in range(1, 8):
        kf, kl, z, t, g, p, q = seg[n][:7]
        link = R * jnp.minimum(seg[n - 1][1], kf)
        lk = link * recip(1.0 + link * z)
        inv = recip(gam + lk)
        h = inv * (rhs + lk * p)
        lt = lk * t
        down.append((h, lt * inv))
        links.append(lk)
        rhs = q + lt * (h - p)
        gam = g + lt * t * (gam * inv)
    u = [None] * 8
    u[7] = rhs * recip(gam)
    for n in range(7, 0, -1):
        u[n - 1] = down[n][0] + down[n][1] * u[n]
    zero4 = jnp.zeros((4, 128), F32)
    fl, uf = [zero4], [None]
    for n in range(1, 8):
        kf, kl, z, t, g, p, q = seg[n][:7]
        fl.append(links[n] * (u[n - 1] - p - t * u[n]))
        uf.append(p + z * fl[n] + t * u[n])
    for n in range(8):
        rows = [fl[n], u[n]]
        if n:
            rows += [seg[n - 1][8] * u[n - 1], seg[n - 1][1], seg[n - 1][8]]
        else:
            rows += [zero4, zero4, zero4 + 1.0]
        if n < 7:
            rows += [seg[n + 1][7] * uf[n + 1], seg[n + 1][0], seg[n + 1][7]]
        else:
            rows += [zero4, zero4, zero4 + 1.0]
        for i, v in enumerate(rows):
            pick[n, 4 * i : 4 * i + 4] = v
    mine = [pick[me_y, 4 * i : 4 * i + 4] for i in range(8)]
    flux, u_b = mine[0], mine[1]
    saved = tuple(ties[NLEV + i, 0:4] for i in range(6))
    u_a, flux_b = descend(saved, flux, u_b)
    flux8 = jnp.concatenate([flux, flux_b], axis=0)
    last8 = jnp.concatenate([u_a, u_b], axis=0)
    levels = get_levels(lambda kind, i: fac[kind, i], 32)
    u_nodes = expand_chain(last8, levels, [ties[i] for i in range(NLEV)], flux8)
    for y in range(64):
        flat[8 * y : 8 * y + 8] = u_nodes[y]
    subf = sub[...]
    for q in range(4):
        planes[pl.ds(q, 128, stride=4), :] = jnp.transpose(
            jnp.concatenate([flat[pl.ds(q, 64, stride=8), :], flat[pl.ds(4 + q, 64, stride=8), :]], axis=0)
        )

    even = (lax.broadcasted_iota(jnp.int32, (4, 128), 1) & 1) == 0

    def both(left, right):
        low = jnp.where(even, left, pltpu.roll(right, 127, 1))
        high = jnp.where(even, pltpu.roll(left, 127, 1), pltpu.roll(right, 126, 1))
        return [low[x : x + 1] for x in range(4)] + [high[x : x + 1] for x in range(4)]

    dh, kh, caph = both(mine[2], mine[5]), both(mine[3], mine[6]), both(mine[4], mine[7])
    for x in range(8):
        kh_out[x : x + 1] = kh[x]

    low, high = wall_terms()

    def x_chain(k, cap, d):
        s = list(cap)
        s[0] = s[0] + low
        s[7] = s[7] + high
        c = [R * jnp.minimum(k[x], k[x + 1]) for x in range(7)] + [None]
        g, q, levels, (p, z, t), tie = reduce_chain(c, s, d, True)
        return levels, tie, (k[0], k[7], z, t, g, p, q)

    base_z = lax.broadcasted_iota(jnp.int32, (8, 128), 0)
    for chunk in range(8):
        zi = base_z + 8 * chunk
        k, cap, d = [], [], []
        for x in range(8):
            k.append(cond[pl.ds(64 * chunk + x, 8, stride=8), :])
            cap.append(jnp.where(zi < subf[x : x + 1], 1.0, 0.6))
            dx = cap[x] * planes[pl.ds(64 * chunk + x, 8, stride=8), :]
            a2_out[pl.ds(64 * chunk + x, 8, stride=8), :] = dx
            d.append(dx)
        levels, tie, port = x_chain(k, cap, d)
        store_x(xfac.at[chunk], levels, tie)
        for i in range(2):
            xp[i, 8 * chunk : 8 * chunk + 8] = port[5 + i]
    levels, tie, port = x_chain(kh, caph, dh)
    store_x(xhfac, levels, tie)
    split_halves(xp, keep, send)
    for i in range(7):
        keep[64 + i : 65 + i] = port[i]
        send[64 + i : 65 + i] = port[i]


def store_x(ref, levels, tie):
    for lev, triple in enumerate(levels):
        base, n = node_order(4, lev)
        for kind in range(3):
            for j in range(n):
                if triple[kind][j] is not None:
                    ref[7 * kind + base + j] = triple[kind][j]
    for lev in range(3):
        ref[21 + lev] = tie[lev]


def load_x(ref):
    levels = get_levels(lambda kind, i: ref[7 * kind + i], 4)
    return levels, [ref[21 + lev] for lev in range(3)]


def read_pack(ref, n):
    main = tuple(ref[32 * i : 32 * i + 32] for i in range(n))
    edge = tuple(ref[32 * n + i : 32 * n + i + 1] for i in range(n))
    return main, edge


def write_pack(ref, main, edge):
    n = len(main)
    for i in range(n):
        ref[32 * i : 32 * i + 32] = main[i]
        ref[32 * n + i : 32 * n + i + 1] = edge[i]


def order(right, mine, theirs):
    a = tuple(jnp.where(right, t, m) for m, t in zip(mine, theirs))
    b = tuple(jnp.where(right, m, t) for m, t in zip(mine, theirs))
    return a, b


def planes_of(ref, n):
    return tuple(ref[32 * i : 32 * i + 32] for i in range(n))


def put_planes(ref, values):
    for i, v in enumerate(values):
        ref[32 * i : 32 * i + 32] = v


def spots():
    me_x = lax.axis_index("gx")
    return [lax.rem(lax.div(me_x, bit), 2) == 1 for bit in (1, 2, 4)]


def core_matrix_kernel(mine, theirs, merged_out, coef_out):
    odd, _, _ = spots()
    merged, coefs = port_coefs(*order(odd, planes_of(mine, 5), planes_of(theirs, 5)))
    put_planes(merged_out, merged)
    put_planes(coef_out, coefs)


def ring_matrix_kernel(own, mid, far, near, merged_out, mine_out, other_out, ring_out):
    _, right, upper = spots()
    packs = [planes_of(r, 5) for r in (own, near, mid, far)]
    mine, mine_c = port_coefs(*order(right, packs[0], packs[1]))
    other, other_c = port_coefs(*order(right, packs[2], packs[3]))
    merged, ring_c = port_coefs(*order(upper, mine, other))
    put_planes(merged_out, merged)
    put_planes(mine_out, mine_c)
    put_planes(other_out, other_c)
    put_planes(ring_out, ring_c)


def read_sides(ref):
    main = (ref[0:32], ref[32:64])
    edge = tuple(ref[64 + i : 65 + i] for i in range(7))
    return main, edge


def core_kernel(mine, theirs, coefs, merged_out, saved_out):
    odd, _, _ = spots()
    m, t = read_sides(mine), read_sides(theirs)
    values, saved = port_values(planes_of(coefs, 7), *order(odd, m[0], t[0]))
    edge, edge_saved = merge_ports(*order(odd, m[1], t[1]))
    put_planes(merged_out, values)
    for i in range(7):
        merged_out[64 + i : 65 + i] = edge[i]
    write_pack(saved_out, saved, edge_saved)


def ring_kernel(own, mid, far, near, matrix, mine_c, other_c, ring_c, merged_out, pair_out, saved_out, top_out):
    _, right, upper = spots()
    last = lax.div(lax.axis_index("gx"), 8) == 1
    main, edge = zip(*[read_sides(r) for r in (own, near, mid, far)])
    mine, pair = port_values(planes_of(mine_c, 7), *order(right, main[0], main[1]))
    other, _ = port_values(planes_of(other_c, 7), *order(right, main[2], main[3]))
    values, saved = port_values(planes_of(ring_c, 7), *order(upper, mine, other))
    e_mine, e_pair = merge_ports(*order(right, edge[0], edge[1]))
    e_other, _ = merge_ports(*order(right, edge[2], edge[3]))
    e_merged, e_saved = merge_ports(*order(upper, e_mine, e_other))
    outs = [planes_of(matrix, 5) + values, e_merged]
    tops = []
    for kf, kl, z, tt, g, p, q in outs:
        tg = tt * recip(g)
        tops.append((jnp.where(last, z + tt * tg, g), jnp.where(last, p + tg * q, q), jnp.where(last, kf, kl)))
    write_pack(merged_out, *outs)
    write_pack(pair_out, pair, e_pair)
    write_pack(saved_out, saved, e_saved)
    write_pack(top_out, *tops)


def top_kernel(merged, near, theirs, sv1, sv2, sv3, own, send):
    me_x = lax.axis_index("gx")
    far = lax.div(me_x, 8) == 1
    mm = read_pack(merged, 7)
    n, t = read_pack(near, 3), read_pack(theirs, 3)
    saved = [read_pack(r, 6) for r in (sv1, sv2, sv3)]
    final = []
    for part in range(2):
        (ga, qa, ka), (zb, pb, kb) = order(far, n[part], t[part])
        link = R * jnp.minimum(ka, kb)
        lk = link * recip(1.0 + link * zb)
        u_a = (qa + lk * pb) * recip(ga + lk)
        kf, kl, z, tt, g, p, q = mm[part]
        flux = jnp.where(far, lk * (u_a - pb), 0.0)
        u = jnp.where(far, (q + tt * flux) * recip(g), u_a)
        for bit, lev in ((4, 2), (2, 1)):
            right = lax.rem(lax.div(me_x, bit), 2) == 1
            ua, fb = descend(saved[lev][part], flux, u)
            flux = jnp.where(right, fb, flux)
            u = jnp.where(right, u, ua)
        ua, fb = descend(saved[0][part], flux, u)
        odd = lax.rem(me_x, 2) == 1
        final.append((jnp.where(odd, fb, flux), jnp.where(odd, u, ua), jnp.where(odd, flux, fb), jnp.where(odd, ua, u)))
    write_pack(own, final[0][:2], final[1][:2])
    send[0:32] = final[0][2]
    send[32:64] = final[0][3]


def coef_kernel(cond, kh, a2, cot, sub, dep, cls, k_y, k_l, k_z, k_s, base):
    me_y = lax.axis_index("gy")
    sub_v, dep_v, kh_v = sub[...], dep[...], kh[...]
    top = film_top(cls[...])
    lane = lax.broadcasted_iota(jnp.int32, (8, 128), 1)
    first, final = lane == 0, lane == 127
    film_y = jnp.where(first & (me_y == 0), SIDE, 0.0) + jnp.where(final & (me_y == 7), SIDE, 0.0)
    for z in range(64):
        rows = slice(8 * z, 8 * z + 8)
        k = cond[rows]
        k_h = pltpu.roll(kh_v, 128 - 2 * z, 1) if z else kh_v
        k_y[rows] = (2.0 * R) * jnp.minimum(k, jnp.where(final, k_h, pltpu.roll(k, 127, 1)))
        k_l[rows] = (2.0 * R) * jnp.minimum(k, k_h)
        if z < 63:
            k_z[rows] = (2.0 * R) * jnp.minimum(k, cond[8 * z + 8 : 8 * z + 16])
        film = film_y + top * (dep_v - 1 == z).astype(F32)
        if z == 0:
            film = film + BOTTOM
        k_s[rows] = 2.0 * jnp.where(z < sub_v, 1.0, 0.6) - (2.0 * R) * film
        base[rows] = cot[rows] - 2.0 * a2[rows]


def last_kernel(
    own, got, xfac, xhfac, k_y, k_l, k_z, k_s, base, sub, temp_out, src_out, s1, fu, t_buf, s_buf, sems
):
    core = own_half()
    for i in range(2):
        fu[i, pl.ds(pl.multiple_of(32 * core, 32), 32), :] = own[32 * i : 32 * i + 32]
        fu[i, pl.ds(pl.multiple_of(32 - 32 * core, 32), 32), :] = got[32 * i : 32 * i + 32]
    levels, tie = load_x(xhfac)
    uh = jnp.concatenate(expand_chain(own[65:66], levels, tie, own[64:65]), axis=0)
    sub_v = sub[...]
    lane = lax.broadcasted_iota(jnp.int32, (8, 128), 1)
    first, final = lane == 0, lane == 127
    up, copies = None, []

    def expand(chunk):
        rows = slice(8 * chunk, 8 * chunk + 8)
        levels, tie = load_x(xfac.at[chunk])
        u = expand_chain(fu[1, rows], levels, tie, fu[0, rows])
        for x in range(8):
            s1[pl.ds(64 * chunk + x, 8, stride=8), :] = u[x]

    expand(0)
    for z in range(64):
        if z & 7 == 0 and z < 56:
            expand(z // 8 + 1)
        rows = slice(8 * z, 8 * z + 8)
        s = s1[rows]
        s_h = pltpu.roll(uh, 128 - 2 * z, 1) if z else uh
        f_y = k_y[rows] * (jnp.where(final, s_h, pltpu.roll(s, 127, 1)) - s)
        f_l = k_l[rows] * (s - s_h)
        total = f_y - jnp.where(first, f_l, pltpu.roll(f_y, 1, 1))
        if z < 63:
            f_z = k_z[rows] * (s1[8 * z + 8 : 8 * z + 16] - s)
            total = total + f_z
        if z:
            total = total - up
        up = f_z
        s_buf[rows] = jnp.where(z < sub_v, 1.0, 0.6) * s
        t_buf[rows] = base[rows] + k_s[rows] * s + total
        if z & 7 == 7:
            part = slice(8 * z - 56, 8 * z + 8)
            for i, (buf, out) in enumerate(((s_buf, src_out), (t_buf, temp_out))):
                cp = pltpu.make_async_copy(buf.at[part], out.at[part], sems.at[2 * (z // 8) + i])
                cp.start()
                copies.append(cp)
    for cp in copies:
        cp.wait()


VMEM = pl.BlockSpec(memory_space=pltpu.VMEM)
HBM = pl.BlockSpec(memory_space=pltpu.MemorySpace.HBM)


def call(kernel, outs, scratch, name, *args, far_in=0, far_out=0, sems=0):
    shapes = [s if isinstance(s, jax.ShapeDtypeStruct) else jax.ShapeDtypeStruct(s, F32) for s in outs]
    scr = [pltpu.VMEM(s, F32) for s in scratch]
    args = [pltpu.with_memory_space_constraint(a, pltpu.MemorySpace.HBM) if i < far_in else a for i, a in enumerate(args)]
    if sems:
        scr.append(pltpu.SemaphoreType.DMA((sems,)))
    return pl.pallas_call(
        kernel,
        out_shape=shapes,
        in_specs=[HBM if i < far_in else VMEM for i in range(len(args))],
        out_specs=[HBM if i < far_out else VMEM for i in range(len(outs))],
        scratch_shapes=scr,
        compiler_params=pltpu.CompilerParams(vmem_limit_bytes=40 * 1024 * 1024),
        name=name,
    )(*args)


def swap(v, bit):
    return lax.ppermute(v, "gx", [(i, i ^ bit) for i in range(16)])


def body(cotangent, saved_temp, substrate_top, deposit_top, top_class):
    cot = cotangent.reshape(512, 128)
    temp = saved_temp.reshape(512, 128)
    small = jax.ShapeDtypeStruct((8, 128), jnp.int32)
    cond, keep_m, send_m, cot, sub, dep, cls = call(
        fields_kernel,
        [(512, 128), (160, 128), (160, 128), (512, 128), small, small, small],
        [(512, 128), (5, 64, 128)],
        "fields",
        cot, temp, substrate_top, deposit_top, top_class,
        far_in=5, sems=5,
    )
    other_m = swap(send_m, 1)
    ypack, fac, ties = call(
        first_kernel,
        [(8, 40, 128), (3, 63, 8, 128), (12, 8, 128)],
        [(3, 512, 128), (512, 128)],
        "first",
        cot, sub, dep, cls, cond,
    )
    mm, core_c = call(core_matrix_kernel, [(160, 128), (224, 128)], [], "matrix_core", keep_m, other_m)
    mm, ypack = lax.optimization_barrier((mm, ypack))
    gat = lax.all_to_all(ypack, "gy", split_axis=0, concat_axis=0, tiled=True)
    ring_m = [swap(mm, bit) for bit in (4, 7, 3)]
    keep, send, xfac, xhfac, a2, kh = call(
        second_kernel,
        [(72, 128), (72, 128), (8, 24, 8, 128), (24, 1, 128), (512, 128), (8, 128)],
        [(8, 32, 128), (512, 128), (512, 128), (2, 64, 128)],
        "second",
        gat, fac, ties, cond, sub,
    )
    m1, sv1 = call(core_kernel, [(72, 128), (200, 128)], [], "merge_core", keep, swap(send, 1), core_c)
    ring_v = [swap(m1, bit) for bit in (4, 7, 3)]
    matrix, mine_c, other_c, ring_c = call(
        ring_matrix_kernel, [(160, 128)] + [(224, 128)] * 3, [], "matrix_ring", mm, *ring_m
    )
    m3, sv2, sv3, near = call(
        ring_kernel,
        [(232, 128), (200, 128), (200, 128), (104, 128)],
        [],
        "merge_ring",
        m1, *ring_v, matrix, mine_c, other_c, ring_c,
    )
    sv3, kh = lax.optimization_barrier((sv3, kh))
    coefs = call(coef_kernel, [(512, 128)] * 5, [], "coef", cond, kh, a2, cot, sub, dep, cls)
    opposite = swap(near, 9)
    sv3, coefs = lax.optimization_barrier((sv3, coefs))
    own, out = call(top_kernel, [(72, 128), (64, 128)], [], "top", m3, near, opposite, sv1, sv2, sv3)
    got = swap(out, 1)
    grad_temp, grad_source = call(
        last_kernel,
        [(512, 128), (512, 128)],
        [(512, 128), (2, 64, 128), (512, 128), (512, 128)],
        "last",
        own, got, xfac, xhfac, *coefs, sub,
        far_out=2, sems=16,
    )
    return grad_temp.reshape(cotangent.shape), grad_source.reshape(cotangent.shape)


def solution(mesh):
    in_specs = (
        P(None, "gx", "gy"),
        P(None, "gx", "gy"),
        P("gx", "gy"),
        P("gx", "gy"),
        P("gx", "gy"),
    )
    out_specs = (P(None, "gx", "gy"), P(None, "gx", "gy"))
    return jax.shard_map(body, mesh=mesh, in_specs=in_specs, out_specs=out_specs, check_vma=False)
```

```python
import jax
import jax.numpy as jnp
from jax import lax
from jax.experimental import pallas as pl
from jax.experimental.pallas import tpu as pltpu
from jax.sharding import PartitionSpec as P

R = 1000.0
SIDE = 0.3
BOTTOM = 0.5
TOPS = (0.05, 0.25, 0.8, 2.0)
F32 = jnp.float32
NLEV = 6


def recip(v):
    return 1.0 / v


def reduce_chain(c, s, d, track):
    levels, port, ties = [], None, []
    while len(s) > 1:
        half = len(s) // 2
        ml, mr, dv = [], [], []
        for j in range(half):
            i = 2 * j
            total = s[i] + c[i]
            if j:
                total = total + c[i - 1]
            inv = recip(total)
            mr.append(c[i] * inv)
            ml.append(c[i - 1] * inv if j else None)
            dv.append(d[i] * inv)
            if track and j == 0:
                if port is None:
                    port = [dv[0], inv, mr[0]]
                    ties.append(inv)
                else:
                    p, z, t = port
                    tie = t * inv
                    ties.append(tie)
                    port = [p + t * dv[0], z + t * tie, t * mr[0]]
        ns, nd, nc = [], [], []
        for j in range(half):
            e, o = 2 * j, 2 * j + 1
            sv = s[o] + mr[j] * s[e]
            dn = d[o] + mr[j] * d[e]
            if j + 1 < half:
                sv = sv + ml[j + 1] * s[e + 2]
                dn = dn + ml[j + 1] * d[e + 2]
                nc.append(ml[j + 1] * c[e + 2])
            ns.append(sv)
            nd.append(dn)
        levels.append((dv, ml, mr))
        c, s, d = nc, ns, nd
    return s[0], d[0], levels, port, ties


def expand_chain(u_last, levels, ties, flux):
    u = [u_last]
    for lev in range(len(levels) - 1, -1, -1):
        dv, ml, mr = levels[lev]
        out = []
        for j in range(len(u)):
            even = dv[j] + mr[j] * u[j]
            if j:
                even = even + ml[j] * u[j - 1]
            elif ties is not None:
                even = even + ties[lev] * flux
            out += [even, u[j]]
        u = out
    return u


def port_coefs(a, b):
    kfa, kla, za, ta, ga = a
    kfb, klb, zb, tb, gb = b
    link = R * jnp.minimum(kla, kfb)
    lk = link * recip(1.0 + link * zb)
    inv = recip(ga + lk)
    ti = ta * inv
    lt = lk * tb
    w = lt * inv
    merged = (kfa, klb, za + ta * ti, ta * w, gb + lt * tb * (ga * inv))
    return merged, (inv, lk, ta, lt, ti, w, tb)


def port_values(coefs, a, b):
    inv, lk, ta, lt, ti, w, tb = coefs
    pa, qa = a
    pb, qb = b
    h = inv * (qa + lk * pb)
    return (pa + ta * h, qb + lt * (h - pb)), (h, ti, w, lk, pb, tb)


def merge_ports(a, b):
    matrix, coefs = port_coefs(a[:5], b[:5])
    values, saved = port_values(coefs, a[5:], b[5:])
    return matrix + values, saved


def descend(saved, flux, u_b):
    h, ti, w, lk, pb, tb = saved
    u_a = h + ti * flux + w * u_b
    flux_b = lk * (u_a - pb - tb * u_b)
    return u_a, flux_b


def film_top(cls):
    total = jnp.zeros(cls.shape, F32)
    for n in range(4):
        total = total + TOPS[n] * (cls == n).astype(F32)
    return total


def node_order(half, lev):
    base, n = 0, half
    for _ in range(lev):
        base += n
        n //= 2
    return base, n


def put_levels(ref, levels):
    half = len(levels[0][0])
    for lev, triple in enumerate(levels):
        base, n = node_order(half, lev)
        for kind in range(3):
            for j in range(n):
                if triple[kind][j] is not None:
                    ref[kind, base + j] = triple[kind][j]


def get_levels(read, half):
    levels, lev = [], 0
    while half >> lev:
        base, n = node_order(half, lev)
        levels.append(
            tuple([None if kind == 1 and j == 0 else read(kind, base + j) for j in range(n)] for kind in range(3))
        )
        lev += 1
    return levels


def chain_matrix(c, s):
    z = t = None
    while len(s) > 1:
        half = len(s) // 2
        ml, mr = [None] * half, [None] * half
        for j in range(half):
            i = 2 * j
            inv = recip(s[i] + c[i] + c[i - 1] if j else s[i] + c[i])
            mr[j] = c[i] * inv
            if j:
                ml[j] = c[i - 1] * inv
            elif z is None:
                z, t = inv, mr[0]
            else:
                z, t = z + t * (t * inv), t * mr[0]
        ns, nc = [], []
        for j in range(half):
            e = 2 * j
            sv = s[e + 1] + mr[j] * s[e]
            if j + 1 < half:
                sv = sv + ml[j + 1] * s[e + 2]
                nc.append(ml[j + 1] * c[e + 2])
            ns.append(sv)
        c, s = nc, ns
    return z, t, s[0]


def wall_terms():
    me_x = lax.axis_index("gx")
    return jnp.where(me_x == 0, R * SIDE, 0.0), jnp.where(me_x == 15, R * SIDE, 0.0)


def own_half():
    me_x = lax.axis_index("gx")
    return lax.rem(me_x + lax.div(me_x, 2) + lax.div(me_x, 8), 2)


def split_halves(planes, keep, send):
    core = own_half()
    for i in range(planes.shape[0]):
        keep[32 * i : 32 * i + 32] = planes[i, pl.ds(pl.multiple_of(32 * core, 32), 32), :]
        send[32 * i : 32 * i + 32] = planes[i, pl.ds(pl.multiple_of(32 - 32 * core, 32), 32), :]


def fields_kernel(cot_in, temp_in, sub_in, dep_in, cls_in, cond, keep, send, cot, sub, dep, cls, temp, planes, sems):
    pieces = [slice(128 * i, 128 * i + 128) for i in range(4)]
    pairs = [(sub_in, sub), (dep_in, dep)] + [(temp_in.at[r], temp.at[r]) for r in pieces]
    pairs += [(cls_in, cls), (cot_in, cot)]
    copies = [pltpu.make_async_copy(a, b, sems.at[i]) for i, (a, b) in enumerate(pairs)]
    for cp in copies:
        cp.start()
    for cp in copies[:2]:
        cp.wait()
    sub_v, dep_v = sub[...], dep[...]
    for z in range(64):
        if z % 16 == 0:
            copies[2 + z // 16].wait()
        base = jnp.where(z < sub_v, 1.0, 0.45)
        sg = 0.5 + jax.nn.sigmoid(temp[8 * z : 8 * z + 8])
        cond[8 * z : 8 * z + 8] = jnp.where(z < dep_v, base * sg, 0.0)
    low, high = wall_terms()
    base_z = lax.broadcasted_iota(jnp.int32, (8, 128), 0)
    for chunk in range(8):
        zi = base_z + 8 * chunk
        k = [cond[pl.ds(64 * chunk + x, 8, stride=8), :] for x in range(8)]
        s = [jnp.where(zi < sub_v[x : x + 1], 1.0, 0.6) for x in range(8)]
        s[0] = s[0] + low
        s[7] = s[7] + high
        c = [R * jnp.minimum(k[x], k[x + 1]) for x in range(7)] + [None]
        for i, v in enumerate((k[0], k[7]) + chain_matrix(c, s)):
            planes[i, 8 * chunk : 8 * chunk + 8] = v
    split_halves(planes, keep, send)
    for cp in copies[6:]:
        cp.wait()


def first_kernel(cot, sub, dep, cls, cond, ypack, fac, tie_out, mid, tr):
    me_y = lax.axis_index("gy")
    sub_v, dep_v = sub[...], dep[...]
    top = film_top(cls[...])
    k, cap, s = [], [], []
    for z in range(64):
        k.append(cond[8 * z : 8 * z + 8])
        cap.append(jnp.where(z < sub_v, 1.0, 0.6))
        film = top * (dep_v - 1 == z).astype(F32)
        if z == 0:
            film = film + BOTTOM
        s.append(cap[z] + R * film)
    c = [R * jnp.minimum(k[z], k[z + 1]) for z in range(63)] + [None]
    d = [cot[8 * z : 8 * z + 8] for z in range(64)]
    g, q, levels, _, _ = reduce_chain(c, s, d, False)
    u = expand_chain(q * recip(g), levels, None, None)
    for z in range(64):
        tr[8 * z : 8 * z + 8] = cap[z] * u[z]

    def turned(rows, dst, q):
        block = jnp.transpose(rows)
        for h in range(2):
            dst[pl.ds(4 * h + q, 64, stride=8), :] = block[64 * h : 64 * h + 64]

    subf = sub_v.astype(F32)
    upper = (lax.broadcasted_iota(jnp.int32, (128, 128), 0) & 1) == 1
    for q in range(4):
        turned(cond[pl.ds(q, 128, stride=4), :], mid.at[0], q)
        turned(tr[pl.ds(q, 128, stride=4), :], mid.at[1], q)
        turned(jnp.where(upper, subf[q + 4 : q + 5], subf[q : q + 1]), mid.at[2], q)
    z_lane = (lax.broadcasted_iota(jnp.int32, (8, 128), 1) >> 1).astype(F32)
    row = lax.broadcasted_iota(jnp.int32, (8, 128), 0)
    ky, sy, dy = [], [], []
    for y in range(64):
        ky.append(mid[0, 8 * y : 8 * y + 8])
        dy.append(mid[1, 8 * y : 8 * y + 8])
        sy.append(jnp.where(z_lane < mid[2, 8 * y : 8 * y + 8], 1.0, 0.6))
    low = jnp.where(me_y == 0, R * SIDE, 0.0)
    high = jnp.where(me_y == 7, R * SIDE, 0.0)
    sy[0] = sy[0] + jnp.where(row < 4, low, 0.0)
    sy[63] = sy[63] + jnp.where(row >= 4, high, 0.0)
    cy = [R * jnp.minimum(ky[y], ky[y + 1]) for y in range(63)] + [None]
    g, q, levels, (p, zz, t), ties = reduce_chain(cy, sy, dy, True)
    put_levels(fac, levels)
    for lev in range(NLEV):
        tie_out[lev] = ties[lev]
    kf, kl = ky[0], ky[63]
    side_a = tuple(v[0:4] for v in (kf, kl, zz, t, g, p, q))
    side_b = tuple(v[4:8] for v in (kf, kl, zz, t, g, p, q))
    merged, saved = merge_ports(side_a, side_b)
    for i, v in enumerate(saved):
        tie_out[NLEV + i, 0:4] = v
    lower = lax.broadcasted_iota(jnp.int32, (4, 128), 1) < 64
    edges = jnp.where(lower, mid[2, 0:4], mid[2, 508:512])
    pack = jnp.concatenate(list(merged) + [edges], axis=0)
    for n in range(8):
        ypack[n] = pack


def second_kernel(gat, fac, ties, cond, sub, keep, send, xfac, xhfac, a2_out, kh_out, pick, flat, planes, xp):
    me_y = lax.axis_index("gy")
    seg = [[gat[n, 4 * i : 4 * i + 4] for i in range(8)] for n in range(8)]
    gam, rhs = seg[0][4], seg[0][6]
    down, links = [None], [None]
    for n in range(1, 8):
        kf, kl, z, t, g, p, q = seg[n][:7]
        link = R * jnp.minimum(seg[n - 1][1], kf)
        lk = link * recip(1.0 + link * z)
        inv = recip(gam + lk)
        h = inv * (rhs + lk * p)
        lt = lk * t
        down.append((h, lt * inv))
        links.append(lk)
        rhs = q + lt * (h - p)
        gam = g + lt * t * (gam * inv)
    u = [None] * 8
    u[7] = rhs * recip(gam)
    for n in range(7, 0, -1):
        u[n - 1] = down[n][0] + down[n][1] * u[n]
    zero4 = jnp.zeros((4, 128), F32)
    fl, uf = [zero4], [None]
    for n in range(1, 8):
        kf, kl, z, t, g, p, q = seg[n][:7]
        fl.append(links[n] * (u[n - 1] - p - t * u[n]))
        uf.append(p + z * fl[n] + t * u[n])
    for n in range(8):
        rows = [fl[n], u[n]]
        if n:
            rows += [u[n - 1], seg[n - 1][1], seg[n - 1][7]]
        else:
            rows += [zero4, zero4, zero4]
        if n < 7:
            rows += [uf[n + 1], seg[n + 1][0], seg[n + 1][7]]
        else:
            rows += [zero4, zero4, zero4]
        for i, v in enumerate(rows):
            pick[n, 4 * i : 4 * i + 4] = v
    mine = [pick[me_y, 4 * i : 4 * i + 4] for i in range(8)]
    flux, u_b = mine[0], mine[1]
    saved = tuple(ties[NLEV + i, 0:4] for i in range(6))
    u_a, flux_b = descend(saved, flux, u_b)
    flux8 = jnp.concatenate([flux, flux_b], axis=0)
    last8 = jnp.concatenate([u_a, u_b], axis=0)
    levels = get_levels(lambda kind, i: fac[kind, i], 32)
    u_nodes = expand_chain(last8, levels, [ties[i] for i in range(NLEV)], flux8)
    for y in range(64):
        flat[8 * y : 8 * y + 8] = u_nodes[y]
    subf = sub[...]
    for q in range(4):
        planes[pl.ds(q, 128, stride=4), :] = jnp.transpose(
            jnp.concatenate([flat[pl.ds(q, 64, stride=8), :], flat[pl.ds(4 + q, 64, stride=8), :]], axis=0)
        )

    lane = lax.broadcasted_iota(jnp.int32, (4, 128), 1)
    even = (lane & 1) == 0
    z_of = (lane >> 1).astype(F32)
    cap_l = jnp.where(z_of < jnp.where(lane < 64, pltpu.roll(mine[4], 64, 1), mine[4]), 1.0, 0.6)
    cap_r = jnp.where(z_of < jnp.where(lane < 64, mine[7], pltpu.roll(mine[7], 64, 1)), 1.0, 0.6)

    def both(left, right):
        low = jnp.where(even, left, pltpu.roll(right, 127, 1))
        high = jnp.where(even, pltpu.roll(left, 127, 1), pltpu.roll(right, 126, 1))
        return [low[x : x + 1] for x in range(4)] + [high[x : x + 1] for x in range(4)]

    dh, kh, caph = both(cap_l * mine[2], cap_r * mine[5]), both(mine[3], mine[6]), both(cap_l, cap_r)
    for x in range(8):
        kh_out[x : x + 1] = kh[x]

    low, high = wall_terms()

    def x_chain(k, cap, d):
        s = list(cap)
        s[0] = s[0] + low
        s[7] = s[7] + high
        c = [R * jnp.minimum(k[x], k[x + 1]) for x in range(7)] + [None]
        g, q, levels, (p, z, t), tie = reduce_chain(c, s, d, True)
        return levels, tie, (k[0], k[7], z, t, g, p, q)

    base_z = lax.broadcasted_iota(jnp.int32, (8, 128), 0)
    for chunk in range(8):
        zi = base_z + 8 * chunk
        k, cap, d = [], [], []
        for x in range(8):
            k.append(cond[pl.ds(64 * chunk + x, 8, stride=8), :])
            cap.append(jnp.where(zi < subf[x : x + 1], 1.0, 0.6))
            dx = cap[x] * planes[pl.ds(64 * chunk + x, 8, stride=8), :]
            a2_out[pl.ds(64 * chunk + x, 8, stride=8), :] = dx
            d.append(dx)
        levels, tie, port = x_chain(k, cap, d)
        store_x(xfac.at[chunk], levels, tie)
        for i in range(2):
            xp[i, 8 * chunk : 8 * chunk + 8] = port[5 + i]
    levels, tie, port = x_chain(kh, caph, dh)
    store_x(xhfac, levels, tie)
    split_halves(xp, keep, send)
    for i in range(7):
        keep[64 + i : 65 + i] = port[i]
        send[64 + i : 65 + i] = port[i]


def store_x(ref, levels, tie):
    for lev, triple in enumerate(levels):
        base, n = node_order(4, lev)
        for kind in range(3):
            for j in range(n):
                if triple[kind][j] is not None:
                    ref[7 * kind + base + j] = triple[kind][j]
    for lev in range(3):
        ref[21 + lev] = tie[lev]


def load_x(ref):
    levels = get_levels(lambda kind, i: ref[7 * kind + i], 4)
    return levels, [ref[21 + lev] for lev in range(3)]


def read_pack(ref, n):
    main = tuple(ref[32 * i : 32 * i + 32] for i in range(n))
    edge = tuple(ref[32 * n + i : 32 * n + i + 1] for i in range(n))
    return main, edge


def write_pack(ref, main, edge):
    n = len(main)
    for i in range(n):
        ref[32 * i : 32 * i + 32] = main[i]
        ref[32 * n + i : 32 * n + i + 1] = edge[i]


def order(right, mine, theirs):
    a = tuple(jnp.where(right, t, m) for m, t in zip(mine, theirs))
    b = tuple(jnp.where(right, m, t) for m, t in zip(mine, theirs))
    return a, b


def planes_of(ref, n):
    return tuple(ref[32 * i : 32 * i + 32] for i in range(n))


def put_planes(ref, values):
    for i, v in enumerate(values):
        ref[32 * i : 32 * i + 32] = v


def spots():
    me_x = lax.axis_index("gx")
    return [lax.rem(lax.div(me_x, bit), 2) == 1 for bit in (1, 2, 4)]


def core_matrix_kernel(mine, theirs, merged_out, coef_out):
    odd, _, _ = spots()
    merged, coefs = port_coefs(*order(odd, planes_of(mine, 5), planes_of(theirs, 5)))
    put_planes(merged_out, merged)
    put_planes(coef_out, coefs)


def ring_matrix_kernel(own, mid, far, near, merged_out, mine_out, other_out, ring_out, top_out):
    _, right, upper = spots()
    packs = [planes_of(r, 5) for r in (own, near, mid, far)]
    mine, mine_c = port_coefs(*order(right, packs[0], packs[1]))
    other, other_c = port_coefs(*order(right, packs[2], packs[3]))
    merged, ring_c = port_coefs(*order(upper, mine, other))
    put_planes(merged_out, merged)
    put_planes(mine_out, mine_c)
    put_planes(other_out, other_c)
    put_planes(ring_out, ring_c)
    last = lax.div(lax.axis_index("gx"), 8) == 1
    kf, kl, z, tt, g = merged
    put_planes(top_out, (jnp.where(last, z + tt * (tt * recip(g)), g), jnp.where(last, kf, kl)))


def read_sides(ref):
    main = (ref[0:32], ref[32:64])
    edge = tuple(ref[64 + i : 65 + i] for i in range(7))
    return main, edge


def core_kernel(mine, theirs, coefs, merged_out, saved_out):
    odd, _, _ = spots()
    m, t = read_sides(mine), read_sides(theirs)
    values, saved = port_values(planes_of(coefs, 7), *order(odd, m[0], t[0]))
    edge, edge_saved = merge_ports(*order(odd, m[1], t[1]))
    put_planes(merged_out, values)
    for i in range(7):
        merged_out[64 + i : 65 + i] = edge[i]
    write_pack(saved_out, saved, edge_saved)


def ring_kernel(own, mid, far, near, matrix, mine_c, other_c, ring_c, merged_out, pair_out, saved_out, top_out):
    _, right, upper = spots()
    last = lax.div(lax.axis_index("gx"), 8) == 1
    main, edge = zip(*[read_sides(r) for r in (own, near, mid, far)])
    mine, pair = port_values(planes_of(mine_c, 7), *order(right, main[0], main[1]))
    other, _ = port_values(planes_of(other_c, 7), *order(right, main[2], main[3]))
    values, saved = port_values(planes_of(ring_c, 7), *order(upper, mine, other))
    e_mine, e_pair = merge_ports(*order(right, edge[0], edge[1]))
    e_other, _ = merge_ports(*order(right, edge[2], edge[3]))
    e_merged, e_saved = merge_ports(*order(upper, e_mine, e_other))
    outs = [planes_of(matrix, 5) + values, e_merged]
    write_pack(merged_out, *outs)
    kf, kl, z, tt, g, p, q = outs[0]
    top_out[0:32] = jnp.where(last, p + tt * recip(g) * q, q)
    kf, kl, z, tt, g, p, q = e_merged
    tg = tt * recip(g)
    for i, (a, b) in enumerate(((z + tt * tg, g), (p + tg * q, q), (kf, kl))):
        top_out[32 + i : 33 + i] = jnp.where(last, a, b)
    write_pack(pair_out, pair, e_pair)
    write_pack(saved_out, saved, e_saved)


def read_top(matrix, values):
    main = (matrix[0:32], values[0:32], matrix[32:64])
    return main, tuple(values[32 + i : 33 + i] for i in range(3))


def top_kernel(merged, near_m, near, theirs_m, theirs, sv1, sv2, sv3, own, send):
    me_x = lax.axis_index("gx")
    far = lax.div(me_x, 8) == 1
    mm = read_pack(merged, 7)
    n, t = read_top(near_m, near), read_top(theirs_m, theirs)
    saved = [read_pack(r, 6) for r in (sv1, sv2, sv3)]
    final = []
    for part in range(2):
        (ga, qa, ka), (zb, pb, kb) = order(far, n[part], t[part])
        link = R * jnp.minimum(ka, kb)
        lk = link * recip(1.0 + link * zb)
        u_a = (qa + lk * pb) * recip(ga + lk)
        kf, kl, z, tt, g, p, q = mm[part]
        flux = jnp.where(far, lk * (u_a - pb), 0.0)
        u = jnp.where(far, (q + tt * flux) * recip(g), u_a)
        for bit, lev in ((4, 2), (2, 1)):
            right = lax.rem(lax.div(me_x, bit), 2) == 1
            ua, fb = descend(saved[lev][part], flux, u)
            flux = jnp.where(right, fb, flux)
            u = jnp.where(right, u, ua)
        ua, fb = descend(saved[0][part], flux, u)
        odd = lax.rem(me_x, 2) == 1
        final.append((jnp.where(odd, fb, flux), jnp.where(odd, u, ua), jnp.where(odd, flux, fb), jnp.where(odd, ua, u)))
    write_pack(own, final[0][:2], final[1][:2])
    send[0:32] = final[0][2]
    send[32:64] = final[0][3]


def coef_kernel(cond, kh, a2, cot, sub, dep, cls, k_y, k_l, k_z, k_s, base):
    me_y = lax.axis_index("gy")
    sub_v, dep_v, kh_v = sub[...], dep[...], kh[...]
    top = film_top(cls[...])
    lane = lax.broadcasted_iota(jnp.int32, (8, 128), 1)
    first, final = lane == 0, lane == 127
    film_y = jnp.where(first & (me_y == 0), SIDE, 0.0) + jnp.where(final & (me_y == 7), SIDE, 0.0)
    for z in range(64):
        rows = slice(8 * z, 8 * z + 8)
        k = cond[rows]
        k_h = pltpu.roll(kh_v, 128 - 2 * z, 1) if z else kh_v
        k_y[rows] = (2.0 * R) * jnp.minimum(k, jnp.where(final, k_h, pltpu.roll(k, 127, 1)))
        k_l[rows] = (2.0 * R) * jnp.minimum(k, k_h)
        if z < 63:
            k_z[rows] = (2.0 * R) * jnp.minimum(k, cond[8 * z + 8 : 8 * z + 16])
        film = film_y + top * (dep_v - 1 == z).astype(F32)
        if z == 0:
            film = film + BOTTOM
        k_s[rows] = 2.0 * jnp.where(z < sub_v, 1.0, 0.6) - (2.0 * R) * film
        base[rows] = cot[rows] - 2.0 * a2[rows]


def last_kernel(
    own, got, xfac, xhfac, k_y, k_l, k_z, k_s, base, sub, temp_out, src_out, s1, fu, t_buf, s_buf, sems
):
    core = own_half()
    for i in range(2):
        fu[i, pl.ds(pl.multiple_of(32 * core, 32), 32), :] = own[32 * i : 32 * i + 32]
        fu[i, pl.ds(pl.multiple_of(32 - 32 * core, 32), 32), :] = got[32 * i : 32 * i + 32]
    levels, tie = load_x(xhfac)
    uh = jnp.concatenate(expand_chain(own[65:66], levels, tie, own[64:65]), axis=0)
    sub_v = sub[...]
    lane = lax.broadcasted_iota(jnp.int32, (8, 128), 1)
    first, final = lane == 0, lane == 127
    up, copies = None, []

    def expand(chunk):
        rows = slice(8 * chunk, 8 * chunk + 8)
        levels, tie = load_x(xfac.at[chunk])
        u = expand_chain(fu[1, rows], levels, tie, fu[0, rows])
        for x in range(8):
            s1[pl.ds(64 * chunk + x, 8, stride=8), :] = u[x]

    expand(0)
    for z in range(64):
        if z & 7 == 0 and z < 56:
            expand(z // 8 + 1)
        rows = slice(8 * z, 8 * z + 8)
        s = s1[rows]
        s_h = pltpu.roll(uh, 128 - 2 * z, 1) if z else uh
        f_y = k_y[rows] * (jnp.where(final, s_h, pltpu.roll(s, 127, 1)) - s)
        f_l = k_l[rows] * (s - s_h)
        total = f_y - jnp.where(first, f_l, pltpu.roll(f_y, 1, 1))
        if z < 63:
            f_z = k_z[rows] * (s1[8 * z + 8 : 8 * z + 16] - s)
            total = total + f_z
        if z:
            total = total - up
        up = f_z
        s_buf[rows] = jnp.where(z < sub_v, 1.0, 0.6) * s
        t_buf[rows] = base[rows] + k_s[rows] * s + total
        if z & 7 == 7:
            part = slice(8 * z - 56, 8 * z + 8)
            for i, (buf, out) in enumerate(((s_buf, src_out), (t_buf, temp_out))):
                cp = pltpu.make_async_copy(buf.at[part], out.at[part], sems.at[2 * (z // 8) + i])
                cp.start()
                copies.append(cp)
    for cp in copies:
        cp.wait()


VMEM = pl.BlockSpec(memory_space=pltpu.VMEM)
HBM = pl.BlockSpec(memory_space=pltpu.MemorySpace.HBM)


def call(kernel, outs, scratch, name, *args, far_in=0, far_out=0, sems=0):
    shapes = [s if isinstance(s, jax.ShapeDtypeStruct) else jax.ShapeDtypeStruct(s, F32) for s in outs]
    scr = [pltpu.VMEM(s, F32) for s in scratch]
    args = [pltpu.with_memory_space_constraint(a, pltpu.MemorySpace.HBM) if i < far_in else a for i, a in enumerate(args)]
    if sems:
        scr.append(pltpu.SemaphoreType.DMA((sems,)))
    return pl.pallas_call(
        kernel,
        out_shape=shapes,
        in_specs=[HBM if i < far_in else VMEM for i in range(len(args))],
        out_specs=[HBM if i < far_out else VMEM for i in range(len(outs))],
        scratch_shapes=scr,
        compiler_params=pltpu.CompilerParams(vmem_limit_bytes=40 * 1024 * 1024),
        name=name,
    )(*args)


def swap(v, bit):
    return lax.ppermute(v, "gx", [(i, i ^ bit) for i in range(16)])


def body(cotangent, saved_temp, substrate_top, deposit_top, top_class):
    cot = cotangent.reshape(512, 128)
    temp = saved_temp.reshape(512, 128)
    small = jax.ShapeDtypeStruct((8, 128), jnp.int32)
    cond, keep_m, send_m, cot, sub, dep, cls = call(
        fields_kernel,
        [(512, 128), (160, 128), (160, 128), (512, 128), small, small, small],
        [(512, 128), (5, 64, 128)],
        "fields",
        cot, temp, substrate_top, deposit_top, top_class,
        far_in=5, sems=8,
    )
    other_m = swap(send_m, 1)
    ypack, fac, ties = call(
        first_kernel,
        [(8, 32, 128), (3, 63, 8, 128), (12, 8, 128)],
        [(3, 512, 128), (512, 128)],
        "first",
        cot, sub, dep, cls, cond,
    )
    mm, core_c = call(core_matrix_kernel, [(160, 128), (224, 128)], [], "matrix_core", keep_m, other_m)
    mm, ypack = lax.optimization_barrier((mm, ypack))
    gat = lax.all_to_all(ypack, "gy", split_axis=0, concat_axis=0, tiled=True)
    ring_m = [swap(mm, bit) for bit in (4, 7, 3)]
    keep, send, xfac, xhfac, a2, kh = call(
        second_kernel,
        [(72, 128), (72, 128), (8, 24, 8, 128), (24, 1, 128), (512, 128), (8, 128)],
        [(8, 32, 128), (512, 128), (512, 128), (2, 64, 128)],
        "second",
        gat, fac, ties, cond, sub,
    )
    m1, sv1 = call(core_kernel, [(72, 128), (200, 128)], [], "merge_core", keep, swap(send, 1), core_c)
    ring_v = [swap(m1, bit) for bit in (4, 7, 3)]
    matrix, mine_c, other_c, ring_c, near_m = call(
        ring_matrix_kernel, [(160, 128)] + [(224, 128)] * 3 + [(64, 128)], [], "matrix_ring", mm, *ring_m
    )
    opposite_m = swap(near_m, 9)
    m3, sv2, sv3, near = call(
        ring_kernel,
        [(232, 128), (200, 128), (200, 128), (40, 128)],
        [],
        "merge_ring",
        m1, *ring_v, matrix, mine_c, other_c, ring_c,
    )
    sv3, kh = lax.optimization_barrier((sv3, kh))
    coefs = call(coef_kernel, [(512, 128)] * 5, [], "coef", cond, kh, a2, cot, sub, dep, cls)
    opposite = swap(near, 9)
    sv3, coefs = lax.optimization_barrier((sv3, coefs))
    own, out = call(top_kernel, [(72, 128), (64, 128)], [], "top", m3, near_m, near, opposite_m, opposite, sv1, sv2, sv3)
    got = swap(out, 1)
    grad_temp, grad_source = call(
        last_kernel,
        [(512, 128), (512, 128)],
        [(512, 128), (2, 64, 128), (512, 128), (512, 128)],
        "last",
        own, got, xfac, xhfac, *coefs, sub,
        far_out=2, sems=16,
    )
    return grad_temp.reshape(cotangent.shape), grad_source.reshape(cotangent.shape)


def solution(mesh):
    in_specs = (
        P(None, "gx", "gy"),
        P(None, "gx", "gy"),
        P("gx", "gy"),
        P("gx", "gy"),
        P("gx", "gy"),
    )
    out_specs = (P(None, "gx", "gy"), P(None, "gx", "gy"))
    return jax.shard_map(body, mesh=mesh, in_specs=in_specs, out_specs=out_specs, check_vma=False)
```

```python
import jax
import jax.numpy as jnp
from jax import lax
from jax.experimental import pallas as pl
from jax.experimental.pallas import tpu as pltpu
from jax.sharding import PartitionSpec as P

R = 1000.0
SIDE = 0.3
BOTTOM = 0.5
TOPS = (0.05, 0.25, 0.8, 2.0)
F32 = jnp.float32
NLEV = 6


def recip(v):
    return 1.0 / v


def reduce_chain(c, s, d, track):
    levels, port, ties = [], None, []
    while len(s) > 1:
        half = len(s) // 2
        ml, mr, dv = [], [], []
        for j in range(half):
            i = 2 * j
            total = s[i] + c[i]
            if j:
                total = total + c[i - 1]
            inv = recip(total)
            mr.append(c[i] * inv)
            ml.append(c[i - 1] * inv if j else None)
            dv.append(d[i] * inv)
            if track and j == 0:
                if port is None:
                    port = [dv[0], inv, mr[0]]
                    ties.append(inv)
                else:
                    p, z, t = port
                    tie = t * inv
                    ties.append(tie)
                    port = [p + t * dv[0], z + t * tie, t * mr[0]]
        ns, nd, nc = [], [], []
        for j in range(half):
            e, o = 2 * j, 2 * j + 1
            sv = s[o] + mr[j] * s[e]
            dn = d[o] + mr[j] * d[e]
            if j + 1 < half:
                sv = sv + ml[j + 1] * s[e + 2]
                dn = dn + ml[j + 1] * d[e + 2]
                nc.append(ml[j + 1] * c[e + 2])
            ns.append(sv)
            nd.append(dn)
        levels.append((dv, ml, mr))
        c, s, d = nc, ns, nd
    return s[0], d[0], levels, port, ties


def expand_chain(u_last, levels, ties, flux):
    u = [u_last]
    for lev in range(len(levels) - 1, -1, -1):
        dv, ml, mr = levels[lev]
        out = []
        for j in range(len(u)):
            even = dv[j] + mr[j] * u[j]
            if j:
                even = even + ml[j] * u[j - 1]
            elif ties is not None:
                even = even + ties[lev] * flux
            out += [even, u[j]]
        u = out
    return u


def port_coefs(a, b):
    kfa, kla, za, ta, ga = a
    kfb, klb, zb, tb, gb = b
    link = R * jnp.minimum(kla, kfb)
    lk = link * recip(1.0 + link * zb)
    inv = recip(ga + lk)
    ti = ta * inv
    lt = lk * tb
    w = lt * inv
    merged = (kfa, klb, za + ta * ti, ta * w, gb + lt * tb * (ga * inv))
    return merged, (inv, lk, ta, lt, ti, w, tb)


def port_values(coefs, a, b):
    inv, lk, ta, lt, ti, w, tb = coefs
    pa, qa = a
    pb, qb = b
    h = inv * (qa + lk * pb)
    return (pa + ta * h, qb + lt * (h - pb)), (h, ti, w, lk, pb, tb)


def merge_ports(a, b):
    matrix, coefs = port_coefs(a[:5], b[:5])
    values, saved = port_values(coefs, a[5:], b[5:])
    return matrix + values, saved


def descend(saved, flux, u_b):
    h, ti, w, lk, pb, tb = saved
    u_a = h + ti * flux + w * u_b
    flux_b = lk * (u_a - pb - tb * u_b)
    return u_a, flux_b


def film_top(cls):
    total = jnp.zeros(cls.shape, F32)
    for n in range(4):
        total = total + TOPS[n] * (cls == n).astype(F32)
    return total


def node_order(half, lev):
    base, n = 0, half
    for _ in range(lev):
        base += n
        n //= 2
    return base, n


def put_levels(ref, levels):
    half = len(levels[0][0])
    for lev, triple in enumerate(levels):
        base, n = node_order(half, lev)
        for kind in range(3):
            for j in range(n):
                if triple[kind][j] is not None:
                    ref[kind, base + j] = triple[kind][j]


def get_levels(read, half):
    levels, lev = [], 0
    while half >> lev:
        base, n = node_order(half, lev)
        levels.append(
            tuple([None if kind == 1 and j == 0 else read(kind, base + j) for j in range(n)] for kind in range(3))
        )
        lev += 1
    return levels


def chain_matrix(c, s):
    z = t = None
    while len(s) > 1:
        half = len(s) // 2
        ml, mr = [None] * half, [None] * half
        for j in range(half):
            i = 2 * j
            inv = recip(s[i] + c[i] + c[i - 1] if j else s[i] + c[i])
            mr[j] = c[i] * inv
            if j:
                ml[j] = c[i - 1] * inv
            elif z is None:
                z, t = inv, mr[0]
            else:
                z, t = z + t * (t * inv), t * mr[0]
        ns, nc = [], []
        for j in range(half):
            e = 2 * j
            sv = s[e + 1] + mr[j] * s[e]
            if j + 1 < half:
                sv = sv + ml[j + 1] * s[e + 2]
                nc.append(ml[j + 1] * c[e + 2])
            ns.append(sv)
        c, s = nc, ns
    return z, t, s[0]


def wall_terms():
    me_x = lax.axis_index("gx")
    return jnp.where(me_x == 0, R * SIDE, 0.0), jnp.where(me_x == 15, R * SIDE, 0.0)


def own_half():
    me_x = lax.axis_index("gx")
    return lax.rem(me_x + lax.div(me_x, 2) + lax.div(me_x, 8), 2)


def split_halves(planes, keep, send):
    core = own_half()
    for i in range(planes.shape[0]):
        keep[32 * i : 32 * i + 32] = planes[i, pl.ds(pl.multiple_of(32 * core, 32), 32), :]
        send[32 * i : 32 * i + 32] = planes[i, pl.ds(pl.multiple_of(32 - 32 * core, 32), 32), :]


def fields_kernel(cot_in, temp_in, sub_in, dep_in, cls_in, cond, keep, send, cot, sub, dep, cls, temp, planes, sems):
    pieces = [slice(128 * i, 128 * i + 128) for i in range(4)]
    pairs = [(sub_in, sub), (dep_in, dep)] + [(temp_in.at[r], temp.at[r]) for r in pieces]
    pairs += [(cls_in, cls), (cot_in, cot)]
    copies = [pltpu.make_async_copy(a, b, sems.at[i]) for i, (a, b) in enumerate(pairs)]
    for cp in copies:
        cp.start()
    for cp in copies[:2]:
        cp.wait()
    sub_v, dep_v = sub[...], dep[...]
    for z in range(64):
        if z % 16 == 0:
            copies[2 + z // 16].wait()
        base = jnp.where(z < sub_v, 1.0, 0.45)
        sg = 0.5 + jax.nn.sigmoid(temp[8 * z : 8 * z + 8])
        cond[8 * z : 8 * z + 8] = jnp.where(z < dep_v, base * sg, 0.0)
    low, high = wall_terms()
    base_z = lax.broadcasted_iota(jnp.int32, (8, 128), 0)
    for chunk in range(8):
        zi = base_z + 8 * chunk
        k = [cond[pl.ds(64 * chunk + x, 8, stride=8), :] for x in range(8)]
        s = [jnp.where(zi < sub_v[x : x + 1], 1.0, 0.6) for x in range(8)]
        s[0] = s[0] + low
        s[7] = s[7] + high
        c = [R * jnp.minimum(k[x], k[x + 1]) for x in range(7)] + [None]
        for i, v in enumerate((k[0], k[7]) + chain_matrix(c, s)):
            planes[i, 8 * chunk : 8 * chunk + 8] = v
    split_halves(planes, keep, send)
    for cp in copies[6:]:
        cp.wait()


def first_kernel(cot, sub, dep, cls, cond, ypack, fac, tie_out, mid, tr):
    me_y = lax.axis_index("gy")
    sub_v, dep_v = sub[...], dep[...]
    top = film_top(cls[...])
    k, cap, s = [], [], []
    for z in range(64):
        k.append(cond[8 * z : 8 * z + 8])
        cap.append(jnp.where(z < sub_v, 1.0, 0.6))
        film = top * (dep_v - 1 == z).astype(F32)
        if z == 0:
            film = film + BOTTOM
        s.append(cap[z] + R * film)
    c = [R * jnp.minimum(k[z], k[z + 1]) for z in range(63)] + [None]
    d = [cot[8 * z : 8 * z + 8] for z in range(64)]
    g, q, levels, _, _ = reduce_chain(c, s, d, False)
    u = expand_chain(q * recip(g), levels, None, None)
    for z in range(64):
        tr[8 * z : 8 * z + 8] = cap[z] * u[z]

    def turned(rows, dst, q):
        block = jnp.transpose(rows)
        for h in range(2):
            dst[pl.ds(4 * h + q, 64, stride=8), :] = block[64 * h : 64 * h + 64]

    subf = sub_v.astype(F32)
    upper = (lax.broadcasted_iota(jnp.int32, (128, 128), 0) & 1) == 1
    for q in range(4):
        turned(cond[pl.ds(q, 128, stride=4), :], mid.at[0], q)
        turned(tr[pl.ds(q, 128, stride=4), :], mid.at[1], q)
        turned(jnp.where(upper, subf[q + 4 : q + 5], subf[q : q + 1]), mid.at[2], q)
    z_lane = (lax.broadcasted_iota(jnp.int32, (8, 128), 1) >> 1).astype(F32)
    row = lax.broadcasted_iota(jnp.int32, (8, 128), 0)
    ky, sy, dy = [], [], []
    for y in range(64):
        ky.append(mid[0, 8 * y : 8 * y + 8])
        dy.append(mid[1, 8 * y : 8 * y + 8])
        sy.append(jnp.where(z_lane < mid[2, 8 * y : 8 * y + 8], 1.0, 0.6))
    low = jnp.where(me_y == 0, R * SIDE, 0.0)
    high = jnp.where(me_y == 7, R * SIDE, 0.0)
    sy[0] = sy[0] + jnp.where(row < 4, low, 0.0)
    sy[63] = sy[63] + jnp.where(row >= 4, high, 0.0)
    cy = [R * jnp.minimum(ky[y], ky[y + 1]) for y in range(63)] + [None]
    g, q, levels, (p, zz, t), ties = reduce_chain(cy, sy, dy, True)
    put_levels(fac, levels)
    for lev in range(NLEV):
        tie_out[lev] = ties[lev]
    kf, kl = ky[0], ky[63]
    side_a = tuple(v[0:4] for v in (kf, kl, zz, t, g, p, q))
    side_b = tuple(v[4:8] for v in (kf, kl, zz, t, g, p, q))
    merged, saved = merge_ports(side_a, side_b)
    for i, v in enumerate(saved):
        tie_out[NLEV + i, 0:4] = v
    lower = lax.broadcasted_iota(jnp.int32, (4, 128), 1) < 64
    edges = jnp.where(lower, mid[2, 0:4], mid[2, 508:512])
    pack = jnp.concatenate(list(merged) + [edges], axis=0)
    for n in range(8):
        ypack[n] = pack


def second_kernel(gat, fac, ties, cond, sub, keep, send, xfac, xhfac, a2_out, kh_out, pick, flat, planes, xp):
    me_y = lax.axis_index("gy")
    seg = [[gat[n, 4 * i : 4 * i + 4] for i in range(8)] for n in range(8)]
    gam, rhs = seg[0][4], seg[0][6]
    down, links = [None], [None]
    for n in range(1, 8):
        kf, kl, z, t, g, p, q = seg[n][:7]
        link = R * jnp.minimum(seg[n - 1][1], kf)
        lk = link * recip(1.0 + link * z)
        inv = recip(gam + lk)
        h = inv * (rhs + lk * p)
        lt = lk * t
        down.append((h, lt * inv))
        links.append(lk)
        rhs = q + lt * (h - p)
        gam = g + lt * t * (gam * inv)
    u = [None] * 8
    u[7] = rhs * recip(gam)
    for n in range(7, 0, -1):
        u[n - 1] = down[n][0] + down[n][1] * u[n]
    zero4 = jnp.zeros((4, 128), F32)
    fl, uf = [zero4], [None]
    for n in range(1, 8):
        kf, kl, z, t, g, p, q = seg[n][:7]
        fl.append(links[n] * (u[n - 1] - p - t * u[n]))
        uf.append(p + z * fl[n] + t * u[n])
    for n in range(8):
        rows = [fl[n], u[n]]
        if n:
            rows += [u[n - 1], seg[n - 1][1], seg[n - 1][7]]
        else:
            rows += [zero4, zero4, zero4]
        if n < 7:
            rows += [uf[n + 1], seg[n + 1][0], seg[n + 1][7]]
        else:
            rows += [zero4, zero4, zero4]
        for i, v in enumerate(rows):
            pick[n, 4 * i : 4 * i + 4] = v
    mine = [pick[me_y, 4 * i : 4 * i + 4] for i in range(8)]
    flux, u_b = mine[0], mine[1]
    saved = tuple(ties[NLEV + i, 0:4] for i in range(6))
    u_a, flux_b = descend(saved, flux, u_b)
    flux8 = jnp.concatenate([flux, flux_b], axis=0)
    last8 = jnp.concatenate([u_a, u_b], axis=0)
    levels = get_levels(lambda kind, i: fac[kind, i], 32)
    u_nodes = expand_chain(last8, levels, [ties[i] for i in range(NLEV)], flux8)
    for y in range(64):
        flat[8 * y : 8 * y + 8] = u_nodes[y]
    subf = sub[...]
    for q in range(4):
        planes[pl.ds(q, 128, stride=4), :] = jnp.transpose(
            jnp.concatenate([flat[pl.ds(q, 64, stride=8), :], flat[pl.ds(4 + q, 64, stride=8), :]], axis=0)
        )

    lane = lax.broadcasted_iota(jnp.int32, (4, 128), 1)
    even = (lane & 1) == 0
    z_of = (lane >> 1).astype(F32)
    cap_l = jnp.where(z_of < jnp.where(lane < 64, pltpu.roll(mine[4], 64, 1), mine[4]), 1.0, 0.6)
    cap_r = jnp.where(z_of < jnp.where(lane < 64, mine[7], pltpu.roll(mine[7], 64, 1)), 1.0, 0.6)

    def both(left, right):
        low = jnp.where(even, left, pltpu.roll(right, 127, 1))
        high = jnp.where(even, pltpu.roll(left, 127, 1), pltpu.roll(right, 126, 1))
        return [low[x : x + 1] for x in range(4)] + [high[x : x + 1] for x in range(4)]

    dh, kh, caph = both(cap_l * mine[2], cap_r * mine[5]), both(mine[3], mine[6]), both(cap_l, cap_r)
    for x in range(8):
        kh_out[x : x + 1] = kh[x]

    low, high = wall_terms()

    def x_chain(k, cap, d):
        s = list(cap)
        s[0] = s[0] + low
        s[7] = s[7] + high
        c = [R * jnp.minimum(k[x], k[x + 1]) for x in range(7)] + [None]
        g, q, levels, (p, z, t), tie = reduce_chain(c, s, d, True)
        return levels, tie, (k[0], k[7], z, t, g, p, q)

    base_z = lax.broadcasted_iota(jnp.int32, (8, 128), 0)
    for chunk in range(8):
        zi = base_z + 8 * chunk
        k, cap, d = [], [], []
        for x in range(8):
            k.append(cond[pl.ds(64 * chunk + x, 8, stride=8), :])
            cap.append(jnp.where(zi < subf[x : x + 1], 1.0, 0.6))
            dx = cap[x] * planes[pl.ds(64 * chunk + x, 8, stride=8), :]
            a2_out[pl.ds(64 * chunk + x, 8, stride=8), :] = dx
            d.append(dx)
        levels, tie, port = x_chain(k, cap, d)
        store_x(xfac.at[chunk], levels, tie)
        for i in range(2):
            xp[i, 8 * chunk : 8 * chunk + 8] = port[5 + i]
    levels, tie, port = x_chain(kh, caph, dh)
    store_x(xhfac, levels, tie)
    split_halves(xp, keep, send)
    for i in range(7):
        keep[64 + i : 65 + i] = port[i]
        send[64 + i : 65 + i] = port[i]


def store_x(ref, levels, tie):
    for lev, triple in enumerate(levels):
        base, n = node_order(4, lev)
        for kind in range(3):
            for j in range(n):
                if triple[kind][j] is not None:
                    ref[7 * kind + base + j] = triple[kind][j]
    for lev in range(3):
        ref[21 + lev] = tie[lev]


def load_x(ref):
    levels = get_levels(lambda kind, i: ref[7 * kind + i], 4)
    return levels, [ref[21 + lev] for lev in range(3)]


def read_pack(ref, n):
    main = tuple(ref[32 * i : 32 * i + 32] for i in range(n))
    edge = tuple(ref[32 * n + i : 32 * n + i + 1] for i in range(n))
    return main, edge


def write_pack(ref, main, edge):
    n = len(main)
    for i in range(n):
        ref[32 * i : 32 * i + 32] = main[i]
        ref[32 * n + i : 32 * n + i + 1] = edge[i]


def order(right, mine, theirs):
    a = tuple(jnp.where(right, t, m) for m, t in zip(mine, theirs))
    b = tuple(jnp.where(right, m, t) for m, t in zip(mine, theirs))
    return a, b


def planes_of(ref, n):
    return tuple(ref[32 * i : 32 * i + 32] for i in range(n))


def put_planes(ref, values):
    for i, v in enumerate(values):
        ref[32 * i : 32 * i + 32] = v


def spots():
    me_x = lax.axis_index("gx")
    return [lax.rem(lax.div(me_x, bit), 2) == 1 for bit in (1, 2, 4)]


def core_matrix_kernel(mine, theirs, merged_out, coef_out):
    odd, _, _ = spots()
    merged, coefs = port_coefs(*order(odd, planes_of(mine, 5), planes_of(theirs, 5)))
    put_planes(merged_out, merged)
    put_planes(coef_out, coefs)


def ring_matrix_kernel(own, mid, far, near, merged_out, mine_out, other_out, ring_out, top_out):
    _, right, upper = spots()
    packs = [planes_of(r, 5) for r in (own, near, mid, far)]
    mine, mine_c = port_coefs(*order(right, packs[0], packs[1]))
    other, other_c = port_coefs(*order(right, packs[2], packs[3]))
    merged, ring_c = port_coefs(*order(upper, mine, other))
    put_planes(merged_out, merged)
    put_planes(mine_out, mine_c)
    put_planes(other_out, other_c)
    put_planes(ring_out, ring_c)
    last = lax.div(lax.axis_index("gx"), 8) == 1
    kf, kl, z, tt, g = merged
    put_planes(top_out, (jnp.where(last, z + tt * (tt * recip(g)), g), jnp.where(last, kf, kl)))


def read_sides(ref):
    main = (ref[0:32], ref[32:64])
    edge = tuple(ref[64 + i : 65 + i] for i in range(7))
    return main, edge


def core_kernel(mine, theirs, coefs, merged_out, saved_out):
    odd, _, _ = spots()
    m, t = read_sides(mine), read_sides(theirs)
    values, saved = port_values(planes_of(coefs, 7), *order(odd, m[0], t[0]))
    edge, edge_saved = merge_ports(*order(odd, m[1], t[1]))
    put_planes(merged_out, values)
    for i in range(7):
        merged_out[64 + i : 65 + i] = edge[i]
    write_pack(saved_out, saved, edge_saved)


def ring_kernel(own, mid, far, near, matrix, mine_c, other_c, ring_c, merged_out, pair_out, saved_out, top_out):
    _, right, upper = spots()
    last = lax.div(lax.axis_index("gx"), 8) == 1
    main, edge = zip(*[read_sides(r) for r in (own, near, mid, far)])
    mine, pair = port_values(planes_of(mine_c, 7), *order(right, main[0], main[1]))
    other, _ = port_values(planes_of(other_c, 7), *order(right, main[2], main[3]))
    values, saved = port_values(planes_of(ring_c, 7), *order(upper, mine, other))
    e_mine, e_pair = merge_ports(*order(right, edge[0], edge[1]))
    e_other, _ = merge_ports(*order(right, edge[2], edge[3]))
    e_merged, e_saved = merge_ports(*order(upper, e_mine, e_other))
    outs = [planes_of(matrix, 5) + values, e_merged]
    write_pack(merged_out, *outs)
    kf, kl, z, tt, g, p, q = outs[0]
    top_out[0:32] = jnp.where(last, p + tt * recip(g) * q, q)
    kf, kl, z, tt, g, p, q = e_merged
    tg = tt * recip(g)
    for i, (a, b) in enumerate(((z + tt * tg, g), (p + tg * q, q), (kf, kl))):
        top_out[32 + i : 33 + i] = jnp.where(last, a, b)
    write_pack(pair_out, pair, e_pair)
    write_pack(saved_out, saved, e_saved)


def read_top(matrix, values):
    main = (matrix[0:32], values[0:32], matrix[32:64])
    return main, tuple(values[32 + i : 33 + i] for i in range(3))


def top_kernel(merged, near_m, near, theirs_m, theirs, sv1, sv2, sv3, own, send):
    me_x = lax.axis_index("gx")
    far = lax.div(me_x, 8) == 1
    mm = read_pack(merged, 7)
    n, t = read_top(near_m, near), read_top(theirs_m, theirs)
    saved = [read_pack(r, 6) for r in (sv1, sv2, sv3)]
    final = []
    for part in range(2):
        (ga, qa, ka), (zb, pb, kb) = order(far, n[part], t[part])
        link = R * jnp.minimum(ka, kb)
        lk = link * recip(1.0 + link * zb)
        u_a = (qa + lk * pb) * recip(ga + lk)
        kf, kl, z, tt, g, p, q = mm[part]
        flux = jnp.where(far, lk * (u_a - pb), 0.0)
        u = jnp.where(far, (q + tt * flux) * recip(g), u_a)
        for bit, lev in ((4, 2), (2, 1)):
            right = lax.rem(lax.div(me_x, bit), 2) == 1
            ua, fb = descend(saved[lev][part], flux, u)
            flux = jnp.where(right, fb, flux)
            u = jnp.where(right, u, ua)
        ua, fb = descend(saved[0][part], flux, u)
        odd = lax.rem(me_x, 2) == 1
        final.append((jnp.where(odd, fb, flux), jnp.where(odd, u, ua), jnp.where(odd, flux, fb), jnp.where(odd, ua, u)))
    write_pack(own, final[0][:2], final[1][:2])
    send[0:32] = final[0][2]
    send[32:64] = final[0][3]


def coef_kernel(cond, kh, a2, cot, sub, dep, cls, k_y, k_l, k_z, k_s, base):
    me_y = lax.axis_index("gy")
    sub_v, dep_v, kh_v = sub[...], dep[...], kh[...]
    top = film_top(cls[...])
    lane = lax.broadcasted_iota(jnp.int32, (8, 128), 1)
    first, final = lane == 0, lane == 127
    film_y = jnp.where(first & (me_y == 0), SIDE, 0.0) + jnp.where(final & (me_y == 7), SIDE, 0.0)
    for z in range(64):
        rows = slice(8 * z, 8 * z + 8)
        k = cond[rows]
        k_h = pltpu.roll(kh_v, 128 - 2 * z, 1) if z else kh_v
        k_y[rows] = (2.0 * R) * jnp.minimum(k, jnp.where(final, k_h, pltpu.roll(k, 127, 1)))
        k_l[rows] = (2.0 * R) * jnp.minimum(k, k_h)
        if z < 63:
            k_z[rows] = (2.0 * R) * jnp.minimum(k, cond[8 * z + 8 : 8 * z + 16])
        else:
            k_z[rows] = jnp.zeros((8, 128), F32)
        film = film_y + top * (dep_v - 1 == z).astype(F32)
        if z == 0:
            film = film + BOTTOM
        k_s[rows] = 2.0 * jnp.where(z < sub_v, 1.0, 0.6) - (2.0 * R) * film
        base[rows] = cot[rows] - 2.0 * a2[rows]


def expand_rows(xfac, half, flux, last, s1):
    for chunk in range(4):
        rows = slice(8 * chunk, 8 * chunk + 8)
        levels, tie = load_x(xfac.at[4 * half + chunk])
        u = expand_chain(last[rows], levels, tie, flux[rows])
        for x in range(8):
            s1[pl.ds(64 * chunk + x, 8, stride=8), :] = u[x]


def stencil(half, uh, s1, k_y, k_l, k_z, k_s, base, sub_v, below, above, src, out, done=None):
    lane = lax.broadcasted_iota(jnp.int32, (8, 128), 1)
    first, final = lane == 0, lane == 127
    up = below
    for i in range(32):
        rows = slice(8 * i, 8 * i + 8)
        at = pl.ds(pl.multiple_of(256 * half + 8 * i, 8), 8)
        s = s1[rows]
        s_h = pltpu.roll(uh, 128 - 2 * i, 1) if i else uh
        f_y = k_y[at, :] * (jnp.where(final, s_h, pltpu.roll(s, 127, 1)) - s)
        f_l = k_l[at, :] * (s - s_h)
        total = f_y - jnp.where(first, f_l, pltpu.roll(f_y, 1, 1))
        f_z = k_z[at, :] * (s1[8 * i + 8 : 8 * i + 16] - s) if i < 31 else above
        if f_z is not None:
            total = total + f_z
        if up is not None:
            total = total - up
        up = f_z
        src[rows] = jnp.where(32 * half + i < sub_v, 1.0, 0.6) * s
        out[rows] = base[at, :] + k_s[at, :] * s + total
        if done is not None and i & 7 == 7:
            done(i // 8)


def own_kernel(own, xfac, xhfac, k_y, k_l, k_z, k_s, base, sub, s1, src, out, uh_out):
    half = own_half()
    levels, tie = load_x(xhfac)
    uh = jnp.concatenate(expand_chain(own[65:66], levels, tie, own[64:65]), axis=0)
    turned = pltpu.roll(uh, 64, 1)
    uh_out[...] = jnp.where(half == 1, uh, turned)
    expand_rows(xfac, half, own.at[0:32], own.at[32:64], s1)
    uh = jnp.where(half == 1, turned, uh)
    stencil(half, uh, s1, k_y, k_l, k_z, k_s, base, sub[...], None, None, src, out)


def last_kernel(
    got, xfac, k_y, k_l, k_z, k_s, base, sub, s_own, src_own, out_own, uh, temp_out, src_out, s1, ends, t_buf, s_buf, sems
):
    mine = own_half()
    half = 1 - mine
    copies = []

    def send(buf, rows, out, start):
        size = rows.stop - rows.start
        cp = pltpu.make_async_copy(buf.at[rows], out.at[pl.ds(pl.multiple_of(start, 8), size)], sems.at[len(copies)])
        cp.start()
        copies.append(cp)

    send(src_own, slice(0, 256), src_out, 256 * mine)
    send(out_own, slice(8, 248), temp_out, 256 * mine + 8)
    expand_rows(xfac, half, got.at[0:32], got.at[32:64], s1)
    inner, outer = s_own[248:256], s_own[0:8]
    low = jnp.where(half == 0, s1[248:256], inner)
    high = jnp.where(half == 0, outer, s1[0:8])
    flux = k_z[248:256] * (high - low)
    ends[0:8] = out_own[0:8] - jnp.where(mine == 1, flux, 0.0)
    ends[8:16] = out_own[248:256] + jnp.where(mine == 0, flux, 0.0)
    send(ends, slice(0, 8), temp_out, 256 * mine)
    send(ends, slice(8, 16), temp_out, 256 * mine + 248)

    def done(piece):
        rows = slice(64 * piece, 64 * piece + 64)
        send(s_buf, rows, src_out, 256 * half + 64 * piece)
        send(t_buf, rows, temp_out, 256 * half + 64 * piece)

    below, above = jnp.where(half == 1, flux, 0.0), jnp.where(half == 0, flux, 0.0)
    stencil(half, uh[...], s1, k_y, k_l, k_z, k_s, base, sub[...], below, above, s_buf, t_buf, done)
    for cp in copies:
        cp.wait()


VMEM = pl.BlockSpec(memory_space=pltpu.VMEM)
HBM = pl.BlockSpec(memory_space=pltpu.MemorySpace.HBM)


def call(kernel, outs, scratch, name, *args, far_in=0, far_out=0, sems=0):
    shapes = [s if isinstance(s, jax.ShapeDtypeStruct) else jax.ShapeDtypeStruct(s, F32) for s in outs]
    scr = [pltpu.VMEM(s, F32) for s in scratch]
    args = [pltpu.with_memory_space_constraint(a, pltpu.MemorySpace.HBM) if i < far_in else a for i, a in enumerate(args)]
    if sems:
        scr.append(pltpu.SemaphoreType.DMA((sems,)))
    return pl.pallas_call(
        kernel,
        out_shape=shapes,
        in_specs=[HBM if i < far_in else VMEM for i in range(len(args))],
        out_specs=[HBM if i < far_out else VMEM for i in range(len(outs))],
        scratch_shapes=scr,
        compiler_params=pltpu.CompilerParams(vmem_limit_bytes=40 * 1024 * 1024),
        name=name,
    )(*args)


def swap(v, bit):
    return lax.ppermute(v, "gx", [(i, i ^ bit) for i in range(16)])


def body(cotangent, saved_temp, substrate_top, deposit_top, top_class):
    cot = cotangent.reshape(512, 128)
    temp = saved_temp.reshape(512, 128)
    small = jax.ShapeDtypeStruct((8, 128), jnp.int32)
    cond, keep_m, send_m, cot, sub, dep, cls = call(
        fields_kernel,
        [(512, 128), (160, 128), (160, 128), (512, 128), small, small, small],
        [(512, 128), (5, 64, 128)],
        "fields",
        cot, temp, substrate_top, deposit_top, top_class,
        far_in=5, sems=8,
    )
    other_m = swap(send_m, 1)
    ypack, fac, ties = call(
        first_kernel,
        [(8, 32, 128), (3, 63, 8, 128), (12, 8, 128)],
        [(3, 512, 128), (512, 128)],
        "first",
        cot, sub, dep, cls, cond,
    )
    mm, core_c = call(core_matrix_kernel, [(160, 128), (224, 128)], [], "matrix_core", keep_m, other_m)
    mm, ypack = lax.optimization_barrier((mm, ypack))
    gat = lax.all_to_all(ypack, "gy", split_axis=0, concat_axis=0, tiled=True)
    ring_m = [swap(mm, bit) for bit in (4, 7, 3)]
    keep, send, xfac, xhfac, a2, kh = call(
        second_kernel,
        [(72, 128), (72, 128), (8, 24, 8, 128), (24, 1, 128), (512, 128), (8, 128)],
        [(8, 32, 128), (512, 128), (512, 128), (2, 64, 128)],
        "second",
        gat, fac, ties, cond, sub,
    )
    m1, sv1 = call(core_kernel, [(72, 128), (200, 128)], [], "merge_core", keep, swap(send, 1), core_c)
    ring_v = [swap(m1, bit) for bit in (4, 7, 3)]
    matrix, mine_c, other_c, ring_c, near_m = call(
        ring_matrix_kernel, [(160, 128)] + [(224, 128)] * 3 + [(64, 128)], [], "matrix_ring", mm, *ring_m
    )
    opposite_m = swap(near_m, 9)
    m3, sv2, sv3, near = call(
        ring_kernel,
        [(232, 128), (200, 128), (200, 128), (40, 128)],
        [],
        "merge_ring",
        m1, *ring_v, matrix, mine_c, other_c, ring_c,
    )
    sv3, kh = lax.optimization_barrier((sv3, kh))
    coefs = call(coef_kernel, [(512, 128)] * 5, [], "coef", cond, kh, a2, cot, sub, dep, cls)
    opposite = swap(near, 9)
    sv3, coefs = lax.optimization_barrier((sv3, coefs))
    own, out = call(top_kernel, [(72, 128), (64, 128)], [], "top", m3, near_m, near, opposite_m, opposite, sv1, sv2, sv3)
    got = swap(out, 1)
    part = call(
        own_kernel,
        [(256, 128), (256, 128), (256, 128), (8, 128)],
        [],
        "own_rows",
        own, xfac, xhfac, *coefs, sub,
    )
    grad_temp, grad_source = call(
        last_kernel,
        [(512, 128), (512, 128)],
        [(256, 128), (16, 128), (256, 128), (256, 128)],
        "last",
        got, xfac, *coefs, sub, *part,
        far_out=2, sems=12,
    )
    return grad_temp.reshape(cotangent.shape), grad_source.reshape(cotangent.shape)


def solution(mesh):
    in_specs = (
        P(None, "gx", "gy"),
        P(None, "gx", "gy"),
        P("gx", "gy"),
        P("gx", "gy"),
        P("gx", "gy"),
    )
    out_specs = (P(None, "gx", "gy"), P(None, "gx", "gy"))
    return jax.shard_map(body, mesh=mesh, in_specs=in_specs, out_specs=out_specs, check_vma=False)
```

```python
import jax
import jax.numpy as jnp
from jax import lax
from jax.experimental import pallas as pl
from jax.experimental.pallas import tpu as pltpu
from jax.sharding import PartitionSpec as P

R = 1000.0
SIDE = 0.3
BOTTOM = 0.5
TOPS = (0.05, 0.25, 0.8, 2.0)
F32 = jnp.float32
NLEV = 6


def recip(v):
    return 1.0 / v


def reduce_chain(c, s, d, track):
    levels, port, ties = [], None, []
    while len(s) > 1:
        half = len(s) // 2
        ml, mr, dv = [], [], []
        for j in range(half):
            i = 2 * j
            total = s[i] + c[i]
            if j:
                total = total + c[i - 1]
            inv = recip(total)
            mr.append(c[i] * inv)
            ml.append(c[i - 1] * inv if j else None)
            dv.append(d[i] * inv)
            if track and j == 0:
                if port is None:
                    port = [dv[0], inv, mr[0]]
                    ties.append(inv)
                else:
                    p, z, t = port
                    tie = t * inv
                    ties.append(tie)
                    port = [p + t * dv[0], z + t * tie, t * mr[0]]
        ns, nd, nc = [], [], []
        for j in range(half):
            e, o = 2 * j, 2 * j + 1
            sv = s[o] + mr[j] * s[e]
            dn = d[o] + mr[j] * d[e]
            if j + 1 < half:
                sv = sv + ml[j + 1] * s[e + 2]
                dn = dn + ml[j + 1] * d[e + 2]
                nc.append(ml[j + 1] * c[e + 2])
            ns.append(sv)
            nd.append(dn)
        levels.append((dv, ml, mr))
        c, s, d = nc, ns, nd
    return s[0], d[0], levels, port, ties


def expand_chain(u_last, levels, ties, flux):
    u = [u_last]
    for lev in range(len(levels) - 1, -1, -1):
        dv, ml, mr = levels[lev]
        out = []
        for j in range(len(u)):
            even = dv[j] + mr[j] * u[j]
            if j:
                even = even + ml[j] * u[j - 1]
            elif ties is not None:
                even = even + ties[lev] * flux
            out += [even, u[j]]
        u = out
    return u


def port_coefs(a, b):
    kfa, kla, za, ta, ga = a
    kfb, klb, zb, tb, gb = b
    link = R * jnp.minimum(kla, kfb)
    lk = link * recip(1.0 + link * zb)
    inv = recip(ga + lk)
    ti = ta * inv
    lt = lk * tb
    w = lt * inv
    merged = (kfa, klb, za + ta * ti, ta * w, gb + lt * tb * (ga * inv))
    return merged, (inv, lk, ta, lt, ti, w, tb)


def port_values(coefs, a, b):
    inv, lk, ta, lt, ti, w, tb = coefs
    pa, qa = a
    pb, qb = b
    h = inv * (qa + lk * pb)
    return (pa + ta * h, qb + lt * (h - pb)), (h, ti, w, lk, pb, tb)


def merge_ports(a, b):
    matrix, coefs = port_coefs(a[:5], b[:5])
    values, saved = port_values(coefs, a[5:], b[5:])
    return matrix + values, saved


def descend(saved, flux, u_b):
    h, ti, w, lk, pb, tb = saved
    u_a = h + ti * flux + w * u_b
    flux_b = lk * (u_a - pb - tb * u_b)
    return u_a, flux_b


def film_top(cls):
    total = jnp.zeros(cls.shape, F32)
    for n in range(4):
        total = total + TOPS[n] * (cls == n).astype(F32)
    return total


def node_order(half, lev):
    base, n = 0, half
    for _ in range(lev):
        base += n
        n //= 2
    return base, n


def put_levels(ref, levels):
    half = len(levels[0][0])
    for lev, triple in enumerate(levels):
        base, n = node_order(half, lev)
        for kind in range(3):
            for j in range(n):
                if triple[kind][j] is not None:
                    ref[kind, base + j] = triple[kind][j]


def get_levels(read, half):
    levels, lev = [], 0
    while half >> lev:
        base, n = node_order(half, lev)
        levels.append(
            tuple([None if kind == 1 and j == 0 else read(kind, base + j) for j in range(n)] for kind in range(3))
        )
        lev += 1
    return levels


def chain_matrix(c, s):
    z = t = None
    while len(s) > 1:
        half = len(s) // 2
        ml, mr = [None] * half, [None] * half
        for j in range(half):
            i = 2 * j
            inv = recip(s[i] + c[i] + c[i - 1] if j else s[i] + c[i])
            mr[j] = c[i] * inv
            if j:
                ml[j] = c[i - 1] * inv
            elif z is None:
                z, t = inv, mr[0]
            else:
                z, t = z + t * (t * inv), t * mr[0]
        ns, nc = [], []
        for j in range(half):
            e = 2 * j
            sv = s[e + 1] + mr[j] * s[e]
            if j + 1 < half:
                sv = sv + ml[j + 1] * s[e + 2]
                nc.append(ml[j + 1] * c[e + 2])
            ns.append(sv)
        c, s = nc, ns
    return z, t, s[0]


def wall_terms():
    me_x = lax.axis_index("gx")
    return jnp.where(me_x == 0, R * SIDE, 0.0), jnp.where(me_x == 15, R * SIDE, 0.0)


def own_half():
    me_x = lax.axis_index("gx")
    return lax.rem(me_x + lax.div(me_x, 2) + lax.div(me_x, 8), 2)


def split_halves(planes, keep, send):
    core = own_half()
    for i in range(planes.shape[0]):
        keep[32 * i : 32 * i + 32] = planes[i, pl.ds(pl.multiple_of(32 * core, 32), 32), :]
        send[32 * i : 32 * i + 32] = planes[i, pl.ds(pl.multiple_of(32 - 32 * core, 32), 32), :]


def turned(rows, dst, q):
    block = jnp.transpose(rows)
    for h in range(2):
        dst[pl.ds(4 * h + q, 64, stride=8), :] = block[64 * h : 64 * h + 64]


def fields_kernel(cot_in, temp_in, sub_in, dep_in, cls_in, cond, keep, send, cot, sub, dep, cls, sub_t, temp, planes, sems):
    pieces = [slice(128 * i, 128 * i + 128) for i in range(4)]
    pairs = [(sub_in, sub), (dep_in, dep)] + [(temp_in.at[r], temp.at[r]) for r in pieces]
    pairs += [(cls_in, cls), (cot_in, cot)]
    copies = [pltpu.make_async_copy(a, b, sems.at[i]) for i, (a, b) in enumerate(pairs)]
    for cp in copies:
        cp.start()
    for cp in copies[:2]:
        cp.wait()
    sub_v, dep_v = sub[...], dep[...]
    subf = sub_v.astype(F32)
    upper = (lax.broadcasted_iota(jnp.int32, (128, 128), 0) & 1) == 1
    for q in range(4):
        turned(jnp.where(upper, subf[q + 4 : q + 5], subf[q : q + 1]), sub_t, q)
    for z in range(64):
        if z % 16 == 0:
            copies[2 + z // 16].wait()
        base = jnp.where(z < sub_v, 1.0, 0.45)
        sg = 0.5 + jax.nn.sigmoid(temp[8 * z : 8 * z + 8])
        cond[8 * z : 8 * z + 8] = jnp.where(z < dep_v, base * sg, 0.0)
    low, high = wall_terms()
    base_z = lax.broadcasted_iota(jnp.int32, (8, 128), 0)
    for chunk in range(8):
        zi = base_z + 8 * chunk
        k = [cond[pl.ds(64 * chunk + x, 8, stride=8), :] for x in range(8)]
        s = [jnp.where(zi < sub_v[x : x + 1], 1.0, 0.6) for x in range(8)]
        s[0] = s[0] + low
        s[7] = s[7] + high
        c = [R * jnp.minimum(k[x], k[x + 1]) for x in range(7)] + [None]
        for i, v in enumerate((k[0], k[7]) + chain_matrix(c, s)):
            planes[i, 8 * chunk : 8 * chunk + 8] = v
    split_halves(planes, keep, send)
    for cp in copies[6:]:
        cp.wait()


def first_kernel(cot, sub, dep, cls, cond, sub_t, ypack, fac, tie_out, mid, tr, pack, sems):
    me_y = lax.axis_index("gy")
    sub_v, dep_v = sub[...], dep[...]
    top = film_top(cls[...])
    k, cap, s = [], [], []
    for z in range(64):
        k.append(cond[8 * z : 8 * z + 8])
        cap.append(jnp.where(z < sub_v, 1.0, 0.6))
        film = top * (dep_v - 1 == z).astype(F32)
        if z == 0:
            film = film + BOTTOM
        s.append(cap[z] + R * film)
    c = [R * jnp.minimum(k[z], k[z + 1]) for z in range(63)] + [None]
    d = [cot[8 * z : 8 * z + 8] for z in range(64)]
    g, q, levels, _, _ = reduce_chain(c, s, d, False)
    u = expand_chain(q * recip(g), levels, None, None)
    for z in range(64):
        tr[8 * z : 8 * z + 8] = cap[z] * u[z]

    for q in range(4):
        turned(cond[pl.ds(q, 128, stride=4), :], mid.at[0], q)
        turned(tr[pl.ds(q, 128, stride=4), :], mid.at[1], q)
    z_lane = (lax.broadcasted_iota(jnp.int32, (8, 128), 1) >> 1).astype(F32)
    row = lax.broadcasted_iota(jnp.int32, (8, 128), 0)
    ky, sy, dy = [], [], []
    for y in range(64):
        ky.append(mid[0, 8 * y : 8 * y + 8])
        dy.append(mid[1, 8 * y : 8 * y + 8])
        sy.append(jnp.where(z_lane < sub_t[8 * y : 8 * y + 8], 1.0, 0.6))
    low = jnp.where(me_y == 0, R * SIDE, 0.0)
    high = jnp.where(me_y == 7, R * SIDE, 0.0)
    sy[0] = sy[0] + jnp.where(row < 4, low, 0.0)
    sy[63] = sy[63] + jnp.where(row >= 4, high, 0.0)
    cy = [R * jnp.minimum(ky[y], ky[y + 1]) for y in range(63)] + [None]
    g, q, levels, (p, zz, t), ties = reduce_chain(cy, sy, dy, True)
    kf, kl = ky[0], ky[63]
    side_a = tuple(v[0:4] for v in (kf, kl, zz, t, g, p, q))
    side_b = tuple(v[4:8] for v in (kf, kl, zz, t, g, p, q))
    merged, saved = merge_ports(side_a, side_b)
    for i, v in enumerate(saved):
        tie_out[NLEV + i, 0:4] = v
    lower = lax.broadcasted_iota(jnp.int32, (4, 128), 1) < 64
    edges = jnp.where(lower, sub_t[0:4], sub_t[508:512])
    pack[...] = jnp.concatenate(list(merged) + [edges], axis=0)
    copies = [pltpu.make_async_copy(pack, ypack.at[n], sems.at[n]) for n in range(8)]
    for cp in copies:
        cp.start()
    put_levels(fac, levels)
    for lev in range(NLEV):
        tie_out[lev] = ties[lev]
    for cp in copies:
        cp.wait()


def x_chain(k, cap, d):
    low, high = wall_terms()
    s = list(cap)
    s[0] = s[0] + low
    s[7] = s[7] + high
    c = [R * jnp.minimum(k[x], k[x + 1]) for x in range(7)] + [None]
    g, q, levels, (p, z, t), tie = reduce_chain(c, s, d, True)
    return levels, tie, (k[0], k[7], z, t, g, p, q)


def x_rows(half, cond, planes, subf, out, xfac):
    base_z = lax.broadcasted_iota(jnp.int32, (8, 128), 0)
    for chunk in range(4):
        zi = base_z + (32 * half + 8 * chunk)
        k, cap, d = [], [], []
        for x in range(8):
            at = pl.ds(256 * half + (64 * chunk + x), 8, stride=8)
            k.append(cond[at, :])
            cap.append(jnp.where(zi < subf[x : x + 1], 1.0, 0.6))
            d.append(cap[x] * planes[at, :])
        levels, tie, port = x_chain(k, cap, d)
        store_x(xfac.at[chunk], levels, tie)
        for i in range(2):
            out[32 * i + 8 * chunk : 32 * i + 8 * chunk + 8] = port[5 + i]


def keep_kernel(cond, planes, sub, keep, xfac):
    x_rows(own_half(), cond, planes, sub[...], keep, xfac)


def second_kernel(gat, fac, ties, cond, sub, send, edge, xfac, xhfac, kh_out, planes, pick, flat):
    me_y = lax.axis_index("gy")
    seg = [[gat[n, 4 * i : 4 * i + 4] for i in range(8)] for n in range(8)]
    gam, rhs = seg[0][4], seg[0][6]
    down, links = [None], [None]
    for n in range(1, 8):
        kf, kl, z, t, g, p, q = seg[n][:7]
        link = R * jnp.minimum(seg[n - 1][1], kf)
        lk = link * recip(1.0 + link * z)
        inv = recip(gam + lk)
        h = inv * (rhs + lk * p)
        lt = lk * t
        down.append((h, lt * inv))
        links.append(lk)
        rhs = q + lt * (h - p)
        gam = g + lt * t * (gam * inv)
    u = [None] * 8
    u[7] = rhs * recip(gam)
    for n in range(7, 0, -1):
        u[n - 1] = down[n][0] + down[n][1] * u[n]
    zero4 = jnp.zeros((4, 128), F32)
    fl, uf = [zero4], [None]
    for n in range(1, 8):
        kf, kl, z, t, g, p, q = seg[n][:7]
        fl.append(links[n] * (u[n - 1] - p - t * u[n]))
        uf.append(p + z * fl[n] + t * u[n])
    for n in range(8):
        rows = [fl[n], u[n]]
        if n:
            rows += [u[n - 1], seg[n - 1][1], seg[n - 1][7]]
        else:
            rows += [zero4, zero4, zero4]
        if n < 7:
            rows += [uf[n + 1], seg[n + 1][0], seg[n + 1][7]]
        else:
            rows += [zero4, zero4, zero4]
        for i, v in enumerate(rows):
            pick[n, 4 * i : 4 * i + 4] = v
    mine = [pick[me_y, 4 * i : 4 * i + 4] for i in range(8)]
    flux, u_b = mine[0], mine[1]
    saved = tuple(ties[NLEV + i, 0:4] for i in range(6))
    u_a, flux_b = descend(saved, flux, u_b)
    flux8 = jnp.concatenate([flux, flux_b], axis=0)
    last8 = jnp.concatenate([u_a, u_b], axis=0)
    levels = get_levels(lambda kind, i: fac[kind, i], 32)
    u_nodes = expand_chain(last8, levels, [ties[i] for i in range(NLEV)], flux8)
    for y in range(64):
        flat[8 * y : 8 * y + 8] = u_nodes[y]
    subf = sub[...]
    for q in range(4):
        planes[pl.ds(q, 128, stride=4), :] = jnp.transpose(
            jnp.concatenate([flat[pl.ds(q, 64, stride=8), :], flat[pl.ds(4 + q, 64, stride=8), :]], axis=0)
        )

    lane = lax.broadcasted_iota(jnp.int32, (4, 128), 1)
    even = (lane & 1) == 0
    z_of = (lane >> 1).astype(F32)
    cap_l = jnp.where(z_of < jnp.where(lane < 64, pltpu.roll(mine[4], 64, 1), mine[4]), 1.0, 0.6)
    cap_r = jnp.where(z_of < jnp.where(lane < 64, mine[7], pltpu.roll(mine[7], 64, 1)), 1.0, 0.6)

    def both(left, right):
        low = jnp.where(even, left, pltpu.roll(right, 127, 1))
        high = jnp.where(even, pltpu.roll(left, 127, 1), pltpu.roll(right, 126, 1))
        return [low[x : x + 1] for x in range(4)] + [high[x : x + 1] for x in range(4)]

    dh, kh, caph = both(cap_l * mine[2], cap_r * mine[5]), both(mine[3], mine[6]), both(cap_l, cap_r)
    for x in range(8):
        kh_out[x : x + 1] = kh[x]

    levels, tie, port = x_chain(kh, caph, dh)
    store_x(xhfac, levels, tie)
    for i in range(7):
        send[64 + i : 65 + i] = port[i]
        edge[i : i + 1] = port[i]
    x_rows(1 - own_half(), cond, planes, subf, send, xfac)


def store_x(ref, levels, tie):
    for lev, triple in enumerate(levels):
        base, n = node_order(4, lev)
        for kind in range(3):
            for j in range(n):
                if triple[kind][j] is not None:
                    ref[7 * kind + base + j] = triple[kind][j]
    for lev in range(3):
        ref[21 + lev] = tie[lev]


def load_x(ref):
    levels = get_levels(lambda kind, i: ref[7 * kind + i], 4)
    return levels, [ref[21 + lev] for lev in range(3)]


def read_pack(ref, n):
    main = tuple(ref[32 * i : 32 * i + 32] for i in range(n))
    edge = tuple(ref[32 * n + i : 32 * n + i + 1] for i in range(n))
    return main, edge


def write_pack(ref, main, edge):
    n = len(main)
    for i in range(n):
        ref[32 * i : 32 * i + 32] = main[i]
        ref[32 * n + i : 32 * n + i + 1] = edge[i]


def order(right, mine, theirs):
    a = tuple(jnp.where(right, t, m) for m, t in zip(mine, theirs))
    b = tuple(jnp.where(right, m, t) for m, t in zip(mine, theirs))
    return a, b


def planes_of(ref, n):
    return tuple(ref[32 * i : 32 * i + 32] for i in range(n))


def put_planes(ref, values):
    for i, v in enumerate(values):
        ref[32 * i : 32 * i + 32] = v


def spots():
    me_x = lax.axis_index("gx")
    return [lax.rem(lax.div(me_x, bit), 2) == 1 for bit in (1, 2, 4)]


def core_matrix_kernel(mine, theirs, merged_out, coef_out):
    odd, _, _ = spots()
    merged, coefs = port_coefs(*order(odd, planes_of(mine, 5), planes_of(theirs, 5)))
    put_planes(merged_out, merged)
    put_planes(coef_out, coefs)


def ring_matrix_kernel(own, mid, far, near, merged_out, mine_out, other_out, ring_out, top_out):
    _, right, upper = spots()
    packs = [planes_of(r, 5) for r in (own, near, mid, far)]
    mine, mine_c = port_coefs(*order(right, packs[0], packs[1]))
    other, other_c = port_coefs(*order(right, packs[2], packs[3]))
    merged, ring_c = port_coefs(*order(upper, mine, other))
    put_planes(merged_out, merged)
    put_planes(mine_out, mine_c)
    put_planes(other_out, other_c)
    put_planes(ring_out, ring_c)
    last = lax.div(lax.axis_index("gx"), 8) == 1
    kf, kl, z, tt, g = merged
    put_planes(top_out, (jnp.where(last, z + tt * (tt * recip(g)), g), jnp.where(last, kf, kl)))


def read_sides(ref):
    main = (ref[0:32], ref[32:64])
    edge = tuple(ref[64 + i : 65 + i] for i in range(7))
    return main, edge


def core_kernel(mine, edge_mine, theirs, coefs, merged_out, saved_out):
    odd, _, _ = spots()
    m = (mine[0:32], mine[32:64]), tuple(edge_mine[i : i + 1] for i in range(7))
    t = read_sides(theirs)
    values, saved = port_values(planes_of(coefs, 7), *order(odd, m[0], t[0]))
    edge, edge_saved = merge_ports(*order(odd, m[1], t[1]))
    put_planes(merged_out, values)
    for i in range(7):
        merged_out[64 + i : 65 + i] = edge[i]
    write_pack(saved_out, saved, edge_saved)


def ring_kernel(own, mid, far, near, matrix, mine_c, other_c, ring_c, merged_out, pair_out, saved_out, top_out):
    _, right, upper = spots()
    last = lax.div(lax.axis_index("gx"), 8) == 1
    main, edge = zip(*[read_sides(r) for r in (own, near, mid, far)])
    mine, pair = port_values(planes_of(mine_c, 7), *order(right, main[0], main[1]))
    other, _ = port_values(planes_of(other_c, 7), *order(right, main[2], main[3]))
    values, saved = port_values(planes_of(ring_c, 7), *order(upper, mine, other))
    e_mine, e_pair = merge_ports(*order(right, edge[0], edge[1]))
    e_other, _ = merge_ports(*order(right, edge[2], edge[3]))
    e_merged, e_saved = merge_ports(*order(upper, e_mine, e_other))
    outs = [planes_of(matrix, 5) + values, e_merged]
    write_pack(merged_out, *outs)
    kf, kl, z, tt, g, p, q = outs[0]
    top_out[0:32] = jnp.where(last, p + tt * recip(g) * q, q)
    kf, kl, z, tt, g, p, q = e_merged
    tg = tt * recip(g)
    for i, (a, b) in enumerate(((z + tt * tg, g), (p + tg * q, q), (kf, kl))):
        top_out[32 + i : 33 + i] = jnp.where(last, a, b)
    write_pack(pair_out, pair, e_pair)
    write_pack(saved_out, saved, e_saved)


def read_top(matrix, values):
    main = (matrix[0:32], values[0:32], matrix[32:64])
    return main, tuple(values[32 + i : 33 + i] for i in range(3))


def top_kernel(merged, near_m, near, theirs_m, theirs, sv1, sv2, sv3, own, send):
    me_x = lax.axis_index("gx")
    far = lax.div(me_x, 8) == 1
    mm = read_pack(merged, 7)
    n, t = read_top(near_m, near), read_top(theirs_m, theirs)
    saved = [read_pack(r, 6) for r in (sv1, sv2, sv3)]
    final = []
    for part in range(2):
        (ga, qa, ka), (zb, pb, kb) = order(far, n[part], t[part])
        link = R * jnp.minimum(ka, kb)
        lk = link * recip(1.0 + link * zb)
        u_a = (qa + lk * pb) * recip(ga + lk)
        kf, kl, z, tt, g, p, q = mm[part]
        flux = jnp.where(far, lk * (u_a - pb), 0.0)
        u = jnp.where(far, (q + tt * flux) * recip(g), u_a)
        for bit, lev in ((4, 2), (2, 1)):
            right = lax.rem(lax.div(me_x, bit), 2) == 1
            ua, fb = descend(saved[lev][part], flux, u)
            flux = jnp.where(right, fb, flux)
            u = jnp.where(right, u, ua)
        ua, fb = descend(saved[0][part], flux, u)
        odd = lax.rem(me_x, 2) == 1
        final.append((jnp.where(odd, fb, flux), jnp.where(odd, u, ua), jnp.where(odd, flux, fb), jnp.where(odd, ua, u)))
    write_pack(own, final[0][:2], final[1][:2])
    send[0:32] = final[0][2]
    send[32:64] = final[0][3]


def coef_kernel(cond, kh, planes, cot, sub, dep, cls, k_y, k_l, k_z, k_s, base):
    me_y = lax.axis_index("gy")
    sub_v, dep_v, kh_v = sub[...], dep[...], kh[...]
    top = film_top(cls[...])
    lane = lax.broadcasted_iota(jnp.int32, (8, 128), 1)
    first, final = lane == 0, lane == 127
    film_y = jnp.where(first & (me_y == 0), SIDE, 0.0) + jnp.where(final & (me_y == 7), SIDE, 0.0)
    for z in range(64):
        rows = slice(8 * z, 8 * z + 8)
        k = cond[rows]
        k_h = pltpu.roll(kh_v, 128 - 2 * z, 1) if z else kh_v
        k_y[rows] = (2.0 * R) * jnp.minimum(k, jnp.where(final, k_h, pltpu.roll(k, 127, 1)))
        k_l[rows] = (2.0 * R) * jnp.minimum(k, k_h)
        if z < 63:
            k_z[rows] = (2.0 * R) * jnp.minimum(k, cond[8 * z + 8 : 8 * z + 16])
        else:
            k_z[rows] = jnp.zeros((8, 128), F32)
        film = film_y + top * (dep_v - 1 == z).astype(F32)
        if z == 0:
            film = film + BOTTOM
        cap = jnp.where(z < sub_v, 1.0, 0.6)
        k_s[rows] = 2.0 * cap - (2.0 * R) * film
        base[rows] = cot[rows] - 2.0 * (cap * planes[rows])


def expand_rows(xfac, flux, last, s1):
    for chunk in range(4):
        rows = slice(8 * chunk, 8 * chunk + 8)
        levels, tie = load_x(xfac.at[chunk])
        u = expand_chain(last[rows], levels, tie, flux[rows])
        for x in range(8):
            s1[pl.ds(64 * chunk + x, 8, stride=8), :] = u[x]


def stencil(half, uh, s1, k_y, k_l, k_z, k_s, base, sub_v, below, above, src, out, done=None):
    lane = lax.broadcasted_iota(jnp.int32, (8, 128), 1)
    first, final = lane == 0, lane == 127
    up = below
    for i in range(32):
        rows = slice(8 * i, 8 * i + 8)
        at = pl.ds(pl.multiple_of(256 * half + 8 * i, 8), 8)
        s = s1[rows]
        s_h = pltpu.roll(uh, 128 - 2 * i, 1) if i else uh
        f_y = k_y[at, :] * (jnp.where(final, s_h, pltpu.roll(s, 127, 1)) - s)
        f_l = k_l[at, :] * (s - s_h)
        total = f_y - jnp.where(first, f_l, pltpu.roll(f_y, 1, 1))
        f_z = k_z[at, :] * (s1[8 * i + 8 : 8 * i + 16] - s) if i < 31 else above
        if f_z is not None:
            total = total + f_z
        if up is not None:
            total = total - up
        up = f_z
        src[rows] = jnp.where(32 * half + i < sub_v, 1.0, 0.6) * s
        out[rows] = base[at, :] + k_s[at, :] * s + total
        if done is not None and i & 7 == 7:
            done(i // 8)


def own_kernel(own, xfac, xhfac, k_y, k_l, k_z, k_s, base, sub, s1, src, out, uh_out):
    half = own_half()
    levels, tie = load_x(xhfac)
    uh = jnp.concatenate(expand_chain(own[65:66], levels, tie, own[64:65]), axis=0)
    turned = pltpu.roll(uh, 64, 1)
    uh_out[...] = jnp.where(half == 1, uh, turned)
    expand_rows(xfac, own.at[0:32], own.at[32:64], s1)
    uh = jnp.where(half == 1, turned, uh)
    stencil(half, uh, s1, k_y, k_l, k_z, k_s, base, sub[...], None, None, src, out)


def last_kernel(
    got, xfac, k_y, k_l, k_z, k_s, base, sub, s_own, src_own, out_own, uh, temp_out, src_out, s1, ends, t_buf, s_buf, sems
):
    mine = own_half()
    half = 1 - mine
    copies = []

    def send(buf, rows, out, start):
        size = rows.stop - rows.start
        cp = pltpu.make_async_copy(buf.at[rows], out.at[pl.ds(pl.multiple_of(start, 8), size)], sems.at[len(copies)])
        cp.start()
        copies.append(cp)

    send(src_own, slice(0, 256), src_out, 256 * mine)
    send(out_own, slice(8, 248), temp_out, 256 * mine + 8)
    expand_rows(xfac, got.at[0:32], got.at[32:64], s1)
    inner, outer = s_own[248:256], s_own[0:8]
    low = jnp.where(half == 0, s1[248:256], inner)
    high = jnp.where(half == 0, outer, s1[0:8])
    flux = k_z[248:256] * (high - low)
    ends[0:8] = out_own[0:8] - jnp.where(mine == 1, flux, 0.0)
    ends[8:16] = out_own[248:256] + jnp.where(mine == 0, flux, 0.0)
    send(ends, slice(0, 8), temp_out, 256 * mine)
    send(ends, slice(8, 16), temp_out, 256 * mine + 248)

    def done(piece):
        rows = slice(64 * piece, 64 * piece + 64)
        send(s_buf, rows, src_out, 256 * half + 64 * piece)
        send(t_buf, rows, temp_out, 256 * half + 64 * piece)

    below, above = jnp.where(half == 1, flux, 0.0), jnp.where(half == 0, flux, 0.0)
    stencil(half, uh[...], s1, k_y, k_l, k_z, k_s, base, sub[...], below, above, s_buf, t_buf, done)
    for cp in copies:
        cp.wait()


VMEM = pl.BlockSpec(memory_space=pltpu.VMEM)
HBM = pl.BlockSpec(memory_space=pltpu.MemorySpace.HBM)


def call(kernel, outs, scratch, name, *args, far_in=0, far_out=0, sems=0):
    shapes = [s if isinstance(s, jax.ShapeDtypeStruct) else jax.ShapeDtypeStruct(s, F32) for s in outs]
    scr = [pltpu.VMEM(s, F32) for s in scratch]
    args = [pltpu.with_memory_space_constraint(a, pltpu.MemorySpace.HBM) if i < far_in else a for i, a in enumerate(args)]
    if sems:
        scr.append(pltpu.SemaphoreType.DMA((sems,)))
    return pl.pallas_call(
        kernel,
        out_shape=shapes,
        in_specs=[HBM if i < far_in else VMEM for i in range(len(args))],
        out_specs=[HBM if i < far_out else VMEM for i in range(len(outs))],
        scratch_shapes=scr,
        compiler_params=pltpu.CompilerParams(vmem_limit_bytes=40 * 1024 * 1024),
        name=name,
    )(*args)


def swap(v, bit):
    return lax.ppermute(v, "gx", [(i, i ^ bit) for i in range(16)])


def body(cotangent, saved_temp, substrate_top, deposit_top, top_class):
    cot = cotangent.reshape(512, 128)
    temp = saved_temp.reshape(512, 128)
    small = jax.ShapeDtypeStruct((8, 128), jnp.int32)
    cond, keep_m, send_m, cot, sub, dep, cls, sub_t = call(
        fields_kernel,
        [(512, 128), (160, 128), (160, 128), (512, 128), small, small, small, (512, 128)],
        [(512, 128), (5, 64, 128)],
        "fields",
        cot, temp, substrate_top, deposit_top, top_class,
        far_in=5, sems=8,
    )
    other_m = swap(send_m, 1)
    ypack, fac, ties = call(
        first_kernel,
        [(8, 32, 128), (3, 63, 8, 128), (12, 8, 128)],
        [(2, 512, 128), (512, 128), (32, 128)],
        "first",
        cot, sub, dep, cls, cond, sub_t,
        far_out=1, sems=8,
    )
    mm, core_c = call(core_matrix_kernel, [(160, 128), (224, 128)], [], "matrix_core", keep_m, other_m)
    mm, ypack = lax.optimization_barrier((mm, ypack))
    gat = lax.all_to_all(ypack, "gy", split_axis=0, concat_axis=0, tiled=True)
    ring_m = [swap(mm, bit) for bit in (4, 7, 3)]
    send, edge, xfac, xhfac, kh, planes = call(
        second_kernel,
        [(72, 128), (8, 128), (4, 24, 8, 128), (24, 1, 128), (8, 128), (512, 128)],
        [(8, 32, 128), (512, 128)],
        "second",
        gat, fac, ties, cond, sub,
    )
    keep, xfac_own = call(keep_kernel, [(64, 128), (4, 24, 8, 128)], [], "keep_rows", cond, planes, sub)
    m1, sv1 = call(core_kernel, [(72, 128), (200, 128)], [], "merge_core", keep, edge, swap(send, 1), core_c)
    ring_v = [swap(m1, bit) for bit in (4, 7, 3)]
    matrix, mine_c, other_c, ring_c, near_m = call(
        ring_matrix_kernel, [(160, 128)] + [(224, 128)] * 3 + [(64, 128)], [], "matrix_ring", mm, *ring_m
    )
    opposite_m = swap(near_m, 9)
    m3, sv2, sv3, near = call(
        ring_kernel,
        [(232, 128), (200, 128), (200, 128), (40, 128)],
        [],
        "merge_ring",
        m1, *ring_v, matrix, mine_c, other_c, ring_c,
    )
    sv3, kh = lax.optimization_barrier((sv3, kh))
    coefs = call(coef_kernel, [(512, 128)] * 5, [], "coef", cond, kh, planes, cot, sub, dep, cls)
    opposite = swap(near, 9)
    sv3, coefs = lax.optimization_barrier((sv3, coefs))
    own, out = call(top_kernel, [(72, 128), (64, 128)], [], "top", m3, near_m, near, opposite_m, opposite, sv1, sv2, sv3)
    got = swap(out, 1)
    part = call(
        own_kernel,
        [(256, 128), (256, 128), (256, 128), (8, 128)],
        [],
        "own_rows",
        own, xfac_own, xhfac, *coefs, sub,
    )
    grad_temp, grad_source = call(
        last_kernel,
        [(512, 128), (512, 128)],
        [(256, 128), (16, 128), (256, 128), (256, 128)],
        "last",
        got, xfac, *coefs, sub, *part,
        far_out=2, sems=12,
    )
    return grad_temp.reshape(cotangent.shape), grad_source.reshape(cotangent.shape)


def solution(mesh):
    in_specs = (
        P(None, "gx", "gy"),
        P(None, "gx", "gy"),
        P("gx", "gy"),
        P("gx", "gy"),
        P("gx", "gy"),
    )
    out_specs = (P(None, "gx", "gy"), P(None, "gx", "gy"))
    return jax.shard_map(body, mesh=mesh, in_specs=in_specs, out_specs=out_specs, check_vma=False)
```

```python
import jax
import jax.numpy as jnp
from jax import lax
from jax.experimental import pallas as pl
from jax.experimental.pallas import tpu as pltpu
from jax.sharding import PartitionSpec as P

R = 1000.0
SIDE = 0.3
BOTTOM = 0.5
TOPS = (0.05, 0.25, 0.8, 2.0)
F32 = jnp.float32
NLEV = 6


def recip(v):
    return 1.0 / v


def reduce_chain(c, s, d, track):
    levels, port, ties = [], None, []
    while len(s) > 1:
        half = len(s) // 2
        ml, mr, dv = [], [], []
        for j in range(half):
            i = 2 * j
            total = s[i] + c[i]
            if j:
                total = total + c[i - 1]
            inv = recip(total)
            mr.append(c[i] * inv)
            ml.append(c[i - 1] * inv if j else None)
            dv.append(d[i] * inv)
            if track and j == 0:
                if port is None:
                    port = [dv[0], inv, mr[0]]
                    ties.append(inv)
                else:
                    p, z, t = port
                    tie = t * inv
                    ties.append(tie)
                    port = [p + t * dv[0], z + t * tie, t * mr[0]]
        ns, nd, nc = [], [], []
        for j in range(half):
            e, o = 2 * j, 2 * j + 1
            sv = s[o] + mr[j] * s[e]
            dn = d[o] + mr[j] * d[e]
            if j + 1 < half:
                sv = sv + ml[j + 1] * s[e + 2]
                dn = dn + ml[j + 1] * d[e + 2]
                nc.append(ml[j + 1] * c[e + 2])
            ns.append(sv)
            nd.append(dn)
        levels.append((dv, ml, mr))
        c, s, d = nc, ns, nd
    return s[0], d[0], levels, port, ties


def expand_chain(u_last, levels, ties, flux):
    u = [u_last]
    for lev in range(len(levels) - 1, -1, -1):
        dv, ml, mr = levels[lev]
        out = []
        for j in range(len(u)):
            even = dv[j] + mr[j] * u[j]
            if j:
                even = even + ml[j] * u[j - 1]
            elif ties is not None:
                even = even + ties[lev] * flux
            out += [even, u[j]]
        u = out
    return u


def port_coefs(a, b):
    kfa, kla, za, ta, ga = a
    kfb, klb, zb, tb, gb = b
    link = R * jnp.minimum(kla, kfb)
    lk = link * recip(1.0 + link * zb)
    inv = recip(ga + lk)
    ti = ta * inv
    lt = lk * tb
    w = lt * inv
    merged = (kfa, klb, za + ta * ti, ta * w, gb + lt * tb * (ga * inv))
    return merged, (inv, lk, ta, lt, ti, w, tb)


def port_values(coefs, a, b):
    inv, lk, ta, lt, ti, w, tb = coefs
    pa, qa = a
    pb, qb = b
    h = inv * (qa + lk * pb)
    return (pa + ta * h, qb + lt * (h - pb)), (h, ti, w, lk, pb, tb)


def merge_ports(a, b):
    matrix, coefs = port_coefs(a[:5], b[:5])
    values, saved = port_values(coefs, a[5:], b[5:])
    return matrix + values, saved


def descend(saved, flux, u_b):
    h, ti, w, lk, pb, tb = saved
    u_a = h + ti * flux + w * u_b
    flux_b = lk * (u_a - pb - tb * u_b)
    return u_a, flux_b


def film_top(cls):
    total = jnp.zeros(cls.shape, F32)
    for n in range(4):
        total = total + TOPS[n] * (cls == n).astype(F32)
    return total


def node_order(half, lev):
    base, n = 0, half
    for _ in range(lev):
        base += n
        n //= 2
    return base, n


def put_levels(ref, levels):
    half = len(levels[0][0])
    for lev, triple in enumerate(levels):
        base, n = node_order(half, lev)
        for kind in range(3):
            for j in range(n):
                if triple[kind][j] is not None:
                    ref[kind, base + j] = triple[kind][j]


def get_levels(read, half):
    levels, lev = [], 0
    while half >> lev:
        base, n = node_order(half, lev)
        levels.append(
            tuple([None if kind == 1 and j == 0 else read(kind, base + j) for j in range(n)] for kind in range(3))
        )
        lev += 1
    return levels


def chain_matrix(c, s):
    z = t = None
    while len(s) > 1:
        half = len(s) // 2
        ml, mr = [None] * half, [None] * half
        for j in range(half):
            i = 2 * j
            inv = recip(s[i] + c[i] + c[i - 1] if j else s[i] + c[i])
            mr[j] = c[i] * inv
            if j:
                ml[j] = c[i - 1] * inv
            elif z is None:
                z, t = inv, mr[0]
            else:
                z, t = z + t * (t * inv), t * mr[0]
        ns, nc = [], []
        for j in range(half):
            e = 2 * j
            sv = s[e + 1] + mr[j] * s[e]
            if j + 1 < half:
                sv = sv + ml[j + 1] * s[e + 2]
                nc.append(ml[j + 1] * c[e + 2])
            ns.append(sv)
        c, s = nc, ns
    return z, t, s[0]


def wall_terms():
    me_x = lax.axis_index("gx")
    return jnp.where(me_x == 0, R * SIDE, 0.0), jnp.where(me_x == 15, R * SIDE, 0.0)


def own_half():
    me_x = lax.axis_index("gx")
    return lax.rem(me_x + lax.div(me_x, 2) + lax.div(me_x, 8), 2)


def split_halves(planes, keep, send):
    core = own_half()
    for i in range(planes.shape[0]):
        keep[32 * i : 32 * i + 32] = planes[i, pl.ds(pl.multiple_of(32 * core, 32), 32), :]
        send[32 * i : 32 * i + 32] = planes[i, pl.ds(pl.multiple_of(32 - 32 * core, 32), 32), :]


def fields_kernel(cot_in, temp_in, sub_in, dep_in, cls_in, cond, keep, send, cot, sub, dep, cls, temp, planes, sems):
    pieces = [slice(128 * i, 128 * i + 128) for i in range(4)]
    pairs = [(sub_in, sub), (dep_in, dep)] + [(temp_in.at[r], temp.at[r]) for r in pieces]
    pairs += [(cls_in, cls), (cot_in, cot)]
    copies = [pltpu.make_async_copy(a, b, sems.at[i]) for i, (a, b) in enumerate(pairs)]
    for cp in copies:
        cp.start()
    for cp in copies[:2]:
        cp.wait()
    sub_v, dep_v = sub[...], dep[...]
    for z in range(64):
        if z % 16 == 0:
            copies[2 + z // 16].wait()
        base = jnp.where(z < sub_v, 1.0, 0.45)
        sg = 0.5 + jax.nn.sigmoid(temp[8 * z : 8 * z + 8])
        cond[8 * z : 8 * z + 8] = jnp.where(z < dep_v, base * sg, 0.0)
    low, high = wall_terms()
    base_z = lax.broadcasted_iota(jnp.int32, (8, 128), 0)
    for chunk in range(8):
        zi = base_z + 8 * chunk
        k = [cond[pl.ds(64 * chunk + x, 8, stride=8), :] for x in range(8)]
        s = [jnp.where(zi < sub_v[x : x + 1], 1.0, 0.6) for x in range(8)]
        s[0] = s[0] + low
        s[7] = s[7] + high
        c = [R * jnp.minimum(k[x], k[x + 1]) for x in range(7)] + [None]
        for i, v in enumerate((k[0], k[7]) + chain_matrix(c, s)):
            planes[i, 8 * chunk : 8 * chunk + 8] = v
    split_halves(planes, keep, send)
    for cp in copies[6:]:
        cp.wait()


def first_kernel(cot, sub, dep, cls, cond, ypack, fac, tie_out, mid, tr):
    me_y = lax.axis_index("gy")
    sub_v, dep_v = sub[...], dep[...]
    top = film_top(cls[...])
    k, cap, s = [], [], []
    for z in range(64):
        k.append(cond[8 * z : 8 * z + 8])
        cap.append(jnp.where(z < sub_v, 1.0, 0.6))
        film = top * (dep_v - 1 == z).astype(F32)
        if z == 0:
            film = film + BOTTOM
        s.append(cap[z] + R * film)
    c = [R * jnp.minimum(k[z], k[z + 1]) for z in range(63)] + [None]
    d = [cot[8 * z : 8 * z + 8] for z in range(64)]
    g, q, levels, _, _ = reduce_chain(c, s, d, False)
    u = expand_chain(q * recip(g), levels, None, None)
    for z in range(64):
        tr[8 * z : 8 * z + 8] = cap[z] * u[z]

    def turned(rows, dst, q):
        block = jnp.transpose(rows)
        for h in range(2):
            dst[pl.ds(4 * h + q, 64, stride=8), :] = block[64 * h : 64 * h + 64]

    subf = sub_v.astype(F32)
    upper = (lax.broadcasted_iota(jnp.int32, (128, 128), 0) & 1) == 1
    for q in range(4):
        turned(cond[pl.ds(q, 128, stride=4), :], mid.at[0], q)
        turned(tr[pl.ds(q, 128, stride=4), :], mid.at[1], q)
        turned(jnp.where(upper, subf[q + 4 : q + 5], subf[q : q + 1]), mid.at[2], q)
    z_lane = (lax.broadcasted_iota(jnp.int32, (8, 128), 1) >> 1).astype(F32)
    row = lax.broadcasted_iota(jnp.int32, (8, 128), 0)
    ky, sy, dy = [], [], []
    for y in range(64):
        ky.append(mid[0, 8 * y : 8 * y + 8])
        dy.append(mid[1, 8 * y : 8 * y + 8])
        sy.append(jnp.where(z_lane < mid[2, 8 * y : 8 * y + 8], 1.0, 0.6))
    low = jnp.where(me_y == 0, R * SIDE, 0.0)
    high = jnp.where(me_y == 7, R * SIDE, 0.0)
    sy[0] = sy[0] + jnp.where(row < 4, low, 0.0)
    sy[63] = sy[63] + jnp.where(row >= 4, high, 0.0)
    cy = [R * jnp.minimum(ky[y], ky[y + 1]) for y in range(63)] + [None]
    g, q, levels, (p, zz, t), ties = reduce_chain(cy, sy, dy, True)
    put_levels(fac, levels)
    for lev in range(NLEV):
        tie_out[lev] = ties[lev]
    kf, kl = ky[0], ky[63]
    side_a = tuple(v[0:4] for v in (kf, kl, zz, t, g, p, q))
    side_b = tuple(v[4:8] for v in (kf, kl, zz, t, g, p, q))
    merged, saved = merge_ports(side_a, side_b)
    for i, v in enumerate(saved):
        tie_out[NLEV + i, 0:4] = v
    lower = lax.broadcasted_iota(jnp.int32, (4, 128), 1) < 64
    edges = jnp.where(lower, mid[2, 0:4], mid[2, 508:512])
    pack = jnp.concatenate(list(merged) + [edges], axis=0)
    for n in range(8):
        ypack[n] = pack


def x_chain(k, cap, d):
    low, high = wall_terms()
    s = list(cap)
    s[0] = s[0] + low
    s[7] = s[7] + high
    c = [R * jnp.minimum(k[x], k[x + 1]) for x in range(7)] + [None]
    g, q, levels, (p, z, t), tie = reduce_chain(c, s, d, True)
    return levels, tie, (k[0], k[7], z, t, g, p, q)


def x_rows(half, cond, planes, subf, out, xfac):
    base_z = lax.broadcasted_iota(jnp.int32, (8, 128), 0)
    for chunk in range(4):
        zi = base_z + (32 * half + 8 * chunk)
        k, cap, d = [], [], []
        for x in range(8):
            at = pl.ds(256 * half + (64 * chunk + x), 8, stride=8)
            k.append(cond[at, :])
            cap.append(jnp.where(zi < subf[x : x + 1], 1.0, 0.6))
            d.append(cap[x] * planes[at, :])
        levels, tie, port = x_chain(k, cap, d)
        store_x(xfac.at[chunk], levels, tie)
        for i in range(2):
            out[32 * i + 8 * chunk : 32 * i + 8 * chunk + 8] = port[5 + i]


def keep_kernel(cond, planes, sub, keep, xfac):
    x_rows(own_half(), cond, planes, sub[...], keep, xfac)


def second_kernel(gat, fac, ties, cond, sub, send, edge, xfac, xhfac, kh_out, planes, pick, flat):
    me_y = lax.axis_index("gy")
    seg = [[gat[n, 4 * i : 4 * i + 4] for i in range(8)] for n in range(8)]
    gam, rhs = seg[0][4], seg[0][6]
    down, links = [None], [None]
    for n in range(1, 8):
        kf, kl, z, t, g, p, q = seg[n][:7]
        link = R * jnp.minimum(seg[n - 1][1], kf)
        lk = link * recip(1.0 + link * z)
        inv = recip(gam + lk)
        h = inv * (rhs + lk * p)
        lt = lk * t
        down.append((h, lt * inv))
        links.append(lk)
        rhs = q + lt * (h - p)
        gam = g + lt * t * (gam * inv)
    u = [None] * 8
    u[7] = rhs * recip(gam)
    for n in range(7, 0, -1):
        u[n - 1] = down[n][0] + down[n][1] * u[n]
    zero4 = jnp.zeros((4, 128), F32)
    fl, uf = [zero4], [None]
    for n in range(1, 8):
        kf, kl, z, t, g, p, q = seg[n][:7]
        fl.append(links[n] * (u[n - 1] - p - t * u[n]))
        uf.append(p + z * fl[n] + t * u[n])
    for n in range(8):
        rows = [fl[n], u[n]]
        if n:
            rows += [u[n - 1], seg[n - 1][1], seg[n - 1][7]]
        else:
            rows += [zero4, zero4, zero4]
        if n < 7:
            rows += [uf[n + 1], seg[n + 1][0], seg[n + 1][7]]
        else:
            rows += [zero4, zero4, zero4]
        for i, v in enumerate(rows):
            pick[n, 4 * i : 4 * i + 4] = v
    mine = [pick[me_y, 4 * i : 4 * i + 4] for i in range(8)]
    flux, u_b = mine[0], mine[1]
    saved = tuple(ties[NLEV + i, 0:4] for i in range(6))
    u_a, flux_b = descend(saved, flux, u_b)
    flux8 = jnp.concatenate([flux, flux_b], axis=0)
    last8 = jnp.concatenate([u_a, u_b], axis=0)
    levels = get_levels(lambda kind, i: fac[kind, i], 32)
    u_nodes = expand_chain(last8, levels, [ties[i] for i in range(NLEV)], flux8)
    for y in range(64):
        flat[8 * y : 8 * y + 8] = u_nodes[y]
    subf = sub[...]
    for q in range(4):
        planes[pl.ds(q, 128, stride=4), :] = jnp.transpose(
            jnp.concatenate([flat[pl.ds(q, 64, stride=8), :], flat[pl.ds(4 + q, 64, stride=8), :]], axis=0)
        )

    lane = lax.broadcasted_iota(jnp.int32, (4, 128), 1)
    even = (lane & 1) == 0
    z_of = (lane >> 1).astype(F32)
    cap_l = jnp.where(z_of < jnp.where(lane < 64, pltpu.roll(mine[4], 64, 1), mine[4]), 1.0, 0.6)
    cap_r = jnp.where(z_of < jnp.where(lane < 64, mine[7], pltpu.roll(mine[7], 64, 1)), 1.0, 0.6)

    def both(left, right):
        low = jnp.where(even, left, pltpu.roll(right, 127, 1))
        high = jnp.where(even, pltpu.roll(left, 127, 1), pltpu.roll(right, 126, 1))
        return [low[x : x + 1] for x in range(4)] + [high[x : x + 1] for x in range(4)]

    dh, kh, caph = both(cap_l * mine[2], cap_r * mine[5]), both(mine[3], mine[6]), both(cap_l, cap_r)
    for x in range(8):
        kh_out[x : x + 1] = kh[x]

    levels, tie, port = x_chain(kh, caph, dh)
    store_x(xhfac, levels, tie)
    for i in range(7):
        send[64 + i : 65 + i] = port[i]
        edge[i : i + 1] = port[i]
    x_rows(1 - own_half(), cond, planes, subf, send, xfac)


def store_x(ref, levels, tie):
    for lev, triple in enumerate(levels):
        base, n = node_order(4, lev)
        for kind in range(3):
            for j in range(n):
                if triple[kind][j] is not None:
                    ref[7 * kind + base + j] = triple[kind][j]
    for lev in range(3):
        ref[21 + lev] = tie[lev]


def load_x(ref):
    levels = get_levels(lambda kind, i: ref[7 * kind + i], 4)
    return levels, [ref[21 + lev] for lev in range(3)]


def read_pack(ref, n):
    main = tuple(ref[32 * i : 32 * i + 32] for i in range(n))
    edge = tuple(ref[32 * n + i : 32 * n + i + 1] for i in range(n))
    return main, edge


def write_pack(ref, main, edge):
    n = len(main)
    for i in range(n):
        ref[32 * i : 32 * i + 32] = main[i]
        ref[32 * n + i : 32 * n + i + 1] = edge[i]


def order(right, mine, theirs):
    a = tuple(jnp.where(right, t, m) for m, t in zip(mine, theirs))
    b = tuple(jnp.where(right, m, t) for m, t in zip(mine, theirs))
    return a, b


def planes_of(ref, n):
    return tuple(ref[32 * i : 32 * i + 32] for i in range(n))


def put_planes(ref, values):
    for i, v in enumerate(values):
        ref[32 * i : 32 * i + 32] = v


def spots():
    me_x = lax.axis_index("gx")
    return [lax.rem(lax.div(me_x, bit), 2) == 1 for bit in (1, 2, 4)]


def core_matrix_kernel(mine, theirs, merged_out, coef_out):
    odd, _, _ = spots()
    merged, coefs = port_coefs(*order(odd, planes_of(mine, 5), planes_of(theirs, 5)))
    put_planes(merged_out, merged)
    put_planes(coef_out, coefs)


def ring_matrix_kernel(own, mid, far, near, merged_out, mine_out, other_out, ring_out, top_out):
    _, right, upper = spots()
    packs = [planes_of(r, 5) for r in (own, near, mid, far)]
    mine, mine_c = port_coefs(*order(right, packs[0], packs[1]))
    other, other_c = port_coefs(*order(right, packs[2], packs[3]))
    merged, ring_c = port_coefs(*order(upper, mine, other))
    put_planes(merged_out, merged)
    put_planes(mine_out, mine_c)
    put_planes(other_out, other_c)
    put_planes(ring_out, ring_c)
    last = lax.div(lax.axis_index("gx"), 8) == 1
    kf, kl, z, tt, g = merged
    put_planes(top_out, (jnp.where(last, z + tt * (tt * recip(g)), g), jnp.where(last, kf, kl)))


def read_sides(ref):
    main = (ref[0:32], ref[32:64])
    edge = tuple(ref[64 + i : 65 + i] for i in range(7))
    return main, edge


def core_kernel(mine, edge_mine, theirs, coefs, merged_out, saved_out):
    odd, _, _ = spots()
    m = (mine[0:32], mine[32:64]), tuple(edge_mine[i : i + 1] for i in range(7))
    t = read_sides(theirs)
    values, saved = port_values(planes_of(coefs, 7), *order(odd, m[0], t[0]))
    edge, edge_saved = merge_ports(*order(odd, m[1], t[1]))
    put_planes(merged_out, values)
    for i in range(7):
        merged_out[64 + i : 65 + i] = edge[i]
    write_pack(saved_out, saved, edge_saved)


def ring_kernel(own, mid, far, near, matrix, mine_c, other_c, ring_c, merged_out, pair_out, saved_out, top_out):
    _, right, upper = spots()
    last = lax.div(lax.axis_index("gx"), 8) == 1
    main, edge = zip(*[read_sides(r) for r in (own, near, mid, far)])
    mine, pair = port_values(planes_of(mine_c, 7), *order(right, main[0], main[1]))
    other, _ = port_values(planes_of(other_c, 7), *order(right, main[2], main[3]))
    values, saved = port_values(planes_of(ring_c, 7), *order(upper, mine, other))
    e_mine, e_pair = merge_ports(*order(right, edge[0], edge[1]))
    e_other, _ = merge_ports(*order(right, edge[2], edge[3]))
    e_merged, e_saved = merge_ports(*order(upper, e_mine, e_other))
    outs = [planes_of(matrix, 5) + values, e_merged]
    write_pack(merged_out, *outs)
    kf, kl, z, tt, g, p, q = outs[0]
    top_out[0:32] = jnp.where(last, p + tt * recip(g) * q, q)
    kf, kl, z, tt, g, p, q = e_merged
    tg = tt * recip(g)
    for i, (a, b) in enumerate(((z + tt * tg, g), (p + tg * q, q), (kf, kl))):
        top_out[32 + i : 33 + i] = jnp.where(last, a, b)
    write_pack(pair_out, pair, e_pair)
    write_pack(saved_out, saved, e_saved)


def read_top(matrix, values):
    main = (matrix[0:32], values[0:32], matrix[32:64])
    return main, tuple(values[32 + i : 33 + i] for i in range(3))


def top_kernel(merged, near_m, near, theirs_m, theirs, sv1, sv2, sv3, own, send):
    me_x = lax.axis_index("gx")
    far = lax.div(me_x, 8) == 1
    mm = read_pack(merged, 7)
    n, t = read_top(near_m, near), read_top(theirs_m, theirs)
    saved = [read_pack(r, 6) for r in (sv1, sv2, sv3)]
    final = []
    for part in range(2):
        (ga, qa, ka), (zb, pb, kb) = order(far, n[part], t[part])
        link = R * jnp.minimum(ka, kb)
        lk = link * recip(1.0 + link * zb)
        u_a = (qa + lk * pb) * recip(ga + lk)
        kf, kl, z, tt, g, p, q = mm[part]
        flux = jnp.where(far, lk * (u_a - pb), 0.0)
        u = jnp.where(far, (q + tt * flux) * recip(g), u_a)
        for bit, lev in ((4, 2), (2, 1)):
            right = lax.rem(lax.div(me_x, bit), 2) == 1
            ua, fb = descend(saved[lev][part], flux, u)
            flux = jnp.where(right, fb, flux)
            u = jnp.where(right, u, ua)
        ua, fb = descend(saved[0][part], flux, u)
        odd = lax.rem(me_x, 2) == 1
        final.append((jnp.where(odd, fb, flux), jnp.where(odd, u, ua), jnp.where(odd, flux, fb), jnp.where(odd, ua, u)))
    write_pack(own, final[0][:2], final[1][:2])
    send[0:32] = final[0][2]
    send[32:64] = final[0][3]


def coef_kernel(cond, kh, planes, cot, sub, dep, cls, k_y, k_l, k_z, k_s, base):
    me_y = lax.axis_index("gy")
    sub_v, dep_v, kh_v = sub[...], dep[...], kh[...]
    top = film_top(cls[...])
    lane = lax.broadcasted_iota(jnp.int32, (8, 128), 1)
    first, final = lane == 0, lane == 127
    film_y = jnp.where(first & (me_y == 0), SIDE, 0.0) + jnp.where(final & (me_y == 7), SIDE, 0.0)
    for z in range(64):
        rows = slice(8 * z, 8 * z + 8)
        k = cond[rows]
        k_h = pltpu.roll(kh_v, 128 - 2 * z, 1) if z else kh_v
        k_y[rows] = (2.0 * R) * jnp.minimum(k, jnp.where(final, k_h, pltpu.roll(k, 127, 1)))
        k_l[rows] = (2.0 * R) * jnp.minimum(k, k_h)
        if z < 63:
            k_z[rows] = (2.0 * R) * jnp.minimum(k, cond[8 * z + 8 : 8 * z + 16])
        else:
            k_z[rows] = jnp.zeros((8, 128), F32)
        film = film_y + top * (dep_v - 1 == z).astype(F32)
        if z == 0:
            film = film + BOTTOM
        cap = jnp.where(z < sub_v, 1.0, 0.6)
        k_s[rows] = 2.0 * cap - (2.0 * R) * film
        base[rows] = cot[rows] - 2.0 * (cap * planes[rows])


def expand_rows(xfac, flux, last, s1):
    for chunk in range(4):
        rows = slice(8 * chunk, 8 * chunk + 8)
        levels, tie = load_x(xfac.at[chunk])
        u = expand_chain(last[rows], levels, tie, flux[rows])
        for x in range(8):
            s1[pl.ds(64 * chunk + x, 8, stride=8), :] = u[x]


def stencil(half, uh, s1, k_y, k_l, k_z, k_s, base, sub_v, below, above, src, out, done=None):
    lane = lax.broadcasted_iota(jnp.int32, (8, 128), 1)
    first, final = lane == 0, lane == 127
    up = below
    for i in range(32):
        rows = slice(8 * i, 8 * i + 8)
        at = pl.ds(pl.multiple_of(256 * half + 8 * i, 8), 8)
        s = s1[rows]
        s_h = pltpu.roll(uh, 128 - 2 * i, 1) if i else uh
        f_y = k_y[at, :] * (jnp.where(final, s_h, pltpu.roll(s, 127, 1)) - s)
        f_l = k_l[at, :] * (s - s_h)
        total = f_y - jnp.where(first, f_l, pltpu.roll(f_y, 1, 1))
        f_z = k_z[at, :] * (s1[8 * i + 8 : 8 * i + 16] - s) if i < 31 else above
        if f_z is not None:
            total = total + f_z
        if up is not None:
            total = total - up
        up = f_z
        src[rows] = jnp.where(32 * half + i < sub_v, 1.0, 0.6) * s
        out[rows] = base[at, :] + k_s[at, :] * s + total
        if done is not None and i & 7 == 7:
            done(i // 8)


def own_kernel(own, xfac, xhfac, k_y, k_l, k_z, k_s, base, sub, s1, src, out, uh_out):
    half = own_half()
    levels, tie = load_x(xhfac)
    uh = jnp.concatenate(expand_chain(own[65:66], levels, tie, own[64:65]), axis=0)
    turned = pltpu.roll(uh, 64, 1)
    uh_out[...] = jnp.where(half == 1, uh, turned)
    expand_rows(xfac, own.at[0:32], own.at[32:64], s1)
    uh = jnp.where(half == 1, turned, uh)
    stencil(half, uh, s1, k_y, k_l, k_z, k_s, base, sub[...], None, None, src, out)


def last_kernel(
    got, xfac, k_y, k_l, k_z, k_s, base, sub, s_own, src_own, out_own, uh, temp_out, src_out, s1, ends, t_buf, s_buf, sems
):
    mine = own_half()
    half = 1 - mine
    copies = []

    def send(buf, rows, out, start):
        size = rows.stop - rows.start
        cp = pltpu.make_async_copy(buf.at[rows], out.at[pl.ds(pl.multiple_of(start, 8), size)], sems.at[len(copies)])
        cp.start()
        copies.append(cp)

    send(src_own, slice(0, 256), src_out, 256 * mine)
    send(out_own, slice(8, 248), temp_out, 256 * mine + 8)
    expand_rows(xfac, got.at[0:32], got.at[32:64], s1)
    inner, outer = s_own[248:256], s_own[0:8]
    low = jnp.where(half == 0, s1[248:256], inner)
    high = jnp.where(half == 0, outer, s1[0:8])
    flux = k_z[248:256] * (high - low)
    ends[0:8] = out_own[0:8] - jnp.where(mine == 1, flux, 0.0)
    ends[8:16] = out_own[248:256] + jnp.where(mine == 0, flux, 0.0)
    send(ends, slice(0, 8), temp_out, 256 * mine)
    send(ends, slice(8, 16), temp_out, 256 * mine + 248)

    def done(piece):
        rows = slice(64 * piece, 64 * piece + 64)
        send(s_buf, rows, src_out, 256 * half + 64 * piece)
        send(t_buf, rows, temp_out, 256 * half + 64 * piece)

    below, above = jnp.where(half == 1, flux, 0.0), jnp.where(half == 0, flux, 0.0)
    stencil(half, uh[...], s1, k_y, k_l, k_z, k_s, base, sub[...], below, above, s_buf, t_buf, done)
    for cp in copies:
        cp.wait()


VMEM = pl.BlockSpec(memory_space=pltpu.VMEM)
HBM = pl.BlockSpec(memory_space=pltpu.MemorySpace.HBM)


def call(kernel, outs, scratch, name, *args, far_in=0, far_out=0, sems=0):
    shapes = [s if isinstance(s, jax.ShapeDtypeStruct) else jax.ShapeDtypeStruct(s, F32) for s in outs]
    scr = [pltpu.VMEM(s, F32) for s in scratch]
    args = [pltpu.with_memory_space_constraint(a, pltpu.MemorySpace.HBM) if i < far_in else a for i, a in enumerate(args)]
    if sems:
        scr.append(pltpu.SemaphoreType.DMA((sems,)))
    return pl.pallas_call(
        kernel,
        out_shape=shapes,
        in_specs=[HBM if i < far_in else VMEM for i in range(len(args))],
        out_specs=[HBM if i < far_out else VMEM for i in range(len(outs))],
        scratch_shapes=scr,
        compiler_params=pltpu.CompilerParams(vmem_limit_bytes=40 * 1024 * 1024),
        name=name,
    )(*args)


def swap(v, bit):
    return lax.ppermute(v, "gx", [(i, i ^ bit) for i in range(16)])


def body(cotangent, saved_temp, substrate_top, deposit_top, top_class):
    cot = cotangent.reshape(512, 128)
    temp = saved_temp.reshape(512, 128)
    small = jax.ShapeDtypeStruct((8, 128), jnp.int32)
    cond, keep_m, send_m, cot, sub, dep, cls = call(
        fields_kernel,
        [(512, 128), (160, 128), (160, 128), (512, 128), small, small, small],
        [(512, 128), (5, 64, 128)],
        "fields",
        cot, temp, substrate_top, deposit_top, top_class,
        far_in=5, sems=8,
    )
    other_m = swap(send_m, 1)
    ypack, fac, ties = call(
        first_kernel,
        [(8, 32, 128), (3, 63, 8, 128), (12, 8, 128)],
        [(3, 512, 128), (512, 128)],
        "first",
        cot, sub, dep, cls, cond,
    )
    mm, core_c = call(core_matrix_kernel, [(160, 128), (224, 128)], [], "matrix_core", keep_m, other_m)
    mm, ypack = lax.optimization_barrier((mm, ypack))
    gat = lax.all_to_all(ypack, "gy", split_axis=0, concat_axis=0, tiled=True)
    ring_m = [swap(mm, bit) for bit in (4, 7, 3)]
    send, edge, xfac, xhfac, kh, planes = call(
        second_kernel,
        [(72, 128), (8, 128), (4, 24, 8, 128), (24, 1, 128), (8, 128), (512, 128)],
        [(8, 32, 128), (512, 128)],
        "second",
        gat, fac, ties, cond, sub,
    )
    keep, xfac_own = call(keep_kernel, [(64, 128), (4, 24, 8, 128)], [], "keep_rows", cond, planes, sub)
    m1, sv1 = call(core_kernel, [(72, 128), (200, 128)], [], "merge_core", keep, edge, swap(send, 1), core_c)
    ring_v = [swap(m1, bit) for bit in (4, 7, 3)]
    matrix, mine_c, other_c, ring_c, near_m = call(
        ring_matrix_kernel, [(160, 128)] + [(224, 128)] * 3 + [(64, 128)], [], "matrix_ring", mm, *ring_m
    )
    opposite_m = swap(near_m, 9)
    m3, sv2, sv3, near = call(
        ring_kernel,
        [(232, 128), (200, 128), (200, 128), (40, 128)],
        [],
        "merge_ring",
        m1, *ring_v, matrix, mine_c, other_c, ring_c,
    )
    sv3, kh = lax.optimization_barrier((sv3, kh))
    coefs = call(coef_kernel, [(512, 128)] * 5, [], "coef", cond, kh, planes, cot, sub, dep, cls)
    opposite = swap(near, 9)
    sv3, coefs = lax.optimization_barrier((sv3, coefs))
    own, out = call(top_kernel, [(72, 128), (64, 128)], [], "top", m3, near_m, near, opposite_m, opposite, sv1, sv2, sv3)
    got = swap(out, 1)
    part = call(
        own_kernel,
        [(256, 128), (256, 128), (256, 128), (8, 128)],
        [],
        "own_rows",
        own, xfac_own, xhfac, *coefs, sub,
    )
    grad_temp, grad_source = call(
        last_kernel,
        [(512, 128), (512, 128)],
        [(256, 128), (16, 128), (256, 128), (256, 128)],
        "last",
        got, xfac, *coefs, sub, *part,
        far_out=2, sems=12,
    )
    return grad_temp.reshape(cotangent.shape), grad_source.reshape(cotangent.shape)


def solution(mesh):
    in_specs = (
        P(None, "gx", "gy"),
        P(None, "gx", "gy"),
        P("gx", "gy"),
        P("gx", "gy"),
        P("gx", "gy"),
    )
    out_specs = (P(None, "gx", "gy"), P(None, "gx", "gy"))
    return jax.shard_map(body, mesh=mesh, in_specs=in_specs, out_specs=out_specs, check_vma=False)
```

```python
import jax
import jax.numpy as jnp
from jax import lax
from jax.experimental import pallas as pl
from jax.experimental.pallas import tpu as pltpu
from jax.sharding import PartitionSpec as P

R = 1000.0
SIDE = 0.3
BOTTOM = 0.5
TOPS = (0.05, 0.25, 0.8, 2.0)
F32 = jnp.float32
NLEV = 6


def recip(v):
    return 1.0 / v


def reduce_chain(c, s, d, track):
    levels, port, ties = [], None, []
    while len(s) > 1:
        half = len(s) // 2
        ml, mr, dv = [], [], []
        for j in range(half):
            i = 2 * j
            total = s[i] + c[i]
            if j:
                total = total + c[i - 1]
            inv = recip(total)
            mr.append(c[i] * inv)
            ml.append(c[i - 1] * inv if j else None)
            dv.append(d[i] * inv)
            if track and j == 0:
                if port is None:
                    port = [dv[0], inv, mr[0]]
                    ties.append(inv)
                else:
                    p, z, t = port
                    tie = t * inv
                    ties.append(tie)
                    port = [p + t * dv[0], z + t * tie, t * mr[0]]
        ns, nd, nc = [], [], []
        for j in range(half):
            e, o = 2 * j, 2 * j + 1
            sv = s[o] + mr[j] * s[e]
            dn = d[o] + mr[j] * d[e]
            if j + 1 < half:
                sv = sv + ml[j + 1] * s[e + 2]
                dn = dn + ml[j + 1] * d[e + 2]
                nc.append(ml[j + 1] * c[e + 2])
            ns.append(sv)
            nd.append(dn)
        levels.append((dv, ml, mr))
        c, s, d = nc, ns, nd
    return s[0], d[0], levels, port, ties


def expand_chain(u_last, levels, ties, flux):
    u = [u_last]
    for lev in range(len(levels) - 1, -1, -1):
        dv, ml, mr = levels[lev]
        out = []
        for j in range(len(u)):
            even = dv[j] + mr[j] * u[j]
            if j:
                even = even + ml[j] * u[j - 1]
            elif ties is not None:
                even = even + ties[lev] * flux
            out += [even, u[j]]
        u = out
    return u


def port_coefs(a, b):
    kfa, kla, za, ta, ga = a
    kfb, klb, zb, tb, gb = b
    link = R * jnp.minimum(kla, kfb)
    lk = link * recip(1.0 + link * zb)
    inv = recip(ga + lk)
    ti = ta * inv
    lt = lk * tb
    w = lt * inv
    merged = (kfa, klb, za + ta * ti, ta * w, gb + lt * tb * (ga * inv))
    return merged, (inv, lk, ta, lt, ti, w, tb)


def port_values(coefs, a, b):
    inv, lk, ta, lt, ti, w, tb = coefs
    pa, qa = a
    pb, qb = b
    h = inv * (qa + lk * pb)
    return (pa + ta * h, qb + lt * (h - pb)), (h, ti, w, lk, pb, tb)


def merge_ports(a, b):
    matrix, coefs = port_coefs(a[:5], b[:5])
    values, saved = port_values(coefs, a[5:], b[5:])
    return matrix + values, saved


def descend(saved, flux, u_b):
    h, ti, w, lk, pb, tb = saved
    u_a = h + ti * flux + w * u_b
    flux_b = lk * (u_a - pb - tb * u_b)
    return u_a, flux_b


def film_top(cls):
    total = jnp.zeros(cls.shape, F32)
    for n in range(4):
        total = total + TOPS[n] * (cls == n).astype(F32)
    return total


def node_order(half, lev):
    base, n = 0, half
    for _ in range(lev):
        base += n
        n //= 2
    return base, n


def put_levels(ref, levels):
    half = len(levels[0][0])
    for lev, triple in enumerate(levels):
        base, n = node_order(half, lev)
        for kind in range(3):
            for j in range(n):
                if triple[kind][j] is not None:
                    ref[kind, base + j] = triple[kind][j]


def get_levels(read, half):
    levels, lev = [], 0
    while half >> lev:
        base, n = node_order(half, lev)
        levels.append(
            tuple([None if kind == 1 and j == 0 else read(kind, base + j) for j in range(n)] for kind in range(3))
        )
        lev += 1
    return levels


def chain_matrix(c, s):
    z = t = None
    while len(s) > 1:
        half = len(s) // 2
        ml, mr = [None] * half, [None] * half
        for j in range(half):
            i = 2 * j
            inv = recip(s[i] + c[i] + c[i - 1] if j else s[i] + c[i])
            mr[j] = c[i] * inv
            if j:
                ml[j] = c[i - 1] * inv
            elif z is None:
                z, t = inv, mr[0]
            else:
                z, t = z + t * (t * inv), t * mr[0]
        ns, nc = [], []
        for j in range(half):
            e = 2 * j
            sv = s[e + 1] + mr[j] * s[e]
            if j + 1 < half:
                sv = sv + ml[j + 1] * s[e + 2]
                nc.append(ml[j + 1] * c[e + 2])
            ns.append(sv)
        c, s = nc, ns
    return z, t, s[0]


def wall_terms():
    me_x = lax.axis_index("gx")
    return jnp.where(me_x == 0, R * SIDE, 0.0), jnp.where(me_x == 15, R * SIDE, 0.0)


def own_half():
    me_x = lax.axis_index("gx")
    return lax.rem(me_x + lax.div(me_x, 2) + lax.div(me_x, 8), 2)


def split_halves(planes, keep, send):
    core = own_half()
    for i in range(planes.shape[0]):
        keep[32 * i : 32 * i + 32] = planes[i, pl.ds(pl.multiple_of(32 * core, 32), 32), :]
        send[32 * i : 32 * i + 32] = planes[i, pl.ds(pl.multiple_of(32 - 32 * core, 32), 32), :]


def fields_kernel(cot_in, temp_in, sub_in, dep_in, cls_in, cond, keep, send, cot, sub, dep, cls, temp, planes, sems):
    pieces = [slice(64 * i, 64 * i + 64) for i in range(8)]
    pairs = [(sub_in, sub), (dep_in, dep)] + [(temp_in.at[r], temp.at[r]) for r in pieces]
    pairs += [(cls_in, cls), (cot_in, cot)]
    copies = [pltpu.make_async_copy(a, b, sems.at[i]) for i, (a, b) in enumerate(pairs)]
    for cp in copies:
        cp.start()
    for cp in copies[:2]:
        cp.wait()
    sub_v, dep_v = sub[...], dep[...]
    for z in range(64):
        if z % 8 == 0:
            copies[2 + z // 8].wait()
        base = jnp.where(z < sub_v, 1.0, 0.45)
        sg = 0.5 + jax.nn.sigmoid(temp[8 * z : 8 * z + 8])
        cond[8 * z : 8 * z + 8] = jnp.where(z < dep_v, base * sg, 0.0)
    low, high = wall_terms()
    base_z = lax.broadcasted_iota(jnp.int32, (8, 128), 0)
    for chunk in range(8):
        zi = base_z + 8 * chunk
        k = [cond[pl.ds(64 * chunk + x, 8, stride=8), :] for x in range(8)]
        s = [jnp.where(zi < sub_v[x : x + 1], 1.0, 0.6) for x in range(8)]
        s[0] = s[0] + low
        s[7] = s[7] + high
        c = [R * jnp.minimum(k[x], k[x + 1]) for x in range(7)] + [None]
        for i, v in enumerate((k[0], k[7]) + chain_matrix(c, s)):
            planes[i, 8 * chunk : 8 * chunk + 8] = v
    split_halves(planes, keep, send)
    for cp in copies[10:]:
        cp.wait()


def first_kernel(cot, sub, dep, cls, cond, ypack, fac, tie_out, mid, tr):
    me_y = lax.axis_index("gy")
    sub_v, dep_v = sub[...], dep[...]
    top = film_top(cls[...])
    k, cap, s = [], [], []
    for z in range(64):
        k.append(cond[8 * z : 8 * z + 8])
        cap.append(jnp.where(z < sub_v, 1.0, 0.6))
        film = top * (dep_v - 1 == z).astype(F32)
        if z == 0:
            film = film + BOTTOM
        s.append(cap[z] + R * film)
    c = [R * jnp.minimum(k[z], k[z + 1]) for z in range(63)] + [None]
    d = [cot[8 * z : 8 * z + 8] for z in range(64)]
    g, q, levels, _, _ = reduce_chain(c, s, d, False)
    u = expand_chain(q * recip(g), levels, None, None)
    for z in range(64):
        tr[8 * z : 8 * z + 8] = cap[z] * u[z]

    def turned(rows, dst, q):
        block = jnp.transpose(rows)
        for h in range(2):
            dst[pl.ds(4 * h + q, 64, stride=8), :] = block[64 * h : 64 * h + 64]

    subf = sub_v.astype(F32)
    upper = (lax.broadcasted_iota(jnp.int32, (128, 128), 0) & 1) == 1
    for q in range(4):
        turned(cond[pl.ds(q, 128, stride=4), :], mid.at[0], q)
        turned(tr[pl.ds(q, 128, stride=4), :], mid.at[1], q)
        turned(jnp.where(upper, subf[q + 4 : q + 5], subf[q : q + 1]), mid.at[2], q)
    z_lane = (lax.broadcasted_iota(jnp.int32, (8, 128), 1) >> 1).astype(F32)
    row = lax.broadcasted_iota(jnp.int32, (8, 128), 0)
    ky, sy, dy = [], [], []
    for y in range(64):
        ky.append(mid[0, 8 * y : 8 * y + 8])
        dy.append(mid[1, 8 * y : 8 * y + 8])
        sy.append(jnp.where(z_lane < mid[2, 8 * y : 8 * y + 8], 1.0, 0.6))
    low = jnp.where(me_y == 0, R * SIDE, 0.0)
    high = jnp.where(me_y == 7, R * SIDE, 0.0)
    sy[0] = sy[0] + jnp.where(row < 4, low, 0.0)
    sy[63] = sy[63] + jnp.where(row >= 4, high, 0.0)
    cy = [R * jnp.minimum(ky[y], ky[y + 1]) for y in range(63)] + [None]
    g, q, levels, (p, zz, t), ties = reduce_chain(cy, sy, dy, True)
    put_levels(fac, levels)
    for lev in range(NLEV):
        tie_out[lev] = ties[lev]
    kf, kl = ky[0], ky[63]
    side_a = tuple(v[0:4] for v in (kf, kl, zz, t, g, p, q))
    side_b = tuple(v[4:8] for v in (kf, kl, zz, t, g, p, q))
    merged, saved = merge_ports(side_a, side_b)
    for i, v in enumerate(saved):
        tie_out[NLEV + i, 0:4] = v
    lower = lax.broadcasted_iota(jnp.int32, (4, 128), 1) < 64
    edges = jnp.where(lower, mid[2, 0:4], mid[2, 508:512])
    pack = jnp.concatenate(list(merged) + [edges], axis=0)
    for n in range(8):
        ypack[n] = pack


def x_chain(k, cap, d):
    low, high = wall_terms()
    s = list(cap)
    s[0] = s[0] + low
    s[7] = s[7] + high
    c = [R * jnp.minimum(k[x], k[x + 1]) for x in range(7)] + [None]
    g, q, levels, (p, z, t), tie = reduce_chain(c, s, d, True)
    return levels, tie, (k[0], k[7], z, t, g, p, q)


def x_rows(half, cond, planes, subf, out, xfac):
    base_z = lax.broadcasted_iota(jnp.int32, (8, 128), 0)
    for chunk in range(4):
        zi = base_z + (32 * half + 8 * chunk)
        k, cap, d = [], [], []
        for x in range(8):
            at = pl.ds(256 * half + (64 * chunk + x), 8, stride=8)
            k.append(cond[at, :])
            cap.append(jnp.where(zi < subf[x : x + 1], 1.0, 0.6))
            d.append(cap[x] * planes[at, :])
        levels, tie, port = x_chain(k, cap, d)
        store_x(xfac.at[chunk], levels, tie)
        for i in range(2):
            out[32 * i + 8 * chunk : 32 * i + 8 * chunk + 8] = port[5 + i]


def keep_kernel(cond, planes, sub, keep, xfac):
    x_rows(own_half(), cond, planes, sub[...], keep, xfac)


def second_kernel(gat, fac, ties, cond, sub, send, edge, xfac, xhfac, kh_out, planes, pick, flat):
    me_y = lax.axis_index("gy")
    seg = [[gat[n, 4 * i : 4 * i + 4] for i in range(8)] for n in range(8)]
    gam, rhs = seg[0][4], seg[0][6]
    down, links = [None], [None]
    for n in range(1, 8):
        kf, kl, z, t, g, p, q = seg[n][:7]
        link = R * jnp.minimum(seg[n - 1][1], kf)
        lk = link * recip(1.0 + link * z)
        inv = recip(gam + lk)
        h = inv * (rhs + lk * p)
        lt = lk * t
        down.append((h, lt * inv))
        links.append(lk)
        rhs = q + lt * (h - p)
        gam = g + lt * t * (gam * inv)
    u = [None] * 8
    u[7] = rhs * recip(gam)
    for n in range(7, 0, -1):
        u[n - 1] = down[n][0] + down[n][1] * u[n]
    zero4 = jnp.zeros((4, 128), F32)
    fl, uf = [zero4], [None]
    for n in range(1, 8):
        kf, kl, z, t, g, p, q = seg[n][:7]
        fl.append(links[n] * (u[n - 1] - p - t * u[n]))
        uf.append(p + z * fl[n] + t * u[n])
    for n in range(8):
        rows = [fl[n], u[n]]
        if n:
            rows += [u[n - 1], seg[n - 1][1], seg[n - 1][7]]
        else:
            rows += [zero4, zero4, zero4]
        if n < 7:
            rows += [uf[n + 1], seg[n + 1][0], seg[n + 1][7]]
        else:
            rows += [zero4, zero4, zero4]
        for i, v in enumerate(rows):
            pick[n, 4 * i : 4 * i + 4] = v
    mine = [pick[me_y, 4 * i : 4 * i + 4] for i in range(8)]
    flux, u_b = mine[0], mine[1]
    saved = tuple(ties[NLEV + i, 0:4] for i in range(6))
    u_a, flux_b = descend(saved, flux, u_b)
    flux8 = jnp.concatenate([flux, flux_b], axis=0)
    last8 = jnp.concatenate([u_a, u_b], axis=0)
    levels = get_levels(lambda kind, i: fac[kind, i], 32)
    u_nodes = expand_chain(last8, levels, [ties[i] for i in range(NLEV)], flux8)
    for y in range(64):
        flat[8 * y : 8 * y + 8] = u_nodes[y]
    subf = sub[...]
    for q in range(4):
        planes[pl.ds(q, 128, stride=4), :] = jnp.transpose(
            jnp.concatenate([flat[pl.ds(q, 64, stride=8), :], flat[pl.ds(4 + q, 64, stride=8), :]], axis=0)
        )

    lane = lax.broadcasted_iota(jnp.int32, (4, 128), 1)
    even = (lane & 1) == 0
    z_of = (lane >> 1).astype(F32)
    cap_l = jnp.where(z_of < jnp.where(lane < 64, pltpu.roll(mine[4], 64, 1), mine[4]), 1.0, 0.6)
    cap_r = jnp.where(z_of < jnp.where(lane < 64, mine[7], pltpu.roll(mine[7], 64, 1)), 1.0, 0.6)

    def both(left, right):
        low = jnp.where(even, left, pltpu.roll(right, 127, 1))
        high = jnp.where(even, pltpu.roll(left, 127, 1), pltpu.roll(right, 126, 1))
        return [low[x : x + 1] for x in range(4)] + [high[x : x + 1] for x in range(4)]

    dh, kh, caph = both(cap_l * mine[2], cap_r * mine[5]), both(mine[3], mine[6]), both(cap_l, cap_r)
    for x in range(8):
        kh_out[x : x + 1] = kh[x]

    levels, tie, port = x_chain(kh, caph, dh)
    store_x(xhfac, levels, tie)
    for i in range(7):
        send[64 + i : 65 + i] = port[i]
        edge[i : i + 1] = port[i]
    x_rows(1 - own_half(), cond, planes, subf, send, xfac)


def store_x(ref, levels, tie):
    for lev, triple in enumerate(levels):
        base, n = node_order(4, lev)
        for kind in range(3):
            for j in range(n):
                if triple[kind][j] is not None:
                    ref[7 * kind + base + j] = triple[kind][j]
    for lev in range(3):
        ref[21 + lev] = tie[lev]


def load_x(ref):
    levels = get_levels(lambda kind, i: ref[7 * kind + i], 4)
    return levels, [ref[21 + lev] for lev in range(3)]


def read_pack(ref, n):
    main = tuple(ref[32 * i : 32 * i + 32] for i in range(n))
    edge = tuple(ref[32 * n + i : 32 * n + i + 1] for i in range(n))
    return main, edge


def write_pack(ref, main, edge):
    n = len(main)
    for i in range(n):
        ref[32 * i : 32 * i + 32] = main[i]
        ref[32 * n + i : 32 * n + i + 1] = edge[i]


def order(right, mine, theirs):
    a = tuple(jnp.where(right, t, m) for m, t in zip(mine, theirs))
    b = tuple(jnp.where(right, m, t) for m, t in zip(mine, theirs))
    return a, b


def planes_of(ref, n):
    return tuple(ref[32 * i : 32 * i + 32] for i in range(n))


def put_planes(ref, values):
    for i, v in enumerate(values):
        ref[32 * i : 32 * i + 32] = v


def spots():
    me_x = lax.axis_index("gx")
    return [lax.rem(lax.div(me_x, bit), 2) == 1 for bit in (1, 2, 4)]


def core_matrix_kernel(mine, theirs, merged_out, coef_out):
    odd, _, _ = spots()
    merged, coefs = port_coefs(*order(odd, planes_of(mine, 5), planes_of(theirs, 5)))
    put_planes(merged_out, merged)
    put_planes(coef_out, coefs)


def ring_matrix_kernel(own, mid, far, near, merged_out, mine_out, other_out, ring_out, top_out):
    _, right, upper = spots()
    packs = [planes_of(r, 5) for r in (own, near, mid, far)]
    mine, mine_c = port_coefs(*order(right, packs[0], packs[1]))
    other, other_c = port_coefs(*order(right, packs[2], packs[3]))
    merged, ring_c = port_coefs(*order(upper, mine, other))
    put_planes(merged_out, merged)
    put_planes(mine_out, mine_c)
    put_planes(other_out, other_c)
    put_planes(ring_out, ring_c)
    last = lax.div(lax.axis_index("gx"), 8) == 1
    kf, kl, z, tt, g = merged
    put_planes(top_out, (jnp.where(last, z + tt * (tt * recip(g)), g), jnp.where(last, kf, kl)))


def read_sides(ref):
    main = (ref[0:32], ref[32:64])
    edge = tuple(ref[64 + i : 65 + i] for i in range(7))
    return main, edge


def core_kernel(mine, edge_mine, theirs, coefs, merged_out, saved_out):
    odd, _, _ = spots()
    m = (mine[0:32], mine[32:64]), tuple(edge_mine[i : i + 1] for i in range(7))
    t = read_sides(theirs)
    values, saved = port_values(planes_of(coefs, 7), *order(odd, m[0], t[0]))
    edge, edge_saved = merge_ports(*order(odd, m[1], t[1]))
    put_planes(merged_out, values)
    for i in range(7):
        merged_out[64 + i : 65 + i] = edge[i]
    write_pack(saved_out, saved, edge_saved)


def ring_kernel(own, mid, far, near, matrix, mine_c, other_c, ring_c, merged_out, pair_out, saved_out, top_out):
    _, right, upper = spots()
    last = lax.div(lax.axis_index("gx"), 8) == 1
    main, edge = zip(*[read_sides(r) for r in (own, near, mid, far)])
    mine, pair = port_values(planes_of(mine_c, 7), *order(right, main[0], main[1]))
    other, _ = port_values(planes_of(other_c, 7), *order(right, main[2], main[3]))
    values, saved = port_values(planes_of(ring_c, 7), *order(upper, mine, other))
    e_mine, e_pair = merge_ports(*order(right, edge[0], edge[1]))
    e_other, _ = merge_ports(*order(right, edge[2], edge[3]))
    e_merged, e_saved = merge_ports(*order(upper, e_mine, e_other))
    outs = [planes_of(matrix, 5) + values, e_merged]
    write_pack(merged_out, *outs)
    kf, kl, z, tt, g, p, q = outs[0]
    top_out[0:32] = jnp.where(last, p + tt * recip(g) * q, q)
    kf, kl, z, tt, g, p, q = e_merged
    tg = tt * recip(g)
    for i, (a, b) in enumerate(((z + tt * tg, g), (p + tg * q, q), (kf, kl))):
        top_out[32 + i : 33 + i] = jnp.where(last, a, b)
    write_pack(pair_out, pair, e_pair)
    write_pack(saved_out, saved, e_saved)


def read_top(matrix, values):
    main = (matrix[0:32], values[0:32], matrix[32:64])
    return main, tuple(values[32 + i : 33 + i] for i in range(3))


def top_kernel(merged, near_m, near, theirs_m, theirs, sv1, sv2, sv3, own, send):
    me_x = lax.axis_index("gx")
    far = lax.div(me_x, 8) == 1
    mm = read_pack(merged, 7)
    n, t = read_top(near_m, near), read_top(theirs_m, theirs)
    saved = [read_pack(r, 6) for r in (sv1, sv2, sv3)]
    final = []
    for part in range(2):
        (ga, qa, ka), (zb, pb, kb) = order(far, n[part], t[part])
        link = R * jnp.minimum(ka, kb)
        lk = link * recip(1.0 + link * zb)
        u_a = (qa + lk * pb) * recip(ga + lk)
        kf, kl, z, tt, g, p, q = mm[part]
        flux = jnp.where(far, lk * (u_a - pb), 0.0)
        u = jnp.where(far, (q + tt * flux) * recip(g), u_a)
        for bit, lev in ((4, 2), (2, 1)):
            right = lax.rem(lax.div(me_x, bit), 2) == 1
            ua, fb = descend(saved[lev][part], flux, u)
            flux = jnp.where(right, fb, flux)
            u = jnp.where(right, u, ua)
        ua, fb = descend(saved[0][part], flux, u)
        odd = lax.rem(me_x, 2) == 1
        final.append((jnp.where(odd, fb, flux), jnp.where(odd, u, ua), jnp.where(odd, flux, fb), jnp.where(odd, ua, u)))
    write_pack(own, final[0][:2], final[1][:2])
    send[0:32] = final[0][2]
    send[32:64] = final[0][3]


def coef_kernel(cond, kh, planes, cot, sub, dep, cls, k_y, k_l, k_z, k_s, base):
    me_y = lax.axis_index("gy")
    sub_v, dep_v, kh_v = sub[...], dep[...], kh[...]
    top = film_top(cls[...])
    lane = lax.broadcasted_iota(jnp.int32, (8, 128), 1)
    first, final = lane == 0, lane == 127
    film_y = jnp.where(first & (me_y == 0), SIDE, 0.0) + jnp.where(final & (me_y == 7), SIDE, 0.0)
    for z in range(64):
        rows = slice(8 * z, 8 * z + 8)
        k = cond[rows]
        k_h = pltpu.roll(kh_v, 128 - 2 * z, 1) if z else kh_v
        k_y[rows] = (2.0 * R) * jnp.minimum(k, jnp.where(final, k_h, pltpu.roll(k, 127, 1)))
        k_l[rows] = (2.0 * R) * jnp.minimum(k, k_h)
        if z < 63:
            k_z[rows] = (2.0 * R) * jnp.minimum(k, cond[8 * z + 8 : 8 * z + 16])
        else:
            k_z[rows] = jnp.zeros((8, 128), F32)
        film = film_y + top * (dep_v - 1 == z).astype(F32)
        if z == 0:
            film = film + BOTTOM
        cap = jnp.where(z < sub_v, 1.0, 0.6)
        k_s[rows] = 2.0 * cap - (2.0 * R) * film
        base[rows] = cot[rows] - 2.0 * (cap * planes[rows])


def expand_rows(xfac, flux, last, s1):
    for chunk in range(4):
        rows = slice(8 * chunk, 8 * chunk + 8)
        levels, tie = load_x(xfac.at[chunk])
        u = expand_chain(last[rows], levels, tie, flux[rows])
        for x in range(8):
            s1[pl.ds(64 * chunk + x, 8, stride=8), :] = u[x]


def stencil(half, uh, s1, k_y, k_l, k_z, k_s, base, sub_v, below, above, src, out, done=None):
    lane = lax.broadcasted_iota(jnp.int32, (8, 128), 1)
    first, final = lane == 0, lane == 127
    up = below
    for i in range(32):
        rows = slice(8 * i, 8 * i + 8)
        at = pl.ds(pl.multiple_of(256 * half + 8 * i, 8), 8)
        s = s1[rows]
        s_h = pltpu.roll(uh, 128 - 2 * i, 1) if i else uh
        f_y = k_y[at, :] * (jnp.where(final, s_h, pltpu.roll(s, 127, 1)) - s)
        f_l = k_l[at, :] * (s - s_h)
        total = f_y - jnp.where(first, f_l, pltpu.roll(f_y, 1, 1))
        f_z = k_z[at, :] * (s1[8 * i + 8 : 8 * i + 16] - s) if i < 31 else above
        if f_z is not None:
            total = total + f_z
        if up is not None:
            total = total - up
        up = f_z
        src[rows] = jnp.where(32 * half + i < sub_v, 1.0, 0.6) * s
        out[rows] = base[at, :] + k_s[at, :] * s + total
        if done is not None and i & 7 == 7:
            done(i // 8)


def own_kernel(own, xfac, xhfac, k_y, k_l, k_z, k_s, base, sub, s1, src, out, uh_out):
    half = own_half()
    levels, tie = load_x(xhfac)
    uh = jnp.concatenate(expand_chain(own[65:66], levels, tie, own[64:65]), axis=0)
    turned = pltpu.roll(uh, 64, 1)
    uh_out[...] = jnp.where(half == 1, uh, turned)
    expand_rows(xfac, own.at[0:32], own.at[32:64], s1)
    uh = jnp.where(half == 1, turned, uh)
    stencil(half, uh, s1, k_y, k_l, k_z, k_s, base, sub[...], None, None, src, out)


def last_kernel(
    got, xfac, k_y, k_l, k_z, k_s, base, sub, s_own, src_own, out_own, uh, temp_out, src_out, s1, ends, t_buf, s_buf, sems
):
    mine = own_half()
    half = 1 - mine
    copies = []

    def send(buf, rows, out, start):
        size = rows.stop - rows.start
        cp = pltpu.make_async_copy(buf.at[rows], out.at[pl.ds(pl.multiple_of(start, 8), size)], sems.at[len(copies)])
        cp.start()
        copies.append(cp)

    send(src_own, slice(0, 256), src_out, 256 * mine)
    send(out_own, slice(8, 248), temp_out, 256 * mine + 8)
    expand_rows(xfac, got.at[0:32], got.at[32:64], s1)
    inner, outer = s_own[248:256], s_own[0:8]
    low = jnp.where(half == 0, s1[248:256], inner)
    high = jnp.where(half == 0, outer, s1[0:8])
    flux = k_z[248:256] * (high - low)
    ends[0:8] = out_own[0:8] - jnp.where(mine == 1, flux, 0.0)
    ends[8:16] = out_own[248:256] + jnp.where(mine == 0, flux, 0.0)
    send(ends, slice(0, 8), temp_out, 256 * mine)
    send(ends, slice(8, 16), temp_out, 256 * mine + 248)

    def done(piece):
        rows = slice(64 * piece, 64 * piece + 64)
        send(s_buf, rows, src_out, 256 * half + 64 * piece)
        send(t_buf, rows, temp_out, 256 * half + 64 * piece)

    below, above = jnp.where(half == 1, flux, 0.0), jnp.where(half == 0, flux, 0.0)
    stencil(half, uh[...], s1, k_y, k_l, k_z, k_s, base, sub[...], below, above, s_buf, t_buf, done)
    for cp in copies:
        cp.wait()


VMEM = pl.BlockSpec(memory_space=pltpu.VMEM)
HBM = pl.BlockSpec(memory_space=pltpu.MemorySpace.HBM)


def call(kernel, outs, scratch, name, *args, far_in=0, far_out=0, sems=0):
    shapes = [s if isinstance(s, jax.ShapeDtypeStruct) else jax.ShapeDtypeStruct(s, F32) for s in outs]
    scr = [pltpu.VMEM(s, F32) for s in scratch]
    args = [pltpu.with_memory_space_constraint(a, pltpu.MemorySpace.HBM) if i < far_in else a for i, a in enumerate(args)]
    if sems:
        scr.append(pltpu.SemaphoreType.DMA((sems,)))
    return pl.pallas_call(
        kernel,
        out_shape=shapes,
        in_specs=[HBM if i < far_in else VMEM for i in range(len(args))],
        out_specs=[HBM if i < far_out else VMEM for i in range(len(outs))],
        scratch_shapes=scr,
        compiler_params=pltpu.CompilerParams(vmem_limit_bytes=40 * 1024 * 1024),
        name=name,
    )(*args)


def swap(v, bit):
    return lax.ppermute(v, "gx", [(i, i ^ bit) for i in range(16)])


def body(cotangent, saved_temp, substrate_top, deposit_top, top_class):
    cot = cotangent.reshape(512, 128)
    temp = saved_temp.reshape(512, 128)
    small = jax.ShapeDtypeStruct((8, 128), jnp.int32)
    cond, keep_m, send_m, cot, sub, dep, cls = call(
        fields_kernel,
        [(512, 128), (160, 128), (160, 128), (512, 128), small, small, small],
        [(512, 128), (5, 64, 128)],
        "fields",
        cot, temp, substrate_top, deposit_top, top_class,
        far_in=5, sems=12,
    )
    other_m = swap(send_m, 1)
    ypack, fac, ties = call(
        first_kernel,
        [(8, 32, 128), (3, 63, 8, 128), (12, 8, 128)],
        [(3, 512, 128), (512, 128)],
        "first",
        cot, sub, dep, cls, cond,
    )
    mm, core_c = call(core_matrix_kernel, [(160, 128), (224, 128)], [], "matrix_core", keep_m, other_m)
    mm, ypack = lax.optimization_barrier((mm, ypack))
    gat = lax.all_to_all(ypack, "gy", split_axis=0, concat_axis=0, tiled=True)
    ring_m = [swap(mm, bit) for bit in (4, 7, 3)]
    send, edge, xfac, xhfac, kh, planes = call(
        second_kernel,
        [(72, 128), (8, 128), (4, 24, 8, 128), (24, 1, 128), (8, 128), (512, 128)],
        [(8, 32, 128), (512, 128)],
        "second",
        gat, fac, ties, cond, sub,
    )
    keep, xfac_own = call(keep_kernel, [(64, 128), (4, 24, 8, 128)], [], "keep_rows", cond, planes, sub)
    m1, sv1 = call(core_kernel, [(72, 128), (200, 128)], [], "merge_core", keep, edge, swap(send, 1), core_c)
    ring_v = [swap(m1, bit) for bit in (4, 7, 3)]
    matrix, mine_c, other_c, ring_c, near_m = call(
        ring_matrix_kernel, [(160, 128)] + [(224, 128)] * 3 + [(64, 128)], [], "matrix_ring", mm, *ring_m
    )
    opposite_m = swap(near_m, 9)
    m3, sv2, sv3, near = call(
        ring_kernel,
        [(232, 128), (200, 128), (200, 128), (40, 128)],
        [],
        "merge_ring",
        m1, *ring_v, matrix, mine_c, other_c, ring_c,
    )
    sv3, kh = lax.optimization_barrier((sv3, kh))
    coefs = call(coef_kernel, [(512, 128)] * 5, [], "coef", cond, kh, planes, cot, sub, dep, cls)
    opposite = swap(near, 9)
    sv3, coefs = lax.optimization_barrier((sv3, coefs))
    own, out = call(top_kernel, [(72, 128), (64, 128)], [], "top", m3, near_m, near, opposite_m, opposite, sv1, sv2, sv3)
    got = swap(out, 1)
    part = call(
        own_kernel,
        [(256, 128), (256, 128), (256, 128), (8, 128)],
        [],
        "own_rows",
        own, xfac_own, xhfac, *coefs, sub,
    )
    grad_temp, grad_source = call(
        last_kernel,
        [(512, 128), (512, 128)],
        [(256, 128), (16, 128), (256, 128), (256, 128)],
        "last",
        got, xfac, *coefs, sub, *part,
        far_out=2, sems=12,
    )
    return grad_temp.reshape(cotangent.shape), grad_source.reshape(cotangent.shape)


def solution(mesh):
    in_specs = (
        P(None, "gx", "gy"),
        P(None, "gx", "gy"),
        P("gx", "gy"),
        P("gx", "gy"),
        P("gx", "gy"),
    )
    out_specs = (P(None, "gx", "gy"), P(None, "gx", "gy"))
    return jax.shard_map(body, mesh=mesh, in_specs=in_specs, out_specs=out_specs, check_vma=False)
```
